128 devices in a mesh: gx: 16 (over x, y), gy: 8 (over z, core).
Axes of the slice: x: 4, y: 4, z: 4, core: 2. Of those that a mesh axis runs over, the one named last changes fastest.
Arguments:
- log_density: float32 [512, 512, 512], P('gx', 'gy'), may hold values from -3 to 3
- weights: bfloat16 [8192, 32, 32, 128], P(('gx', 'gy')), may hold values from -0.09375 to 0.09375
- observed: float32 [8192, 32], P(('gx', 'gy')), may hold values from -6 to 6
- inverse_var: float32 [8192, 32], P(('gx', 'gy')), may hold values from 0.25 to 4
- star_counts: int32 [8192], P(('gx', 'gy')), may hold values from 1 to 32
- block_ids: int32 [8192, 32], P(('gx', 'gy')), may hold values from 0 to 1048575, as said below
Outputs:
- new_log_density: float32 [512, 512, 512], P('gx', 'gy')
- extinction: float32 [8192, 32], P(('gx', 'gy'))
The draws below stay inside these ranges and needn't reach their ends.
Inputs may be any that keep to these rules, and one draw needn't show every extreme that they name: `block_ids`: among the 2048 ids of one device's rows (rows d * 64 to (d + 1) * 64 - 1), at most 32 name blocks of any one tile (blocks t * 8192 to (t + 1) * 8192 - 1), and exactly 32 name blocks of tile d.
All inputs are finite; a program needn't handle non-finite values.
Results may differ from the reference program's by a relative error of at most 0.0029.
Values may be sent and summed in bfloat16 or wider, within the bound.
A program may use at most 128 MiB of HBM per device.

```python
import math
import jax
import jax.numpy as jnp
from jax import lax

CX = 32
CY = 64
NZ = 512
VB = 128
SB = 32
K = 32
SBD = 64
NDEV = 128
ZB = 4
VBD = 8192
CAP = 32
NX = 512
NY = 512
N_GX = 16
N_GY = 8


def draw_block_ids(key, part):
    total = SBD * K

    def one_device(device):
        dev_key = jax.random.fold_in(key, device)
        key_a, key_b, key_c = jax.random.split(dev_key, 3)
        others = jax.random.permutation(key_a, (NDEV - 1) * CAP)[:total - CAP]
        target_other = (device + 1 + others // CAP) % NDEV
        target = jnp.concatenate([jnp.full((CAP,), device, jnp.int32), target_other.astype(jnp.int32)])
        order = jax.random.permutation(key_b, total)
        target = target[order]
        within = jax.random.randint(key_c, (total,), 0, VBD, jnp.int32)
        return (target * VBD + within).reshape(SBD, K)
    return jax.vmap(one_device)(jnp.arange(NDEV, dtype=jnp.int32)).reshape(NDEV * SBD, K)


def with_ends(drawn, own_key, low, top_value):
    index_at = [jax.random.randint(jax.random.fold_in(own_key, axis), (), 0, length) for axis, length in enumerate(drawn.shape)]
    main_axis = drawn.shape.index(max(drawn.shape))
    next_to = index_at[:main_axis] + [(index_at[main_axis] + 1) % drawn.shape[main_axis]] + index_at[main_axis + 1:]
    return drawn.at[tuple(index_at)].set(low).at[tuple(next_to)].set(top_value)


def steps_of(rng, dims, pieces, least, top_value):
    factor_of, own = 1.0, jax.random.fold_in(rng, 6)
    for axis_at, parts in pieces:
        steps = jnp.exp(jax.random.uniform(jax.random.fold_in(own, axis_at), (parts,), jnp.float32, least / len(pieces), top_value / len(pieces)))
        factor_of = factor_of * jnp.repeat(steps, dims[axis_at] // parts).reshape([-1 if axis == axis_at else 1 for axis in range(len(dims))])
    return factor_of


def gaussian(own_key, extent, spread, most, pieces=(), kind=jnp.bfloat16):
    array = jax.random.normal(own_key, extent, jnp.float32) * spread
    if len(pieces) > 0:
        array = steps_of(own_key, extent, pieces, -0.22, 0.18) * array
    return jnp.clip(array, min=-most, max=most).astype(kind)


def setup_inputs(seed: int = 0) -> dict:
    streams_of = jax.random.split(jax.random.key(seed), 7)
    return {
        "log_density": gaussian(streams_of[0], (NX, NY, NZ), 0.5, 3.0, ((0, 16), (1, 8)), jnp.float32),
        "weights": gaussian(streams_of[1], (NDEV * SBD, K, SB, VB), (K * VB) ** -0.5, 0.09375, ((0, 128),)),
        "observed": gaussian(streams_of[2], (NDEV * SBD, SB), 1.0, 6.0, ((0, 128),), jnp.float32),
        "inverse_var": jnp.clip(jnp.exp(math.log(4.0) - 2.7725887 * jax.random.uniform(streams_of[3], (NDEV * SBD, SB), jnp.float32) ** steps_of(streams_of[3], (NDEV * SBD, SB), ((0, 128),), -0.2, 0.2)), 0.25, 4.0),
        "star_counts": with_ends(jax.random.randint(streams_of[4], (NDEV * SBD,), 1, SB + 1), jax.random.fold_in(streams_of[4], 1), 1, SB).astype(jnp.int32),
        "block_ids": draw_block_ids(jax.random.fold_in(streams_of[6], 71), 0),
    }


shift_kappa = 0.5
prior_weight = 0.05
step_rate = 2.0


def operate(field):
    padded = jnp.pad(field, 1)
    beside = padded[2:, 1:-1, 1:-1] + padded[:-2, 1:-1, 1:-1]
    beside = beside + padded[1:-1, 2:, 1:-1] + padded[1:-1, :-2, 1:-1]
    beside = beside + padded[1:-1, 1:-1, 2:] + padded[1:-1, 1:-1, :-2]
    return (shift_kappa + 6.0) * field - beside


def reference(log_density, weights, observed, inverse_var, star_counts, block_ids):
    dens_field = jnp.exp(log_density)
    table = dens_field.astype(jnp.bfloat16).reshape(N_GX, CX, N_GY, CY, ZB, VB)
    table = table.transpose(0, 2, 1, 3, 4, 5).reshape(NDEV * VBD, VB)
    fetched = table[block_ids]

    def per_device(packed):
        w_dev, f_dev, obs_dev, inv_dev, cnt_dev = packed
        w_full = w_dev.astype(jnp.float32)
        ext = jnp.einsum("bksv,bkv->bs", w_full, f_dev.astype(jnp.float32))
        live = jnp.arange(SB)[None, :] < cnt_dev[:, None]
        weighted = jnp.where(live, inv_dev * (ext - obs_dev), 0.0).astype(jnp.bfloat16)
        sens = jnp.einsum("bksv,bs->bkv", w_full, weighted.astype(jnp.float32))
        return ext, sens

    ext, sens = lax.map(per_device, (weights.reshape(NDEV, SBD, K, SB, VB),
                                      fetched.reshape(NDEV, SBD, K, VB),
                                      observed.reshape(NDEV, SBD, SB),
                                      inverse_var.reshape(NDEV, SBD, SB),
                                      star_counts.reshape(NDEV, SBD)))
    collected = jnp.zeros((NDEV * VBD, VB), jnp.float32).at[block_ids.reshape(-1)].add(sens.reshape(-1, VB))
    collected = collected.reshape(N_GX, N_GY, CX, CY, ZB, VB).transpose(0, 2, 1, 3, 4, 5)
    data_grad = collected.reshape(NX, NY, NZ) * dens_field
    smooth = operate(log_density)
    prior_grad = operate(smooth)
    new_log_density = log_density - step_rate * (data_grad + prior_weight * prior_grad)
    return new_log_density, ext.reshape(NDEV * SBD, SB)
```

```python
import functools

import jax
import jax.numpy as jnp
from jax import lax
from jax.experimental import pallas as pl
from jax.experimental.pallas import tpu as pltpu
from jax.sharding import PartitionSpec as P

MESH = pl.DeviceIdType.MESH
DMA = pltpu.SemaphoreType.DMA
shift_kappa = 0.5
prior_weight = 0.05
step_rate = 2.0
f32, bf16, i32 = jnp.float32, jnp.bfloat16, jnp.int32

NDEV, CAP, WIDTH = 128, 32, 128
BLOCKS, SLOTS, STARS = 64, 32, 32
REQ = BLOCKS * SLOTS
CX, CY, NZ = 32, 64, 512
LOCAL_BITS = 13


def vmem(shape, dtype):
    return pltpu.VMEM(shape, dtype)


def whole(space):
    return pl.BlockSpec(memory_space=space)


def bucket_kernel(ids_ref, out_ref, inv_ref, pos_ref, at_ref, bt_ref):
    ids = ids_ref[...]
    target = ids >> LOCAL_BITS
    within = ids & ((1 << LOCAL_BITS) - 1)
    order = lax.broadcasted_iota(i32, (1, REQ), 1)
    at = lax.broadcasted_iota(i32, (NDEV, REQ), 0) == target
    at_ref[...] = jnp.where(at, 1.0, 0.0).astype(bf16)
    step = 256
    before = (lax.broadcasted_iota(i32, (step, step), 0) < lax.broadcasted_iota(i32, (step, step), 1))
    before = jnp.where(before, 1.0, 0.0).astype(bf16)
    running = jnp.zeros((NDEV, 1), f32)
    slot = lax.broadcasted_iota(i32, (CAP, step), 0)
    for k in range(REQ // step):
        cut = slice(k * step, (k + 1) * step)
        part = at_ref[:, cut]
        prefix = jnp.dot(part, before, preferred_element_type=f32) + running
        wide = part.astype(f32)
        rank = jnp.sum(wide * prefix, axis=0, keepdims=True).astype(i32)
        running = running + jnp.sum(wide, axis=1, keepdims=True)
        hit = slot == rank
        pos_ref[:, cut] = target[:, cut] * CAP + rank
        for n, value in enumerate((within[:, cut] >> 7, within[:, cut] & 127, order[:, cut] >> 7, order[:, cut] & 127, None)):
            value = 1.0 if value is None else value.astype(f32)
            bt_ref[n * CAP:(n + 1) * CAP, cut] = jnp.where(hit, value, 0.0).astype(bf16)
    table = lax.dot_general(at_ref[...], bt_ref[...], (((1,), (1,)), ((), ())), preferred_element_type=f32)
    parts = [table[:, n * CAP:(n + 1) * CAP] for n in range(5)]
    present = parts[4] > 0.5
    out_ref[...] = jnp.where(present, parts[0] * 128.0 + parts[1], -1.0).astype(i32)[:, None, :]
    inv_ref[...] = jnp.where(present, parts[2] * 128.0 + parts[3], float(REQ)).astype(i32)


def bucket(block_ids):
    return pl.pallas_call(
        bucket_kernel,
        out_shape=(
            jax.ShapeDtypeStruct((NDEV, 1, CAP), i32),
            jax.ShapeDtypeStruct((NDEV, CAP), i32),
            jax.ShapeDtypeStruct((1, REQ), i32),
        ),
        in_specs=[whole(pltpu.VMEM)],
        out_specs=[whole(pltpu.VMEM)] * 3,
        scratch_shapes=[vmem((NDEV, REQ), bf16), vmem((5 * CAP, REQ), bf16)],
        name="bucket",
    )(block_ids.reshape(1, REQ))


def position_tables():
    gx, gy = lax.axis_index("gx"), lax.axis_index("gy")
    around = lambda v, n: [lax.rem(v + d, n) for d in range(n)]
    return gx, gy, around(gx // 4, 4), around(lax.rem(gx, 4), 4), around(gy // 2, 4), around(lax.rem(gy, 2), 2)


def signal_all(tables):
    gx, gy, xs, ys, zs, cs = tables
    barrier = pltpu.get_barrier_semaphore()
    for j in range(1, NDEV):
        pl.semaphore_signal(
            barrier, inc=1, device_id=(xs[j // 32] * 4 + ys[j // 8 % 4], zs[j // 2 % 4] * 2 + cs[j % 2]), device_id_type=MESH
        )


def wait_all():
    pl.semaphore_wait(pltpu.get_barrier_semaphore(), NDEV - 1)


def peer(gx, gy, j):
    o = lax.rem(j * 37, NDEV)
    x = lax.rem(gx // 4 + o // 32, 4)
    y = lax.rem(gx + lax.rem(o // 8, 4), 4)
    z = lax.rem(gy // 2 + lax.rem(o // 2, 4), 4)
    c = lax.rem(gy + o, 2)
    return x * 4 + y, z * 2 + c


def remote(src, dst, send, recv, to):
    return pltpu.make_async_remote_copy(
        src_ref=src, dst_ref=dst, send_sem=send, recv_sem=recv, device_id=to, device_id_type=MESH
    )


def drain(ref, sem):
    pltpu.make_async_copy(ref, ref, sem).wait()


def fetch_kernel(out_ids, dens_hbm, ret_ref, in_ids, exp_ref, xlo, xhi, ylo, yhi,
                 dens, served, ids_smem, s_id, r_id, s_row, r_row, local, s_halo, r_halo):
    tables = position_tables()
    gx, gy, xs, ys, zs, cs = tables
    me = gx * 8 + gy
    loads = [pltpu.make_async_copy(dens_hbm.at[:, :, pl.ds(q * WIDTH, WIDTH)], dens.at[q], local.at[q]) for q in range(4)]
    for load in loads:
        load.start()
    signal_all(tables)
    wait_all()
    own = pltpu.make_async_copy(out_ids.at[me], in_ids.at[me], local.at[4])
    own.start()
    for j in range(1, NDEV):
        tx, ty = xs[j // 32] * 4 + ys[j // 8 % 4], zs[j // 2 % 4] * 2 + cs[j % 2]
        remote(out_ids.at[tx * 8 + ty], in_ids.at[me], s_id, r_id, (tx, ty)).start()
    gxm, gxp = lax.rem(gx + 15, 16), lax.rem(gx + 1, 16)
    gym, gyp = lax.rem(gy + 7, 8), lax.rem(gy + 1, 8)
    halos = [
        (dens_hbm.at[pl.ds(CX - 2, 2)], xlo, (gxp, gy)),
        (dens_hbm.at[pl.ds(0, 2)], xhi, (gxm, gy)),
        (dens_hbm.at[:, pl.ds(CY - 8, 8)], ylo.at[pl.ds(1, CX)], (gx, gyp)),
        (dens_hbm.at[:, pl.ds(0, 8)], yhi.at[pl.ds(1, CX)], (gx, gym)),
        (dens_hbm.at[CX - 1, pl.ds(CY - 8, 8)], ylo.at[0], (gxp, gyp)),
        (dens_hbm.at[0, pl.ds(CY - 8, 8)], ylo.at[CX + 1], (gxm, gyp)),
        (dens_hbm.at[CX - 1, pl.ds(0, 8)], yhi.at[0], (gxp, gym)),
        (dens_hbm.at[0, pl.ds(0, 8)], yhi.at[CX + 1], (gxm, gym)),
    ]
    halos = [remote(src, dst, s_halo.at[n], r_halo.at[n], to) for n, (src, dst, to) in enumerate(halos)]
    own.wait()
    drain(in_ids.at[pl.ds(0, NDEV - 1)], r_id)
    to_smem = pltpu.make_async_copy(in_ids, ids_smem, local.at[4])
    to_smem.start()
    for copy in halos:
        copy.start()
    to_smem.wait()
    for load in loads:
        load.wait()

    def serve(at):
        for c in range(CAP):
            n = jnp.maximum(ids_smem[at, 0, c], 0)
            exp_ref[at, c, :] = dens[n & 3, n >> 8, (n >> 2) & 63, :]
        rows = jnp.exp(exp_ref[at])
        exp_ref[at] = rows
        served[at] = rows.astype(bf16)

    def send(j, _):
        tx, ty = peer(gx, gy, j)
        at = tx * 8 + ty
        serve(at)
        remote(served.at[at], ret_ref.at[me], s_row, r_row, (tx, ty)).start()
        return 0

    lax.fori_loop(1, NDEV, send, 0)
    serve(me)
    keep = pltpu.make_async_copy(served.at[me], ret_ref.at[me], local.at[0])
    keep.start()
    keep.wait()
    drain(out_ids.at[pl.ds(0, NDEV - 1)], s_id)
    for copy in halos:
        copy.wait()
    drain(served.at[pl.ds(0, NDEV - 1)], s_row)
    drain(ret_ref.at[pl.ds(0, NDEV - 1)], r_row)


def fetch(out_ids, dens):
    return pl.pallas_call(
        fetch_kernel,
        out_shape=(
            jax.ShapeDtypeStruct((NDEV, CAP, WIDTH), bf16),
            jax.ShapeDtypeStruct((NDEV, 1, CAP), i32),
            jax.ShapeDtypeStruct((NDEV, CAP, WIDTH), f32),
            jax.ShapeDtypeStruct((2, CY, NZ), f32),
            jax.ShapeDtypeStruct((2, CY, NZ), f32),
            jax.ShapeDtypeStruct((CX + 2, 8, NZ), f32),
            jax.ShapeDtypeStruct((CX + 2, 8, NZ), f32),
        ),
        in_specs=[whole(pltpu.VMEM), whole(pl.ANY)],
        out_specs=[whole(pltpu.VMEM)] * 7,
        scratch_shapes=[
            vmem((4, CX, CY, WIDTH), f32), vmem((NDEV, CAP, WIDTH), bf16), pltpu.SMEM((NDEV, 1, CAP), i32),
            DMA, DMA, DMA, DMA, DMA((5,)), DMA((8,)), DMA((8,)),
        ],
        name="fetch",
        compiler_params=pltpu.CompilerParams(collective_id=0, has_side_effects=True, vmem_limit_bytes=40 << 20),
    )(out_ids, dens)


CHUNK = 8


def stars_kernel(pos, counts, ret, weights, observed, inverse_var, ext_ref, sens_ref, rows, stage, obs4, inv4):
    step = pl.program_id(0)

    @pl.when(step == 0)
    def _():
        rows[...] = ret[...].astype(f32).reshape(NDEV * CAP, WIDTH)
        obs4[...] = jnp.concatenate([observed[...]] * 4, axis=1)
        inv4[...] = jnp.concatenate([inverse_var[...]] * 4, axis=1)
        sens_ref[pl.ds(REQ, 8), :] = jnp.zeros((8, WIDTH), f32)

    group = lax.broadcasted_iota(i32, (SLOTS, SLOTS * STARS), 1) >> 5
    mine = group == lax.broadcasted_iota(i32, (SLOTS, SLOTS * STARS), 0)
    star = lax.broadcasted_iota(i32, (1, WIDTH), 1) & (STARS - 1)
    for u in range(CHUNK):
        b = step * CHUNK + u
        for k in range(SLOTS):
            stage[u, k, :] = rows[pos[0, b * SLOTS + k], :]
        values = stage[u].astype(bf16)
        w = weights[u].reshape(SLOTS * STARS, WIDTH)
        every = lax.dot_general(values, w, (((1,), (1,)), ((), ())), preferred_element_type=f32)
        every = jnp.sum(jnp.where(mine, every, 0.0), axis=0, keepdims=True)
        tiles = [every[:, n * WIDTH:(n + 1) * WIDTH] for n in range(SLOTS * STARS // WIDTH)]
        while len(tiles) > 1:
            tiles = [tiles[n] + tiles[n + 1] for n in range(0, len(tiles), 2)]
        ext = tiles[0]
        ext = ext + pltpu.roll(ext, 64, 1)
        ext = ext + pltpu.roll(ext, 32, 1)
        ext_ref[pl.ds(b, 1), :] = ext[:, :STARS]
        weighted = jnp.where(star < counts[b], inv4[pl.ds(b, 1), :] * (ext - obs4[pl.ds(b, 1), :]), 0.0)
        spread = jnp.concatenate([weighted] * 8, axis=1)
        left = jnp.where(mine, spread, 0.0).astype(bf16)
        sens_ref[pl.ds(b * SLOTS, SLOTS), :] = jnp.dot(left, w, preferred_element_type=f32)


def stars_step(pos, counts, ret, weights, observed, inverse_var):
    fixed = lambda i: (0, 0)
    return pl.pallas_call(
        stars_kernel,
        grid=(BLOCKS // CHUNK,),
        out_shape=(jax.ShapeDtypeStruct((BLOCKS, STARS), f32), jax.ShapeDtypeStruct((REQ + 8, WIDTH), f32)),
        in_specs=[
            whole(pltpu.SMEM), whole(pltpu.SMEM), whole(pltpu.VMEM),
            pl.BlockSpec((CHUNK, SLOTS, STARS, WIDTH), lambda i: (i, 0, 0, 0)),
            whole(pltpu.VMEM), whole(pltpu.VMEM),
        ],
        out_specs=[pl.BlockSpec((BLOCKS, STARS), fixed), pl.BlockSpec((REQ + 8, WIDTH), fixed)],
        scratch_shapes=[vmem((NDEV * CAP, WIDTH), f32), vmem((CHUNK, SLOTS, WIDTH), f32), vmem((BLOCKS, WIDTH), f32), vmem((BLOCKS, WIDTH), f32)],
        name="stars",
        compiler_params=pltpu.CompilerParams(dimension_semantics=("arbitrary",), vmem_limit_bytes=32 << 20),
    )(pos, counts, ret, weights, observed, inverse_var)


def return_kernel(inv, sens, arr_ref, stage, parcel, s_row, r_row, local):
    tables = position_tables()
    gx, gy = tables[:2]
    me = gx * 8 + gy
    signal_all(tables)
    wait_all()

    def pack(at):
        for c in range(CAP):
            stage[c, :] = sens[inv[at, c], :]
        parcel[at] = stage[...].astype(bf16)

    def send(j, _):
        tx, ty = peer(gx, gy, j)
        at = tx * 8 + ty
        pack(at)
        remote(parcel.at[at], arr_ref.at[me], s_row, r_row, (tx, ty)).start()
        return 0

    lax.fori_loop(1, NDEV, send, 0)
    pack(me)
    keep = pltpu.make_async_copy(parcel.at[me], arr_ref.at[me], local)
    keep.start()
    keep.wait()
    drain(parcel.at[pl.ds(0, NDEV - 1)], s_row)
    drain(arr_ref.at[pl.ds(0, NDEV - 1)], r_row)


def give_back(inv, sens):
    return pl.pallas_call(
        return_kernel,
        out_shape=jax.ShapeDtypeStruct((NDEV, CAP, WIDTH), bf16),
        in_specs=[whole(pltpu.SMEM), whole(pltpu.VMEM)],
        out_specs=whole(pltpu.VMEM),
        scratch_shapes=[vmem((CAP, WIDTH), f32), vmem((NDEV, CAP, WIDTH), bf16), DMA, DMA, DMA],
        name="give_back",
        compiler_params=pltpu.CompilerParams(collective_id=1, has_side_effects=True, vmem_limit_bytes=16 << 20),
    )(inv, sens)


def update_kernel(ids, dens, xlo, xhi, ylo, yhi, rows_exp, arrived, out_hbm, smooth, add, new, sem):
    gx, gy = lax.axis_index("gx"), lax.axis_index("gy")
    TALL = CY + 16
    lane = lax.broadcasted_iota(i32, (TALL, NZ), 1)
    row = lax.broadcasted_iota(i32, (TALL, NZ), 0)
    inside = ((row >= 8) | (gy > 0)) & ((row < CY + 8) | (gy < 7))
    low, high = lane == 0, lane == NZ - 1

    def apply(center, before, after):
        side = before + after
        side = side + pltpu.roll(center, 1, 0) + pltpu.roll(center, TALL - 1, 0)
        side = side + jnp.where(low, 0.0, pltpu.roll(center, 1, 1))
        side = side + jnp.where(high, 0.0, pltpu.roll(center, NZ - 1, 1))
        return (shift_kappa + 6.0) * center - side

    def plane(body, lo, hi):
        return jnp.where(inside, jnp.concatenate([lo, body, hi], axis=0), 0.0)

    blank = jnp.zeros((8, NZ), f32)
    at_low, at_high = gx == 0, gx == 15

    def outer(body, lo, hi, gone):
        return jnp.where(gone, 0.0, plane(body, lo, hi))

    e_m2 = outer(xlo[0], blank, blank, at_low)
    e_m1 = outer(xlo[1], ylo[0], yhi[0], at_low)
    e_p0 = outer(xhi[0], ylo[CX + 1], yhi[CX + 1], at_high)
    e_p1 = outer(xhi[1], blank, blank, at_high)

    def inner(x):
        return plane(dens[x], ylo[x + 1], yhi[x + 1])

    smooth[0] = jnp.where(inside & (gx > 0), apply(e_m1, e_m2, inner(0)), 0.0)
    smooth[1] = jnp.where(inside, apply(inner(0), e_m1, inner(1)), 0.0)

    def middle(x, _):
        smooth[x + 1] = jnp.where(inside, apply(inner(x), inner(x - 1), inner(x + 1)), 0.0)
        return 0

    lax.fori_loop(1, CX - 1, middle, 0)
    smooth[CX] = jnp.where(inside, apply(inner(CX - 1), inner(CX - 2), e_p0), 0.0)
    smooth[CX + 1] = jnp.where(inside & (gx < 15), apply(e_p0, inner(CX - 1), e_p1), 0.0)

    def last(x, _):
        prior = apply(smooth[x + 1], smooth[x], smooth[x + 2])
        fresh = dens[x] - (step_rate * prior_weight) * prior[8:8 + CY]
        for q in range(4):
            new[q, x] = fresh[:, q * WIDTH:(q + 1) * WIDTH]
        return 0

    lax.fori_loop(0, CX, last, 0)

    def scale(t, _):
        add[t] = step_rate * rows_exp[t] * arrived[t].astype(f32)
        return 0

    lax.fori_loop(0, NDEV, scale, 0)

    def source(t, _):
        for g in range(CAP // 8):
            @pl.when(ids[t, 0, g * 8] >= 0)
            def _():
                for c in range(g * 8, g * 8 + 8):
                    n = jnp.maximum(ids[t, 0, c], 0)
                    at = (n & 3, n >> 8, (n >> 2) & 63)
                    new[at] = new[at] - add[t, c, :]
        return 0

    lax.fori_loop(0, NDEV, source, 0)
    stores = [pltpu.make_async_copy(new.at[q], out_hbm.at[:, :, pl.ds(q * WIDTH, WIDTH)], sem.at[q]) for q in range(4)]
    for store in stores:
        store.start()
    for store in stores:
        store.wait()


def update(ids, dens, xlo, xhi, ylo, yhi, rows_exp, arrived):
    return pl.pallas_call(
        update_kernel,
        out_shape=jax.ShapeDtypeStruct((CX, CY, NZ), f32),
        in_specs=[whole(pltpu.SMEM)] + [whole(pltpu.VMEM)] * 7,
        out_specs=whole(pl.ANY),
        scratch_shapes=[
            vmem((CX + 2, CY + 16, NZ), f32), vmem((NDEV, CAP, WIDTH), f32), vmem((4, CX, CY, WIDTH), f32), DMA((4,)),
        ],
        name="update",
        compiler_params=pltpu.CompilerParams(vmem_limit_bytes=40 << 20),
    )(ids, dens, xlo, xhi, ylo, yhi, rows_exp, arrived)


def on_device(log_density, weights, observed, inverse_var, star_counts, block_ids):
    out_ids, inv, pos = bucket(block_ids)
    ret, in_ids, rows_exp, xlo, xhi, ylo, yhi = fetch(out_ids, log_density)
    extinction, sens = stars_step(pos, star_counts, ret, weights, observed, inverse_var)
    arrived = give_back(inv, sens)
    new = update(in_ids, log_density, xlo, xhi, ylo, yhi, rows_exp, arrived)
    return (new, extinction)


def solution(mesh):
    placed = (
        P("gx", "gy", None),
        P(("gx", "gy"), None, None, None),
        P(("gx", "gy"), None),
        P(("gx", "gy"), None),
        P(("gx", "gy")),
        P(("gx", "gy"), None),
    )
    return jax.shard_map(
        on_device,
        mesh=mesh,
        in_specs=placed,
        out_specs=(P("gx", "gy", None), P(("gx", "gy"), None)),
        check_vma=False,
    )
```

```python
import jax
import jax.numpy as jnp
from jax import lax
from jax.experimental import pallas as pl
from jax.experimental.pallas import tpu as pltpu
from jax.sharding import PartitionSpec as P

MESH = pl.DeviceIdType.MESH
DMA = pltpu.SemaphoreType.DMA
shift_kappa = 0.5
prior_weight = 0.05
step_rate = 2.0
f32, bf16, i32 = jnp.float32, jnp.bfloat16, jnp.int32

GX, GY = 16, 8
NDEV, CAP, WIDTH = 128, 32, 128
BLOCKS, SLOTS, STARS = 64, 32, 32
REQ = BLOCKS * SLOTS
CX, CY, ZB = 32, 64, 4
ROWS = CX * CY * ZB
LOCAL_BITS = 13
UNROLL = 4
center_weight = shift_kappa + 6.0


def whole(space):
    return pl.BlockSpec(memory_space=space)


def remote(src, dst, send, recv, to):
    return pltpu.make_async_remote_copy(
        src_ref=src, dst_ref=dst, send_sem=send, recv_sem=recv, device_id=to, device_id_type=MESH
    )


def drain(ref, sem):
    pltpu.make_async_copy(ref, ref, sem).wait()


def peer(gx, gy, j):
    o = lax.rem(j * 37, NDEV)
    x = lax.rem(gx // 4 + o // 32, 4)
    y = lax.rem(gx + lax.rem(o // 8, 4), 4)
    z = lax.rem(gy // 2 + lax.rem(o // 2, 4), 4)
    c = lax.rem(gy + o, 2)
    return x * 4 + y, z * 2 + c


def bucket_kernel(blocks, out_ids, inv_ref, pos_ref, at_ref, bt_ref):
    ids = jnp.concatenate([blocks[k:k + 1, :] for k in range(SLOTS)], axis=1)
    target = ids >> LOCAL_BITS
    within = ids & (ROWS - 1)
    within = (within & (ZB - 1)) * (CX * CY) + (within >> 2)
    order = lax.broadcasted_iota(i32, (1, REQ), 1)
    order = (order & (BLOCKS - 1)) * SLOTS + (order >> 6)
    at_ref[...] = jnp.where(lax.broadcasted_iota(i32, (NDEV, REQ), 0) == target, 1.0, 0.0).astype(bf16)
    step = 256
    before = lax.broadcasted_iota(i32, (step, step), 0) < lax.broadcasted_iota(i32, (step, step), 1)
    before = jnp.where(before, 1.0, 0.0).astype(bf16)
    running = jnp.zeros((NDEV, 1), f32)
    slot = lax.broadcasted_iota(i32, (CAP, step), 0)
    for k in range(REQ // step):
        cut = slice(k * step, (k + 1) * step)
        part = at_ref[:, cut]
        prefix = jnp.dot(part, before, preferred_element_type=f32) + running
        wide = part.astype(f32)
        rank = jnp.sum(wide * prefix, axis=0, keepdims=True).astype(i32)
        running = running + jnp.sum(wide, axis=1, keepdims=True)
        hit = slot == rank
        pos_ref[:, cut] = target[:, cut] * CAP + rank
        for n, value in enumerate((within[:, cut] >> 7, within[:, cut] & 127, order[:, cut] >> 7, order[:, cut] & 127, None)):
            value = 1.0 if value is None else value.astype(f32)
            bt_ref[n * CAP:(n + 1) * CAP, cut] = jnp.where(hit, value, 0.0).astype(bf16)
    table = lax.dot_general(at_ref[...], bt_ref[...], (((1,), (1,)), ((), ())), preferred_element_type=f32)
    parts = [table[:, n * CAP:(n + 1) * CAP] for n in range(5)]
    present = parts[4] > 0.5
    row = jnp.where(present, parts[0] * 128.0 + parts[1], float(ROWS)).astype(i32)
    out_ids[...] = row.reshape(GX, GY, 1, CAP)
    inv_ref[...] = jnp.where(present, parts[2] * 128.0 + parts[3], float(REQ)).astype(i32)


def bucket(blocks):
    shape, v = jax.ShapeDtypeStruct, pltpu.VMEM
    return pl.pallas_call(
        bucket_kernel,
        out_shape=(shape((GX, GY, 1, CAP), i32), shape((NDEV, CAP), i32), shape((1, REQ), i32)),
        in_specs=[whole(v)],
        out_specs=[whole(v)] * 3,
        scratch_shapes=[v((NDEV, REQ), bf16), v((5 * CAP, REQ), bf16)],
        name="bucket",
    )(blocks)


def shifted_sum(field, x, row):
    lane = lax.broadcasted_iota(i32, (8, WIDTH), 1)
    first, final = lane == 0, lane == WIDTH - 1
    at = lambda q, dx, dr: field[q, x + dx, pl.ds(row + dr, 8), :]
    centers = [at(q, 0, 0) for q in range(ZB)]
    up = [pltpu.roll(c, 1, 1) for c in centers]
    down = [pltpu.roll(c, WIDTH - 1, 1) for c in centers]
    sides = []
    for q in range(ZB):
        below = jnp.where(first, up[q - 1] if q > 0 else 0.0, up[q])
        above = jnp.where(final, down[q + 1] if q < ZB - 1 else 0.0, down[q])
        sides.append((at(q, -1, 0) + at(q, 1, 0)) + (at(q, 0, -1) + at(q, 0, 1)) + (below + above))
    return centers, sides


def step_kernel(out_ids, inv_s, pos_s, dens_hbm, weights_hbm, counts, observed, inverse_var,
                ext_out, ids_out, exp_hbm, same_out, base_hbm, arr_hbm,
                dens, mid_ids, in_ids, ids_s,
                rows_exp, served, ret, rows, w_ref, obs4, inv4, ext4, wgt4, sens, stage, parcel,
                xlo, xhi, ylo, yhi, field, smooth, base,
                entered, s_id, r_id, s_row, r_row, local, s_halo, r_halo):
    gx, gy = lax.axis_index("gx"), lax.axis_index("gy")
    me = gx * GY + gy
    gxm, gxp = lax.rem(gx + GX - 1, GX), lax.rem(gx + 1, GX)
    gym, gyp = lax.rem(gy + GY - 1, GY), lax.rem(gy + 1, GY)
    column = [lax.rem(gx + d, GX) for d in (1, 15, 4, 12, 3, 13, 5, 11, 7, 9, 2, 14, 6, 10, 8)]
    line = [lax.rem(gy + d, GY) for d in (1, 7, 2, 6, 3, 5, 4)]
    greeted = [(t, gy) for t in column] + [(gx, t) for t in line] + [(a, b) for a in (gxm, gxp) for b in (gym, gyp)]
    barrier = pltpu.get_barrier_semaphore()
    for to in greeted:
        pl.semaphore_signal(barrier, inc=1, device_id=to, device_id_type=MESH)

    loads = []
    for q in range(ZB):
        part = dens_hbm.at[:, :, pl.ds(q * WIDTH, WIDTH)]
        loads.append(pltpu.make_async_copy(part, field.at[q, pl.ds(2, CX), pl.ds(8, CY)], local.at[q]))
    w_load = pltpu.make_async_copy(weights_hbm, w_ref, local.at[4])
    for load in loads:
        load.start()
    w_load.start()

    pl.semaphore_wait(barrier, len(greeted))
    for t in line:
        pl.semaphore_signal(entered, inc=1, device_id=(gx, t), device_id_type=MESH)
    own = pltpu.make_async_copy(out_ids.at[gx], mid_ids.at[gx], local.at[7])
    own.start()
    for t in column:
        remote(out_ids.at[t], mid_ids.at[gx], s_id.at[0], r_id.at[0], (t, gy)).start()

    for load in loads:
        load.wait()
    halos = [
        (field.at[:, pl.ds(CX, 2), pl.ds(8, CY)], xlo, (gxp, gy)),
        (field.at[:, pl.ds(2, 2), pl.ds(8, CY)], xhi, (gxm, gy)),
        (field.at[:, pl.ds(2, CX), pl.ds(CY, 8)], ylo.at[:, pl.ds(1, CX)], (gx, gyp)),
        (field.at[:, pl.ds(2, CX), pl.ds(8, 8)], yhi.at[:, pl.ds(1, CX)], (gx, gym)),
        (field.at[:, CX + 1, pl.ds(CY, 8)], ylo.at[:, 0], (gxp, gyp)),
        (field.at[:, 2, pl.ds(CY, 8)], ylo.at[:, CX + 1], (gxm, gyp)),
        (field.at[:, CX + 1, pl.ds(8, 8)], yhi.at[:, 0], (gxp, gym)),
        (field.at[:, 2, pl.ds(8, 8)], yhi.at[:, CX + 1], (gxm, gym)),
    ]
    halos = [remote(src, dst, s_halo.at[n], r_halo.at[n], to) for n, (src, dst, to) in enumerate(halos)]

    def gather_source(x, _):
        for q in range(ZB):
            dens[pl.ds(pl.multiple_of(q * CX * CY + x * CY, CY), CY), :] = field[q, x + 2, pl.ds(8, CY), :]
        return 0

    lax.fori_loop(0, CX, gather_source, 0)
    dens[pl.ds(ROWS, 8), :] = jnp.zeros((8, WIDTH), f32)
    own.wait()
    drain(mid_ids.at[pl.ds(0, GX - 1)], r_id.at[0])
    pl.semaphore_wait(entered, len(line))
    own = pltpu.make_async_copy(mid_ids.at[:, gy], in_ids.at[:, gy], local.at[7])
    own.start()
    for t in line:
        remote(mid_ids.at[:, t], in_ids.at[:, gy], s_id.at[1], r_id.at[1], (gx, t)).start()
    for copy in halos:
        copy.start()

    for ref, four in ((observed, obs4), (inverse_var, inv4)):
        wide = jnp.concatenate([ref[...], ref[...]], axis=1)
        four[...] = jnp.concatenate([wide] * 4, axis=0).T
    sens[pl.ds(REQ, 8), :] = jnp.zeros((8, WIDTH), f32)
    own.wait()
    drain(in_ids.at[:, pl.ds(0, GY - 1)], r_id.at[1])
    ids_copy = pltpu.make_async_copy(in_ids, ids_s, local.at[7])
    ids_copy.start()
    ids_copy.wait()
    slot_a, slot_b = lax.broadcasted_iota(i32, (CAP, CAP), 0), lax.broadcasted_iota(i32, (CAP, CAP), 1)
    eye, together = slot_a == slot_b, (slot_a >> 3) == (slot_b >> 3)

    def serve(tx, ty, at):
        for c in range(CAP):
            rows_exp[at, c, :] = dens[ids_s[tx, ty, 0, c], :]
        values = jnp.exp(rows_exp[at])
        rows_exp[at] = values
        served[at] = values.astype(bf16)
        across = jnp.broadcast_to(in_ids[tx, ty].astype(f32), (CAP, CAP))
        down = jnp.sum(jnp.where(eye, across, 0.0), axis=1, keepdims=True)
        same_out[at] = jnp.where((down == across) & together, 1.0, 0.0).astype(bf16)

    def send_rows(j, _):
        tx, ty = peer(gx, gy, j)
        at = tx * GY + ty
        serve(tx, ty, at)
        remote(served.at[at], ret.at[me], s_row.at[0], r_row.at[0], (tx, ty)).start()
        return 0

    lax.fori_loop(1, NDEV, send_rows, 0)
    serve(gx, gy, me)
    keep = pltpu.make_async_copy(served.at[me], ret.at[me], local.at[0])
    keep.start()
    ids_out[...] = in_ids[...]
    exp_store = pltpu.make_async_copy(rows_exp, exp_hbm, local.at[1])
    exp_store.start()

    for copy in halos:
        copy.wait()
    low_x, high_x, low_y, high_y = gx > 0, gx < GX - 1, gy > 0, gy < GY - 1
    blank = jnp.zeros((8, WIDTH), f32)
    for q in range(ZB):
        for n in range(2):
            field[q, n, pl.ds(8, CY), :] = jnp.where(low_x, xlo[q, n], 0.0)
            field[q, CX + 2 + n, pl.ds(8, CY), :] = jnp.where(high_x, xhi[q, n], 0.0)

        def edge(x, _):
            field[q, x + 1, pl.ds(0, 8), :] = jnp.where(low_y, ylo[q, x], 0.0)
            field[q, x + 1, pl.ds(8 + CY, 8), :] = jnp.where(high_y, yhi[q, x], 0.0)
            return 0

        lax.fori_loop(1, CX + 1, edge, 0)
        for x, inside in ((0, low_x), (CX + 1, high_x)):
            field[q, x + 1, pl.ds(0, 8), :] = jnp.where(low_y & inside, ylo[q, x], 0.0)
            field[q, x + 1, pl.ds(8 + CY, 8), :] = jnp.where(high_y & inside, yhi[q, x], 0.0)
    sub = lax.broadcasted_iota(i32, (8, WIDTH), 0)
    top_keep = (sub > 0) | low_y
    bottom_keep = (sub != 1) | high_y

    def smooth_plane(x, inside=None):
        for n in range(9):
            centers, sides = shifted_sum(field, x + 1, 7 + 8 * n)
            for q in range(ZB):
                value = center_weight * centers[q] - sides[q]
                if n == 0:
                    value = jnp.where(top_keep, value, 0.0)
                if n == 8:
                    value = jnp.where(bottom_keep, value, 0.0)
                if inside is not None:
                    value = jnp.where(inside, value, 0.0)
                smooth[q, x, pl.ds(8 * n, 8), :] = value

    def base_plane(x):
        for n in range(8):
            centers, sides = shifted_sum(smooth, x + 1, 8 * n + 1)
            for q in range(ZB):
                prior = center_weight * centers[q] - sides[q]
                now = field[q, x + 2, pl.ds(8 + 8 * n, 8), :]
                base[q, x, pl.ds(8 * n, 8), :] = now - (step_rate * prior_weight) * prior

    smooth_plane(0, low_x)
    smooth_plane(1)
    smooth_plane(2)
    w_load.wait()
    keep.wait()
    drain(ret.at[pl.ds(0, NDEV - 1)], r_row.at[0])

    def widen(n, _):
        for u in range(UNROLL):
            rows[pl.ds(pl.multiple_of((n * UNROLL + u) * CAP, CAP), CAP), :] = ret[n * UNROLL + u].astype(f32)
        return 0

    lax.fori_loop(0, NDEV // UNROLL, widen, 0)
    group = lax.broadcasted_iota(i32, (SLOTS, SLOTS * STARS), 1) >> 5
    mine = group == lax.broadcasted_iota(i32, (SLOTS, SLOTS * STARS), 0)
    lane = lax.broadcasted_iota(i32, (STARS, WIDTH), 1)
    diagonal = (lane & (STARS - 1)) == lax.broadcasted_iota(i32, (STARS, WIDTH), 0)
    star = lax.broadcasted_iota(i32, (1, WIDTH), 1) & (STARS - 1)

    def extinct(i):
        for u in range(UNROLL):
            b = i * UNROLL + u
            totals = [jnp.zeros((STARS, WIDTH), f32) for _ in range(2)]
            for k in range(SLOTS):
                line_k = rows[pl.ds(pos_s[0, k * BLOCKS + b], 1), :]
                totals[k % 2] = totals[k % 2] + w_ref[b, k].astype(f32) * line_k
            total = jnp.sum(totals[0] + totals[1], axis=1, keepdims=True)
            ext = jnp.sum(jnp.where(diagonal, total, 0.0), axis=0, keepdims=True)
            ext4[pl.ds(b, 1), :] = ext
            residual = inv4[pl.ds(b, 1), :] * (ext - obs4[pl.ds(b, 1), :])
            wgt4[pl.ds(b, 1), :] = jnp.where(star < counts[b], residual, 0.0)

    def sensitive(i):
        for u in range(UNROLL):
            b = i * UNROLL + u
            spread = jnp.concatenate([wgt4[pl.ds(b, 1), :]] * (SLOTS * STARS // WIDTH), axis=1)
            left = jnp.where(mine, spread, 0.0).astype(bf16)
            sens[pl.ds(pl.multiple_of(b * SLOTS, SLOTS), SLOTS), :] = jnp.dot(
                left, w_ref[b].reshape(SLOTS * STARS, WIDTH), preferred_element_type=f32
            )

    extinct(0)

    def both(i, _):
        sensitive(i - 1)
        extinct(i)
        return 0

    lax.fori_loop(1, BLOCKS // UNROLL, both, 0)
    sensitive(BLOCKS // UNROLL - 1)

    def pack(at):
        for c in range(CAP):
            stage[at, c, :] = sens[inv_s[at, c], :]
        parcel[at] = stage[at].astype(bf16)

    def give_back(it, _):
        for u in range(UNROLL):
            j = it * UNROLL + u + 1
            tx, ty = peer(gx, gy, j)
            at = tx * GY + ty
            pack(at)
            remote(parcel.at[at], arr_hbm.at[me], s_row.at[1], r_row.at[1], (tx, ty)).start()
        smooth_plane(it + 3, (it < CX - 2) | high_x)
        base_plane(it)
        return 0

    def last_trip():
        for u in range(UNROLL):
            j = NDEV - UNROLL + u + 1
            tx, ty = peer(gx, gy, j)
            at = tx * GY + ty
            pack(at)
            if u < UNROLL - 1:
                remote(parcel.at[at], arr_hbm.at[me], s_row.at[1], r_row.at[1], (tx, ty)).start()
        base_plane(CX - 1)

    lax.fori_loop(0, NDEV // UNROLL - 1, give_back, 0)
    last_trip()
    keep = pltpu.make_async_copy(parcel.at[me], arr_hbm.at[me], local.at[0])
    keep.start()
    base_store = pltpu.make_async_copy(base, base_hbm, local.at[2])
    base_store.start()
    ext_out[...] = jnp.concatenate([ext4[...], ext4[...]], axis=0).T[:STARS, :BLOCKS]
    keep.wait()
    exp_store.wait()
    base_store.wait()
    drain(out_ids.at[pl.ds(0, GX - 1)], s_id.at[0])
    drain(mid_ids.at[:, pl.ds(0, GY - 1)], s_id.at[1])
    drain(served.at[pl.ds(0, NDEV - 1)], s_row.at[0])
    drain(parcel.at[pl.ds(0, NDEV - 1)], s_row.at[1])
    drain(arr_hbm.at[pl.ds(0, NDEV - 1)], r_row.at[1])


def step(ids, inv, pos, dens, weights, counts, observed, inverse_var):
    shape = jax.ShapeDtypeStruct
    v = pltpu.VMEM
    return pl.pallas_call(
        step_kernel,
        out_shape=(
            shape((STARS, BLOCKS), f32),
            shape((GX, GY, 1, CAP), i32),
            shape((NDEV, CAP, WIDTH), f32),
            shape((NDEV, CAP, CAP), bf16),
            shape((ZB, CX, CY, WIDTH), f32),
            shape((NDEV, CAP, WIDTH), bf16),
        ),
        in_specs=[
            whole(v), whole(pltpu.SMEM), whole(pltpu.SMEM),
            whole(pltpu.HBM), whole(pltpu.HBM), whole(pltpu.SMEM), whole(v), whole(v),
        ],
        out_specs=[whole(v), whole(v), whole(pltpu.HBM), whole(v), whole(pltpu.HBM), whole(pltpu.HBM)],
        scratch_shapes=[
            v((ROWS + 8, WIDTH), f32),
            v((GX, GY, 1, CAP), i32), v((GX, GY, 1, CAP), i32), pltpu.SMEM((GX, GY, 1, CAP), i32),
            v((NDEV, CAP, WIDTH), f32), v((NDEV, CAP, WIDTH), bf16), v((NDEV, CAP, WIDTH), bf16),
            v((NDEV * CAP, WIDTH), f32), v((BLOCKS, SLOTS, STARS, WIDTH), bf16),
            v((WIDTH, WIDTH), f32), v((WIDTH, WIDTH), f32), v((BLOCKS, WIDTH), f32), v((BLOCKS, WIDTH), f32),
            v((REQ + 8, WIDTH), f32), v((NDEV, CAP, WIDTH), f32), v((NDEV, CAP, WIDTH), bf16),
            v((ZB, 2, CY, WIDTH), f32), v((ZB, 2, CY, WIDTH), f32),
            v((ZB, CX + 2, 8, WIDTH), f32), v((ZB, CX + 2, 8, WIDTH), f32),
            v((ZB, CX + 4, CY + 16, WIDTH), f32), v((ZB, CX + 2, CY + 8, WIDTH), f32), v((ZB, CX, CY, WIDTH), f32),
            pltpu.SemaphoreType.REGULAR, DMA((2,)), DMA((2,)), DMA((2,)), DMA((2,)), DMA((8,)), DMA((8,)), DMA((8,)),
        ],
        name="step",
        compiler_params=pltpu.CompilerParams(collective_id=0, has_side_effects=True, vmem_limit_bytes=60 << 20),
    )(ids, inv, pos, dens, weights, counts, observed, inverse_var)


def update_kernel(ids, ext_in, exp_hbm, same, base_hbm, arr_hbm, ext_out, out_hbm, new, rows_exp, arrived, add, sem):
    load_exp = pltpu.make_async_copy(exp_hbm, rows_exp, sem.at[0])
    load_arr = pltpu.make_async_copy(arr_hbm, arrived, sem.at[1])
    load_exp.start()
    load_arr.start()
    bases = []
    for q in range(ZB):
        bases.append(pltpu.make_async_copy(base_hbm.at[q], new.at[pl.ds(q * CX * CY, CX * CY)], sem.at[2 + q]))
        bases[q].start()
    ext_out[...] = ext_in[...]
    new[pl.ds(ROWS, 8), :] = jnp.zeros((8, WIDTH), f32)
    load_exp.wait()
    load_arr.wait()

    def scale(n, _):
        for u in range(UNROLL):
            t = n * UNROLL + u
            add[t] = step_rate * rows_exp[t] * jnp.dot(same[t], arrived[t], preferred_element_type=f32)
        return 0

    lax.fori_loop(0, NDEV // UNROLL, scale, 0)
    for load in bases:
        load.wait()

    def source(t, _):
        tx, ty = t // GY, lax.rem(t, GY)
        for first in range(0, CAP, 8):
            at = [ids[tx, ty, 0, first + c] for c in range(8)]
            values = [new[pl.ds(n, 1), :] - add[t, pl.ds(first + c, 1), :] for c, n in enumerate(at)]
            for n, value in zip(at, values):
                new[pl.ds(n, 1), :] = value
        return 0

    lax.fori_loop(0, NDEV, source, 0)
    stores = []
    for q in range(ZB):
        rows_of = new.at[pl.ds(q * CX * CY, CX * CY)]
        stores.append(pltpu.make_async_copy(
            rows_of.reshape(CX, CY, WIDTH), out_hbm.at[:, :, pl.ds(q * WIDTH, WIDTH)], sem.at[2 + q]
        ))
        stores[q].start()
    for store in stores:
        store.wait()


def update(ids, ext, rows_exp, same, base, arrived):
    v = pltpu.VMEM
    return pl.pallas_call(
        update_kernel,
        out_shape=(jax.ShapeDtypeStruct((STARS, BLOCKS), f32), jax.ShapeDtypeStruct((CX, CY, ZB * WIDTH), f32)),
        in_specs=[whole(pltpu.SMEM), whole(v), whole(pltpu.HBM), whole(v), whole(pltpu.HBM), whole(pltpu.HBM)],
        out_specs=[whole(v), whole(pltpu.HBM)],
        scratch_shapes=[
            v((ROWS + 8, WIDTH), f32), v((NDEV, CAP, WIDTH), f32), v((NDEV, CAP, WIDTH), bf16), v((NDEV, CAP, WIDTH), f32),
            DMA((6,)),
        ],
        name="update",
        compiler_params=pltpu.CompilerParams(vmem_limit_bytes=24 << 20),
    )(ids, ext, rows_exp, same, base.reshape(ZB, CX * CY, WIDTH), arrived)


def on_device(log_density, weights, observed, inverse_var, star_counts, block_ids):
    ids, inv, pos = bucket(block_ids.T)
    ext, ids, rows_exp, same, base, arrived = step(
        ids, inv, pos, log_density, weights, star_counts, observed.T, inverse_var.T
    )
    ext, new = update(ids, ext, rows_exp, same, base, arrived)
    return (new, ext.T)


def solution(mesh):
    placed = (
        P("gx", "gy", None),
        P(("gx", "gy"), None, None, None),
        P(("gx", "gy"), None),
        P(("gx", "gy"), None),
        P(("gx", "gy")),
        P(("gx", "gy"), None),
    )
    return jax.shard_map(
        on_device,
        mesh=mesh,
        in_specs=placed,
        out_specs=(P("gx", "gy", None), P(("gx", "gy"), None)),
        check_vma=False,
    )
```

```python
import jax
import jax.numpy as jnp
from jax import lax
from jax.experimental import pallas as pl
from jax.experimental.pallas import tpu as pltpu
from jax.sharding import PartitionSpec as P

MESH = pl.DeviceIdType.MESH
DMA = pltpu.SemaphoreType.DMA
shift_kappa = 0.5
prior_weight = 0.05
step_rate = 2.0
f32, bf16, i32 = jnp.float32, jnp.bfloat16, jnp.int32

GX, GY = 16, 8
NDEV, CAP, WIDTH = 128, 32, 128
BLOCKS, SLOTS, STARS = 64, 32, 32
REQ = BLOCKS * SLOTS
CX, CY, ZB = 32, 64, 4
ROWS = CX * CY * ZB
LOCAL_BITS = 13
UNROLL = 4
center_weight = shift_kappa + 6.0


def whole(space):
    return pl.BlockSpec(memory_space=space)


def remote(src, dst, send, recv, to):
    return pltpu.make_async_remote_copy(
        src_ref=src, dst_ref=dst, send_sem=send, recv_sem=recv, device_id=to, device_id_type=MESH
    )


def drain(ref, sem):
    pltpu.make_async_copy(ref, ref, sem).wait()


def peer(gx, gy, j):
    o = lax.rem(j * 37, NDEV)
    x = lax.rem(gx // 4 + o // 32, 4)
    y = lax.rem(gx + lax.rem(o // 8, 4), 4)
    z = lax.rem(gy // 2 + lax.rem(o // 2, 4), 4)
    c = lax.rem(gy + o, 2)
    return x * 4 + y, z * 2 + c


def bucket_kernel(blocks, out_ids, inv_ref, pos_ref, at_ref, bt_ref):
    ids = jnp.concatenate([blocks[k:k + 1, :] for k in range(SLOTS)], axis=1)
    target = ids >> LOCAL_BITS
    within = ids & (ROWS - 1)
    within = (within & (ZB - 1)) * (CX * CY) + (within >> 2)
    order = lax.broadcasted_iota(i32, (1, REQ), 1)
    order = (order & (BLOCKS - 1)) * SLOTS + (order >> 6)
    at_ref[...] = jnp.where(lax.broadcasted_iota(i32, (NDEV, REQ), 0) == target, 1.0, 0.0).astype(bf16)
    step = 256
    before = lax.broadcasted_iota(i32, (step, step), 0) < lax.broadcasted_iota(i32, (step, step), 1)
    before = jnp.where(before, 1.0, 0.0).astype(bf16)
    running = jnp.zeros((NDEV, 1), f32)
    slot = lax.broadcasted_iota(i32, (CAP, step), 0)
    for k in range(REQ // step):
        cut = slice(k * step, (k + 1) * step)
        part = at_ref[:, cut]
        prefix = jnp.dot(part, before, preferred_element_type=f32) + running
        wide = part.astype(f32)
        rank = jnp.sum(wide * prefix, axis=0, keepdims=True).astype(i32)
        running = running + jnp.sum(wide, axis=1, keepdims=True)
        hit = slot == rank
        pos_ref[:, cut] = target[:, cut] * CAP + rank
        for n, value in enumerate((within[:, cut] >> 7, within[:, cut] & 127, order[:, cut] >> 7, order[:, cut] & 127, None)):
            value = 1.0 if value is None else value.astype(f32)
            bt_ref[n * CAP:(n + 1) * CAP, cut] = jnp.where(hit, value, 0.0).astype(bf16)
    table = lax.dot_general(at_ref[...], bt_ref[...], (((1,), (1,)), ((), ())), preferred_element_type=f32)
    parts = [table[:, n * CAP:(n + 1) * CAP] for n in range(5)]
    present = parts[4] > 0.5
    row = jnp.where(present, parts[0] * 128.0 + parts[1], float(ROWS)).astype(i32)
    out_ids[...] = row.reshape(GX, GY, 1, CAP)
    inv_ref[...] = jnp.where(present, parts[2] * 128.0 + parts[3], float(REQ)).astype(i32)


def bucket(blocks):
    shape, v = jax.ShapeDtypeStruct, pltpu.VMEM
    return pl.pallas_call(
        bucket_kernel,
        out_shape=(shape((GX, GY, 1, CAP), i32), shape((NDEV, CAP), i32), shape((1, REQ), i32)),
        in_specs=[whole(v)],
        out_specs=[whole(v)] * 3,
        scratch_shapes=[v((NDEV, REQ), bf16), v((5 * CAP, REQ), bf16)],
        name="bucket",
    )(blocks)


def shifted_sum(field, x, row):
    lane = lax.broadcasted_iota(i32, (8, WIDTH), 1)
    first, final = lane == 0, lane == WIDTH - 1
    at = lambda q, dx, dr: field[q, x + dx, pl.ds(row + dr, 8), :]
    centers = [at(q, 0, 0) for q in range(ZB)]
    up = [pltpu.roll(c, 1, 1) for c in centers]
    down = [pltpu.roll(c, WIDTH - 1, 1) for c in centers]
    sides = []
    for q in range(ZB):
        below = jnp.where(first, up[q - 1] if q > 0 else 0.0, up[q])
        above = jnp.where(final, down[q + 1] if q < ZB - 1 else 0.0, down[q])
        sides.append((at(q, -1, 0) + at(q, 1, 0)) + (at(q, 0, -1) + at(q, 0, 1)) + (below + above))
    return centers, sides


def step_kernel(out_ids, inv_s, pos_s, dens_hbm, weights_hbm, counts, observed, inverse_var,
                ext_out, ids_out, exp_hbm, base_hbm, arr_hbm,
                dens, mid_ids, in_ids, ids_s,
                rows_exp, served, ret, rows, w_ref, obs4, inv4, ext4, wgt4, sens, stage, parcel,
                xlo, xhi, ylo, yhi, field, smooth, base,
                entered, s_id, r_id, s_row, r_row, local, s_halo, r_halo):
    gx, gy = lax.axis_index("gx"), lax.axis_index("gy")
    me = gx * GY + gy
    gxm, gxp = lax.rem(gx + GX - 1, GX), lax.rem(gx + 1, GX)
    gym, gyp = lax.rem(gy + GY - 1, GY), lax.rem(gy + 1, GY)
    column = [lax.rem(gx + d, GX) for d in (1, 15, 4, 12, 3, 13, 5, 11, 7, 9, 2, 14, 6, 10, 8)]
    line = [lax.rem(gy + d, GY) for d in (1, 7, 2, 6, 3, 5, 4)]
    greeted = [(t, gy) for t in column] + [(gx, t) for t in line] + [(a, b) for a in (gxm, gxp) for b in (gym, gyp)]
    barrier = pltpu.get_barrier_semaphore()
    for to in greeted:
        pl.semaphore_signal(barrier, inc=1, device_id=to, device_id_type=MESH)

    loads = []
    for q in range(ZB):
        part = dens_hbm.at[:, :, pl.ds(q * WIDTH, WIDTH)]
        loads.append(pltpu.make_async_copy(part, field.at[q, pl.ds(2, CX), pl.ds(8, CY)], local.at[q]))
    w_load = pltpu.make_async_copy(weights_hbm, w_ref, local.at[4])
    for load in loads:
        load.start()
    w_load.start()

    pl.semaphore_wait(barrier, len(greeted))
    for t in line:
        pl.semaphore_signal(entered, inc=1, device_id=(gx, t), device_id_type=MESH)
    own = pltpu.make_async_copy(out_ids.at[gx], mid_ids.at[gx], local.at[7])
    own.start()
    for t in column:
        remote(out_ids.at[t], mid_ids.at[gx], s_id.at[0], r_id.at[0], (t, gy)).start()

    for load in loads:
        load.wait()
    halos = [
        (field.at[:, pl.ds(CX, 2), pl.ds(8, CY)], xlo, (gxp, gy)),
        (field.at[:, pl.ds(2, 2), pl.ds(8, CY)], xhi, (gxm, gy)),
        (field.at[:, pl.ds(2, CX), pl.ds(CY, 8)], ylo.at[:, pl.ds(1, CX)], (gx, gyp)),
        (field.at[:, pl.ds(2, CX), pl.ds(8, 8)], yhi.at[:, pl.ds(1, CX)], (gx, gym)),
        (field.at[:, CX + 1, pl.ds(CY, 8)], ylo.at[:, 0], (gxp, gyp)),
        (field.at[:, 2, pl.ds(CY, 8)], ylo.at[:, CX + 1], (gxm, gyp)),
        (field.at[:, CX + 1, pl.ds(8, 8)], yhi.at[:, 0], (gxp, gym)),
        (field.at[:, 2, pl.ds(8, 8)], yhi.at[:, CX + 1], (gxm, gym)),
    ]
    halos = [remote(src, dst, s_halo.at[n], r_halo.at[n], to) for n, (src, dst, to) in enumerate(halos)]

    def gather_source(x, _):
        for q in range(ZB):
            dens[pl.ds(pl.multiple_of(q * CX * CY + x * CY, CY), CY), :] = field[q, x + 2, pl.ds(8, CY), :]
        return 0

    lax.fori_loop(0, CX, gather_source, 0)
    dens[pl.ds(ROWS, 8), :] = jnp.zeros((8, WIDTH), f32)
    own.wait()
    drain(mid_ids.at[pl.ds(0, GX - 1)], r_id.at[0])
    pl.semaphore_wait(entered, len(line))
    own = pltpu.make_async_copy(mid_ids.at[:, gy], in_ids.at[:, gy], local.at[7])
    own.start()
    for t in line:
        remote(mid_ids.at[:, t], in_ids.at[:, gy], s_id.at[1], r_id.at[1], (gx, t)).start()
    for copy in halos:
        copy.start()

    for ref, four in ((observed, obs4), (inverse_var, inv4)):
        wide = jnp.concatenate([ref[...], ref[...]], axis=1)
        four[...] = jnp.concatenate([wide] * 4, axis=0).T
    sens[pl.ds(REQ, 8), :] = jnp.zeros((8, WIDTH), f32)
    own.wait()
    drain(in_ids.at[:, pl.ds(0, GY - 1)], r_id.at[1])
    ids_copy = pltpu.make_async_copy(in_ids, ids_s, local.at[7])
    ids_copy.start()
    ids_copy.wait()

    def serve(tx, ty, at):
        for c in range(CAP):
            rows_exp[at, c, :] = dens[ids_s[tx, ty, 0, c], :]
        values = jnp.exp(rows_exp[at])
        rows_exp[at] = step_rate * values
        served[at] = values.astype(bf16)

    def send_rows(j, _):
        tx, ty = peer(gx, gy, j)
        at = tx * GY + ty
        serve(tx, ty, at)
        remote(served.at[at], ret.at[me], s_row.at[0], r_row.at[0], (tx, ty)).start()
        return 0

    lax.fori_loop(1, NDEV, send_rows, 0)
    serve(gx, gy, me)
    keep = pltpu.make_async_copy(served.at[me], ret.at[me], local.at[0])
    keep.start()
    ids_out[...] = in_ids[...]
    exp_store = pltpu.make_async_copy(rows_exp, exp_hbm, local.at[1])
    exp_store.start()

    for copy in halos:
        copy.wait()
    low_x, high_x, low_y, high_y = gx > 0, gx < GX - 1, gy > 0, gy < GY - 1
    blank = jnp.zeros((8, WIDTH), f32)
    for q in range(ZB):
        for n in range(2):
            field[q, n, pl.ds(8, CY), :] = jnp.where(low_x, xlo[q, n], 0.0)
            field[q, CX + 2 + n, pl.ds(8, CY), :] = jnp.where(high_x, xhi[q, n], 0.0)

        def edge(x, _):
            field[q, x + 1, pl.ds(0, 8), :] = jnp.where(low_y, ylo[q, x], 0.0)
            field[q, x + 1, pl.ds(8 + CY, 8), :] = jnp.where(high_y, yhi[q, x], 0.0)
            return 0

        lax.fori_loop(1, CX + 1, edge, 0)
        for x, inside in ((0, low_x), (CX + 1, high_x)):
            field[q, x + 1, pl.ds(0, 8), :] = jnp.where(low_y & inside, ylo[q, x], 0.0)
            field[q, x + 1, pl.ds(8 + CY, 8), :] = jnp.where(high_y & inside, yhi[q, x], 0.0)
    sub = lax.broadcasted_iota(i32, (8, WIDTH), 0)
    top_keep = (sub > 0) | low_y
    bottom_keep = (sub != 1) | high_y

    def smooth_plane(x, inside=None):
        for n in range(9):
            centers, sides = shifted_sum(field, x + 1, 7 + 8 * n)
            for q in range(ZB):
                value = center_weight * centers[q] - sides[q]
                if n == 0:
                    value = jnp.where(top_keep, value, 0.0)
                if n == 8:
                    value = jnp.where(bottom_keep, value, 0.0)
                if inside is not None:
                    value = jnp.where(inside, value, 0.0)
                smooth[q, x, pl.ds(8 * n, 8), :] = value

    def base_plane(x):
        for n in range(8):
            centers, sides = shifted_sum(smooth, x + 1, 8 * n + 1)
            for q in range(ZB):
                prior = center_weight * centers[q] - sides[q]
                now = field[q, x + 2, pl.ds(8 + 8 * n, 8), :]
                base[q, x, pl.ds(8 * n, 8), :] = now - (step_rate * prior_weight) * prior

    smooth_plane(0, low_x)
    smooth_plane(1)
    smooth_plane(2)
    w_load.wait()
    keep.wait()
    drain(ret.at[pl.ds(0, NDEV - 1)], r_row.at[0])

    def widen(n, _):
        for u in range(UNROLL):
            rows[pl.ds(pl.multiple_of((n * UNROLL + u) * CAP, CAP), CAP), :] = ret[n * UNROLL + u].astype(f32)
        return 0

    lax.fori_loop(0, NDEV // UNROLL, widen, 0)
    deep = 8 * STARS
    mine = (lax.broadcasted_iota(i32, (8, deep), 1) >> 5) == lax.broadcasted_iota(i32, (8, deep), 0)
    lane = lax.broadcasted_iota(i32, (STARS, WIDTH), 1)
    diagonal = (lane & (STARS - 1)) == lax.broadcasted_iota(i32, (STARS, WIDTH), 0)
    star = lax.broadcasted_iota(i32, (1, WIDTH), 1) & (STARS - 1)

    def extinct(i):
        for u in range(UNROLL):
            b = i * UNROLL + u
            totals = [jnp.zeros((STARS, WIDTH), f32) for _ in range(2)]
            for k in range(SLOTS):
                line_k = rows[pl.ds(pos_s[0, k * BLOCKS + b], 1), :]
                totals[k % 2] = totals[k % 2] + w_ref[b, k].astype(f32) * line_k
            total = jnp.sum(totals[0] + totals[1], axis=1, keepdims=True)
            ext = jnp.sum(jnp.where(diagonal, total, 0.0), axis=0, keepdims=True)
            ext4[pl.ds(b, 1), :] = ext
            residual = inv4[pl.ds(b, 1), :] * (ext - obs4[pl.ds(b, 1), :])
            wgt4[pl.ds(b, 1), :] = jnp.where(star < counts[b], residual, 0.0)

    def sensitive(i):
        for u in range(UNROLL):
            b = i * UNROLL + u
            line_b = wgt4[pl.ds(b, 1), :]
            left = jnp.where(mine, jnp.concatenate([line_b, line_b], axis=1), 0.0).astype(bf16)
            for n in range(SLOTS // 8):
                sens[pl.ds(pl.multiple_of(b * SLOTS + n * 8, 8), 8), :] = jnp.dot(
                    left, w_ref[b, pl.ds(n * 8, 8)].reshape(deep, WIDTH), preferred_element_type=f32
                )

    extinct(0)

    def both(i, _):
        sensitive(i - 1)
        extinct(i)
        return 0

    lax.fori_loop(1, BLOCKS // UNROLL, both, 0)
    sensitive(BLOCKS // UNROLL - 1)

    slot_a, slot_b = lax.broadcasted_iota(i32, (CAP, CAP), 0), lax.broadcasted_iota(i32, (CAP, CAP), 1)
    eye, together = slot_a == slot_b, (slot_a >> 3) == (slot_b >> 3)

    def pack(tx, ty, at):
        for c in range(CAP):
            stage[at, c, :] = sens[inv_s[at, c], :]
        across = jnp.broadcast_to(out_ids[tx, ty].astype(f32), (CAP, CAP))
        down = jnp.sum(jnp.where(eye, across, 0.0), axis=1, keepdims=True)
        same = jnp.where((down == across) & together, 1.0, 0.0).astype(bf16)
        parcel[at] = jnp.dot(same, stage[at].astype(bf16), preferred_element_type=f32).astype(bf16)

    def give_back(it, _):
        for u in range(UNROLL):
            j = it * UNROLL + u + 1
            tx, ty = peer(gx, gy, j)
            at = tx * GY + ty
            pack(tx, ty, at)
            remote(parcel.at[at], arr_hbm.at[me], s_row.at[1], r_row.at[1], (tx, ty)).start()
        smooth_plane(it + 3, (it < CX - 2) | high_x)
        base_plane(it)
        return 0

    def last_trip():
        for u in range(UNROLL):
            j = NDEV - UNROLL + u + 1
            tx, ty = peer(gx, gy, j)
            at = tx * GY + ty
            pack(tx, ty, at)
            if u < UNROLL - 1:
                remote(parcel.at[at], arr_hbm.at[me], s_row.at[1], r_row.at[1], (tx, ty)).start()
        base_plane(CX - 1)

    lax.fori_loop(0, NDEV // UNROLL - 1, give_back, 0)
    last_trip()
    keep = pltpu.make_async_copy(parcel.at[me], arr_hbm.at[me], local.at[0])
    keep.start()
    base_store = pltpu.make_async_copy(base, base_hbm, local.at[2])
    base_store.start()
    ext_out[...] = jnp.concatenate([ext4[...], ext4[...]], axis=0).T[:STARS, :BLOCKS]
    keep.wait()
    exp_store.wait()
    base_store.wait()
    drain(out_ids.at[pl.ds(0, GX - 1)], s_id.at[0])
    drain(mid_ids.at[:, pl.ds(0, GY - 1)], s_id.at[1])
    drain(served.at[pl.ds(0, NDEV - 1)], s_row.at[0])
    drain(parcel.at[pl.ds(0, NDEV - 1)], s_row.at[1])
    drain(arr_hbm.at[pl.ds(0, NDEV - 1)], r_row.at[1])


def step(ids, inv, pos, dens, weights, counts, observed, inverse_var):
    shape = jax.ShapeDtypeStruct
    v = pltpu.VMEM
    return pl.pallas_call(
        step_kernel,
        out_shape=(
            shape((STARS, BLOCKS), f32),
            shape((GX, GY, 1, CAP), i32),
            shape((NDEV, CAP, WIDTH), f32),
            shape((ZB, CX, CY, WIDTH), f32),
            shape((NDEV, CAP, WIDTH), bf16),
        ),
        in_specs=[
            whole(v), whole(pltpu.SMEM), whole(pltpu.SMEM),
            whole(pltpu.HBM), whole(pltpu.HBM), whole(pltpu.SMEM), whole(v), whole(v),
        ],
        out_specs=[whole(v), whole(v), whole(pltpu.HBM), whole(pltpu.HBM), whole(pltpu.HBM)],
        scratch_shapes=[
            v((ROWS + 8, WIDTH), f32),
            v((GX, GY, 1, CAP), i32), v((GX, GY, 1, CAP), i32), pltpu.SMEM((GX, GY, 1, CAP), i32),
            v((NDEV, CAP, WIDTH), f32), v((NDEV, CAP, WIDTH), bf16), v((NDEV, CAP, WIDTH), bf16),
            v((NDEV * CAP, WIDTH), f32), v((BLOCKS, SLOTS, STARS, WIDTH), bf16),
            v((WIDTH, WIDTH), f32), v((WIDTH, WIDTH), f32), v((BLOCKS, WIDTH), f32), v((BLOCKS, WIDTH), f32),
            v((REQ + 8, WIDTH), f32), v((NDEV, CAP, WIDTH), f32), v((NDEV, CAP, WIDTH), bf16),
            v((ZB, 2, CY, WIDTH), f32), v((ZB, 2, CY, WIDTH), f32),
            v((ZB, CX + 2, 8, WIDTH), f32), v((ZB, CX + 2, 8, WIDTH), f32),
            v((ZB, CX + 4, CY + 16, WIDTH), f32), v((ZB, CX + 2, CY + 8, WIDTH), f32), v((ZB, CX, CY, WIDTH), f32),
            pltpu.SemaphoreType.REGULAR, DMA((2,)), DMA((2,)), DMA((2,)), DMA((2,)), DMA((8,)), DMA((8,)), DMA((8,)),
        ],
        name="step",
        compiler_params=pltpu.CompilerParams(collective_id=0, has_side_effects=True, vmem_limit_bytes=60 << 20),
    )(ids, inv, pos, dens, weights, counts, observed, inverse_var)


def update_kernel(ids, ext_in, exp_hbm, base_hbm, arr_hbm, ext_out, out_hbm, new, rows_exp, arrived, add, sem):
    load_exp = pltpu.make_async_copy(exp_hbm, rows_exp, sem.at[0])
    load_arr = pltpu.make_async_copy(arr_hbm, arrived, sem.at[1])
    load_exp.start()
    load_arr.start()
    bases = []
    for q in range(ZB):
        bases.append(pltpu.make_async_copy(base_hbm.at[q], new.at[pl.ds(q * CX * CY, CX * CY)], sem.at[2 + q]))
        bases[q].start()
    ext_out[...] = ext_in[...]
    new[pl.ds(ROWS, 8), :] = jnp.zeros((8, WIDTH), f32)
    load_exp.wait()
    load_arr.wait()

    def scale(n, _):
        for u in range(UNROLL):
            t = n * UNROLL + u
            add[t] = rows_exp[t] * arrived[t].astype(f32)
        return 0

    lax.fori_loop(0, NDEV // UNROLL, scale, 0)
    for load in bases:
        load.wait()

    def source(t, _):
        tx, ty = t // GY, lax.rem(t, GY)

        def eight(first):
            at = [ids[tx, ty, 0, first + c] for c in range(8)]
            values = [new[pl.ds(n, 1), :] - add[t, pl.ds(first + c, 1), :] for c, n in enumerate(at)]
            for n, value in zip(at, values):
                new[pl.ds(n, 1), :] = value

        eight(0)
        eight(8)

        @pl.when(ids[tx, ty, 0, 16] < ROWS)
        def _():
            eight(16)

            @pl.when(ids[tx, ty, 0, 24] < ROWS)
            def _():
                eight(24)

        return 0

    lax.fori_loop(0, NDEV, source, 0)
    stores = []
    for q in range(ZB):
        rows_of = new.at[pl.ds(q * CX * CY, CX * CY)]
        stores.append(pltpu.make_async_copy(
            rows_of.reshape(CX, CY, WIDTH), out_hbm.at[:, :, pl.ds(q * WIDTH, WIDTH)], sem.at[2 + q]
        ))
        stores[q].start()
    for store in stores:
        store.wait()


def update(ids, ext, rows_exp, base, arrived):
    v = pltpu.VMEM
    return pl.pallas_call(
        update_kernel,
        out_shape=(jax.ShapeDtypeStruct((STARS, BLOCKS), f32), jax.ShapeDtypeStruct((CX, CY, ZB * WIDTH), f32)),
        in_specs=[whole(pltpu.SMEM), whole(v), whole(pltpu.HBM), whole(pltpu.HBM), whole(pltpu.HBM)],
        out_specs=[whole(v), whole(pltpu.HBM)],
        scratch_shapes=[
            v((ROWS + 8, WIDTH), f32), v((NDEV, CAP, WIDTH), f32), v((NDEV, CAP, WIDTH), bf16), v((NDEV, CAP, WIDTH), f32),
            DMA((6,)),
        ],
        name="update",
        compiler_params=pltpu.CompilerParams(vmem_limit_bytes=62 << 20),
    )(ids, ext, rows_exp, base.reshape(ZB, CX * CY, WIDTH), arrived)


def on_device(log_density, weights, observed, inverse_var, star_counts, block_ids):
    ids, inv, pos = bucket(block_ids.T)
    ext, ids, rows_exp, base, arrived = step(
        ids, inv, pos, log_density, weights, star_counts, observed.T, inverse_var.T
    )
    ext, new = update(ids, ext, rows_exp, base, arrived)
    return (new, ext.T)


def solution(mesh):
    placed = (
        P("gx", "gy", None),
        P(("gx", "gy"), None, None, None),
        P(("gx", "gy"), None),
        P(("gx", "gy"), None),
        P(("gx", "gy")),
        P(("gx", "gy"), None),
    )
    return jax.shard_map(
        on_device,
        mesh=mesh,
        in_specs=placed,
        out_specs=(P("gx", "gy", None), P(("gx", "gy"), None)),
        check_vma=False,
    )
```

```python
import jax
import jax.numpy as jnp
from jax import lax
from jax.experimental import pallas as pl
from jax.experimental.pallas import tpu as pltpu
from jax.sharding import PartitionSpec as P

MESH = pl.DeviceIdType.MESH
DMA = pltpu.SemaphoreType.DMA
shift_kappa = 0.5
prior_weight = 0.05
step_rate = 2.0
f32, bf16, i32 = jnp.float32, jnp.bfloat16, jnp.int32

GX, GY = 16, 8
NDEV, CAP, WIDTH = 128, 32, 128
BLOCKS, SLOTS, STARS = 64, 32, 32
REQ = BLOCKS * SLOTS
CX, CY, ZB = 32, 64, 4
ROWS = CX * CY * ZB
LOCAL_BITS = 13
UNROLL = 4
center_weight = shift_kappa + 6.0


def whole(space):
    return pl.BlockSpec(memory_space=space)


def remote(src, dst, send, recv, to):
    return pltpu.make_async_remote_copy(
        src_ref=src, dst_ref=dst, send_sem=send, recv_sem=recv, device_id=to, device_id_type=MESH
    )


def drain(ref, sem):
    pltpu.make_async_copy(ref, ref, sem).wait()


def peer(gx, gy, j):
    o = lax.rem(j * 37, NDEV)
    x = lax.rem(gx // 4 + o // 32, 4)
    y = lax.rem(gx + lax.rem(o // 8, 4), 4)
    z = lax.rem(gy // 2 + lax.rem(o // 2, 4), 4)
    c = lax.rem(gy + o, 2)
    return x * 4 + y, z * 2 + c


def bucket_kernel(blocks, out_ids, inv_ref, pos_ref, at_ref, bt_ref):
    ids = jnp.concatenate([blocks[k:k + 1, :] for k in range(SLOTS)], axis=1)
    target = ids >> LOCAL_BITS
    within = ids & (ROWS - 1)
    within = (within & (ZB - 1)) * (CX * CY) + (within >> 2)
    order = lax.broadcasted_iota(i32, (1, REQ), 1)
    order = (order & (BLOCKS - 1)) * SLOTS + (order >> 6)
    at_ref[...] = jnp.where(lax.broadcasted_iota(i32, (NDEV, REQ), 0) == target, 1.0, 0.0).astype(bf16)
    step = 256
    before = lax.broadcasted_iota(i32, (step, step), 0) < lax.broadcasted_iota(i32, (step, step), 1)
    before = jnp.where(before, 1.0, 0.0).astype(bf16)
    running = jnp.zeros((NDEV, 1), f32)
    slot = lax.broadcasted_iota(i32, (CAP, step), 0)
    for k in range(REQ // step):
        cut = slice(k * step, (k + 1) * step)
        part = at_ref[:, cut]
        prefix = jnp.dot(part, before, preferred_element_type=f32) + running
        wide = part.astype(f32)
        rank = jnp.sum(wide * prefix, axis=0, keepdims=True).astype(i32)
        running = running + jnp.sum(wide, axis=1, keepdims=True)
        hit = slot == rank
        pos_ref[:, cut] = target[:, cut] * CAP + rank
        for n, value in enumerate((within[:, cut] >> 7, within[:, cut] & 127, order[:, cut] >> 7, order[:, cut] & 127, None)):
            value = 1.0 if value is None else value.astype(f32)
            bt_ref[n * CAP:(n + 1) * CAP, cut] = jnp.where(hit, value, 0.0).astype(bf16)
    table = lax.dot_general(at_ref[...], bt_ref[...], (((1,), (1,)), ((), ())), preferred_element_type=f32)
    parts = [table[:, n * CAP:(n + 1) * CAP] for n in range(5)]
    present = parts[4] > 0.5
    row = jnp.where(present, parts[0] * 128.0 + parts[1], float(ROWS)).astype(i32)
    out_ids[...] = row.reshape(GX, GY, 1, CAP)
    inv_ref[...] = jnp.where(present, parts[2] * 128.0 + parts[3], float(REQ)).astype(i32)


def bucket(blocks):
    shape, v = jax.ShapeDtypeStruct, pltpu.VMEM
    return pl.pallas_call(
        bucket_kernel,
        out_shape=(shape((GX, GY, 1, CAP), i32), shape((NDEV, CAP), i32), shape((1, REQ), i32)),
        in_specs=[whole(v)],
        out_specs=[whole(v)] * 3,
        scratch_shapes=[v((NDEV, REQ), bf16), v((5 * CAP, REQ), bf16)],
        name="bucket",
    )(blocks)


def shifted_sum(field, x, row):
    lane = lax.broadcasted_iota(i32, (8, WIDTH), 1)
    first, final = lane == 0, lane == WIDTH - 1
    at = lambda q, dx, dr: field[q, x + dx, pl.ds(row + dr, 8), :]
    centers = [at(q, 0, 0) for q in range(ZB)]
    up = [pltpu.roll(c, 1, 1) for c in centers]
    down = [pltpu.roll(c, WIDTH - 1, 1) for c in centers]
    sides = []
    for q in range(ZB):
        below = jnp.where(first, up[q - 1] if q > 0 else 0.0, up[q])
        above = jnp.where(final, down[q + 1] if q < ZB - 1 else 0.0, down[q])
        sides.append((at(q, -1, 0) + at(q, 1, 0)) + (at(q, 0, -1) + at(q, 0, 1)) + (below + above))
    return centers, sides


def step_kernel(out_ids, inv_s, pos_s, dens_hbm, weights_hbm, counts, observed, inverse_var,
                ext_out, ids_out, exp_hbm, base_hbm, arr_hbm,
                dens, mid_ids, in_ids, ids_s,
                rows_exp, served, ret, rows, w_ref, obs4, inv4, ext4, wgt4, sens, stage, parcel,
                xlo, xhi, ylo, yhi, field, smooth, base,
                entered, s_id, r_id, s_row, r_row, local, s_halo, r_halo):
    gx, gy = lax.axis_index("gx"), lax.axis_index("gy")
    me = gx * GY + gy
    gxm, gxp = lax.rem(gx + GX - 1, GX), lax.rem(gx + 1, GX)
    gym, gyp = lax.rem(gy + GY - 1, GY), lax.rem(gy + 1, GY)
    column = [lax.rem(gx + d, GX) for d in (1, 15, 4, 12, 3, 13, 5, 11, 7, 9, 2, 14, 6, 10, 8)]
    line = [lax.rem(gy + d, GY) for d in (1, 7, 2, 6, 3, 5, 4)]
    greeted = [(t, gy) for t in column] + [(gx, t) for t in line] + [(a, b) for a in (gxm, gxp) for b in (gym, gyp)]
    barrier = pltpu.get_barrier_semaphore()
    for to in greeted:
        pl.semaphore_signal(barrier, inc=1, device_id=to, device_id_type=MESH)

    loads = []
    for q in range(ZB):
        part = dens_hbm.at[:, :, pl.ds(q * WIDTH, WIDTH)]
        loads.append(pltpu.make_async_copy(part, field.at[q, pl.ds(2, CX), pl.ds(8, CY)], local.at[q]))
    w_load = pltpu.make_async_copy(weights_hbm, w_ref, local.at[4])
    for load in loads:
        load.start()
    w_load.start()

    pl.semaphore_wait(barrier, len(greeted))
    for t in line:
        pl.semaphore_signal(entered, inc=1, device_id=(gx, t), device_id_type=MESH)
    own = pltpu.make_async_copy(out_ids.at[gx], mid_ids.at[gx], local.at[7])
    own.start()
    for t in column:
        remote(out_ids.at[t], mid_ids.at[gx], s_id.at[0], r_id.at[0], (t, gy)).start()

    for load in loads:
        load.wait()
    halos = [
        (field.at[:, pl.ds(CX, 2), pl.ds(8, CY)], xlo, (gxp, gy)),
        (field.at[:, pl.ds(2, 2), pl.ds(8, CY)], xhi, (gxm, gy)),
        (field.at[:, pl.ds(2, CX), pl.ds(CY, 8)], ylo.at[:, pl.ds(1, CX)], (gx, gyp)),
        (field.at[:, pl.ds(2, CX), pl.ds(8, 8)], yhi.at[:, pl.ds(1, CX)], (gx, gym)),
        (field.at[:, CX + 1, pl.ds(CY, 8)], ylo.at[:, 0], (gxp, gyp)),
        (field.at[:, 2, pl.ds(CY, 8)], ylo.at[:, CX + 1], (gxm, gyp)),
        (field.at[:, CX + 1, pl.ds(8, 8)], yhi.at[:, 0], (gxp, gym)),
        (field.at[:, 2, pl.ds(8, 8)], yhi.at[:, CX + 1], (gxm, gym)),
    ]
    halos = [remote(src, dst, s_halo.at[n], r_halo.at[n], to) for n, (src, dst, to) in enumerate(halos)]

    def gather_source(x, _):
        for q in range(ZB):
            dens[pl.ds(pl.multiple_of(q * CX * CY + x * CY, CY), CY), :] = field[q, x + 2, pl.ds(8, CY), :]
        return 0

    lax.fori_loop(0, CX, gather_source, 0)
    dens[pl.ds(ROWS, 8), :] = jnp.zeros((8, WIDTH), f32)
    own.wait()
    drain(mid_ids.at[pl.ds(0, GX - 1)], r_id.at[0])
    pl.semaphore_wait(entered, len(line))
    own = pltpu.make_async_copy(mid_ids.at[:, gy], in_ids.at[:, gy], local.at[7])
    own.start()
    for t in line:
        remote(mid_ids.at[:, t], in_ids.at[:, gy], s_id.at[1], r_id.at[1], (gx, t)).start()
    for copy in halos:
        copy.start()

    for ref, four in ((observed, obs4), (inverse_var, inv4)):
        wide = jnp.concatenate([ref[...], ref[...]], axis=1)
        four[...] = jnp.concatenate([wide] * 4, axis=0).T
    sens[pl.ds(REQ, 8), :] = jnp.zeros((8, WIDTH), f32)
    own.wait()
    drain(in_ids.at[:, pl.ds(0, GY - 1)], r_id.at[1])
    ids_copy = pltpu.make_async_copy(in_ids, ids_s, local.at[7])
    ids_copy.start()
    ids_copy.wait()

    def serve(tx, ty, at):
        for c in range(CAP):
            rows_exp[at, c, :] = dens[ids_s[tx, ty, 0, c], :]
        values = jnp.exp(rows_exp[at])
        rows_exp[at] = step_rate * values
        served[at] = values.astype(bf16)

    def send_rows(j, _):
        tx, ty = peer(gx, gy, j)
        at = tx * GY + ty
        serve(tx, ty, at)
        remote(served.at[at], ret.at[me], s_row.at[0], r_row.at[0], (tx, ty)).start()
        return 0

    lax.fori_loop(1, NDEV, send_rows, 0)
    serve(gx, gy, me)
    keep = pltpu.make_async_copy(served.at[me], ret.at[me], local.at[0])
    keep.start()
    ids_out[...] = in_ids[...]
    exp_store = pltpu.make_async_copy(rows_exp, exp_hbm, local.at[1])
    exp_store.start()

    for copy in halos:
        copy.wait()
    low_x, high_x, low_y, high_y = gx > 0, gx < GX - 1, gy > 0, gy < GY - 1
    blank = jnp.zeros((8, WIDTH), f32)
    for q in range(ZB):
        for n in range(2):
            field[q, n, pl.ds(8, CY), :] = jnp.where(low_x, xlo[q, n], 0.0)
            field[q, CX + 2 + n, pl.ds(8, CY), :] = jnp.where(high_x, xhi[q, n], 0.0)

        def edge(x, _):
            field[q, x + 1, pl.ds(0, 8), :] = jnp.where(low_y, ylo[q, x], 0.0)
            field[q, x + 1, pl.ds(8 + CY, 8), :] = jnp.where(high_y, yhi[q, x], 0.0)
            return 0

        lax.fori_loop(1, CX + 1, edge, 0)
        for x, inside in ((0, low_x), (CX + 1, high_x)):
            field[q, x + 1, pl.ds(0, 8), :] = jnp.where(low_y & inside, ylo[q, x], 0.0)
            field[q, x + 1, pl.ds(8 + CY, 8), :] = jnp.where(high_y & inside, yhi[q, x], 0.0)
    sub = lax.broadcasted_iota(i32, (8, WIDTH), 0)
    top_keep = (sub > 0) | low_y
    bottom_keep = (sub != 1) | high_y

    def smooth_plane(x, inside=None):
        for n in range(9):
            centers, sides = shifted_sum(field, x + 1, 7 + 8 * n)
            for q in range(ZB):
                value = center_weight * centers[q] - sides[q]
                if n == 0:
                    value = jnp.where(top_keep, value, 0.0)
                if n == 8:
                    value = jnp.where(bottom_keep, value, 0.0)
                if inside is not None:
                    value = jnp.where(inside, value, 0.0)
                smooth[q, x, pl.ds(8 * n, 8), :] = value

    def base_plane(x):
        for n in range(8):
            centers, sides = shifted_sum(smooth, x + 1, 8 * n + 1)
            for q in range(ZB):
                prior = center_weight * centers[q] - sides[q]
                now = field[q, x + 2, pl.ds(8 + 8 * n, 8), :]
                base[q, x, pl.ds(8 * n, 8), :] = now - (step_rate * prior_weight) * prior

    smooth_plane(0, low_x)
    smooth_plane(1)
    smooth_plane(2)
    w_load.wait()
    keep.wait()
    drain(ret.at[pl.ds(0, NDEV - 1)], r_row.at[0])

    def widen(n, _):
        for u in range(UNROLL):
            rows[pl.ds(pl.multiple_of((n * UNROLL + u) * CAP, CAP), CAP), :] = ret[n * UNROLL + u].astype(f32)
        return 0

    lax.fori_loop(0, NDEV // UNROLL, widen, 0)
    deep = 8 * STARS
    mine = (lax.broadcasted_iota(i32, (8, deep), 1) >> 5) == lax.broadcasted_iota(i32, (8, deep), 0)
    lane = lax.broadcasted_iota(i32, (STARS, WIDTH), 1)
    diagonal = (lane & (STARS - 1)) == lax.broadcasted_iota(i32, (STARS, WIDTH), 0)
    star = lax.broadcasted_iota(i32, (1, WIDTH), 1) & (STARS - 1)

    def extinct(i):
        for u in range(UNROLL):
            b = i * UNROLL + u
            totals = [jnp.zeros((STARS, WIDTH), f32) for _ in range(2)]
            for k in range(SLOTS):
                line_k = rows[pl.ds(pos_s[0, k * BLOCKS + b], 1), :]
                totals[k % 2] = totals[k % 2] + w_ref[b, k].astype(f32) * line_k
            total = jnp.sum(totals[0] + totals[1], axis=1, keepdims=True)
            ext = jnp.sum(jnp.where(diagonal, total, 0.0), axis=0, keepdims=True)
            ext4[pl.ds(b, 1), :] = ext
            residual = inv4[pl.ds(b, 1), :] * (ext - obs4[pl.ds(b, 1), :])
            wgt4[pl.ds(b, 1), :] = jnp.where(star < counts[b], residual, 0.0)

    def sensitive(i):
        for u in range(UNROLL):
            b = i * UNROLL + u
            line_b = wgt4[pl.ds(b, 1), :]
            left = jnp.where(mine, jnp.concatenate([line_b, line_b], axis=1), 0.0).astype(bf16)
            for n in range(SLOTS // 8):
                sens[pl.ds(pl.multiple_of(b * SLOTS + n * 8, 8), 8), :] = jnp.dot(
                    left, w_ref[b, pl.ds(n * 8, 8)].reshape(deep, WIDTH), preferred_element_type=f32
                )

    extinct(0)

    def both(i, _):
        sensitive(i - 1)
        extinct(i)
        return 0

    lax.fori_loop(1, BLOCKS // UNROLL, both, 0)
    sensitive(BLOCKS // UNROLL - 1)

    slot_a, slot_b = lax.broadcasted_iota(i32, (CAP, CAP), 0), lax.broadcasted_iota(i32, (CAP, CAP), 1)
    eye, together = slot_a == slot_b, (slot_a >> 3) == (slot_b >> 3)

    def pack(tx, ty, at):
        for c in range(CAP):
            stage[at, c, :] = sens[inv_s[at, c], :]
        across = jnp.broadcast_to(out_ids[tx, ty].astype(f32), (CAP, CAP))
        down = jnp.sum(jnp.where(eye, across, 0.0), axis=1, keepdims=True)
        same = jnp.where((down == across) & together, 1.0, 0.0).astype(bf16)
        parcel[at] = jnp.dot(same, stage[at].astype(bf16), preferred_element_type=f32).astype(bf16)

    def partners(it):
        return [peer(gx, gy, it * UNROLL + u + 1) for u in range(UNROLL)]

    def pack_all(it):
        for tx, ty in partners(it):
            pack(tx, ty, tx * GY + ty)

    def send_back(it, count):
        for tx, ty in partners(it)[:count]:
            remote(parcel.at[tx * GY + ty], arr_hbm.at[me], s_row.at[1], r_row.at[1], (tx, ty)).start()

    def give_back(it, _):
        pack_all(it)
        smooth_plane(it + 3, (it < CX - 2) | high_x)
        base_plane(it)
        send_back(it, UNROLL)
        return 0

    lax.fori_loop(0, CX - 1, give_back, 0)
    pack_all(CX - 1)
    send_back(CX - 1, UNROLL - 1)
    base_plane(CX - 1)
    keep = pltpu.make_async_copy(parcel.at[me], arr_hbm.at[me], local.at[0])
    keep.start()
    base_store = pltpu.make_async_copy(base, base_hbm, local.at[2])
    base_store.start()
    ext_out[...] = jnp.concatenate([ext4[...], ext4[...]], axis=0).T[:STARS, :BLOCKS]
    keep.wait()
    exp_store.wait()
    base_store.wait()
    drain(out_ids.at[pl.ds(0, GX - 1)], s_id.at[0])
    drain(mid_ids.at[:, pl.ds(0, GY - 1)], s_id.at[1])
    drain(served.at[pl.ds(0, NDEV - 1)], s_row.at[0])
    drain(parcel.at[pl.ds(0, NDEV - 1)], s_row.at[1])
    drain(arr_hbm.at[pl.ds(0, NDEV - 1)], r_row.at[1])


def step(ids, inv, pos, dens, weights, counts, observed, inverse_var):
    shape = jax.ShapeDtypeStruct
    v = pltpu.VMEM
    return pl.pallas_call(
        step_kernel,
        out_shape=(
            shape((STARS, BLOCKS), f32),
            shape((GX, GY, 1, CAP), i32),
            shape((NDEV, CAP, WIDTH), f32),
            shape((ZB, CX, CY, WIDTH), f32),
            shape((NDEV, CAP, WIDTH), bf16),
        ),
        in_specs=[
            whole(v), whole(pltpu.SMEM), whole(pltpu.SMEM),
            whole(pltpu.HBM), whole(pltpu.HBM), whole(pltpu.SMEM), whole(v), whole(v),
        ],
        out_specs=[whole(v), whole(v), whole(pltpu.HBM), whole(pltpu.HBM), whole(pltpu.HBM)],
        scratch_shapes=[
            v((ROWS + 8, WIDTH), f32),
            v((GX, GY, 1, CAP), i32), v((GX, GY, 1, CAP), i32), pltpu.SMEM((GX, GY, 1, CAP), i32),
            v((NDEV, CAP, WIDTH), f32), v((NDEV, CAP, WIDTH), bf16), v((NDEV, CAP, WIDTH), bf16),
            v((NDEV * CAP, WIDTH), f32), v((BLOCKS, SLOTS, STARS, WIDTH), bf16),
            v((WIDTH, WIDTH), f32), v((WIDTH, WIDTH), f32), v((BLOCKS, WIDTH), f32), v((BLOCKS, WIDTH), f32),
            v((REQ + 8, WIDTH), f32), v((NDEV, CAP, WIDTH), f32), v((NDEV, CAP, WIDTH), bf16),
            v((ZB, 2, CY, WIDTH), f32), v((ZB, 2, CY, WIDTH), f32),
            v((ZB, CX + 2, 8, WIDTH), f32), v((ZB, CX + 2, 8, WIDTH), f32),
            v((ZB, CX + 4, CY + 16, WIDTH), f32), v((ZB, CX + 2, CY + 8, WIDTH), f32), v((ZB, CX, CY, WIDTH), f32),
            pltpu.SemaphoreType.REGULAR, DMA((2,)), DMA((2,)), DMA((2,)), DMA((2,)), DMA((8,)), DMA((8,)), DMA((8,)),
        ],
        name="step",
        compiler_params=pltpu.CompilerParams(collective_id=0, has_side_effects=True, vmem_limit_bytes=60 << 20),
    )(ids, inv, pos, dens, weights, counts, observed, inverse_var)


def update_kernel(ids, ext_in, exp_hbm, base_hbm, arr_hbm, ext_out, out_hbm, new, rows_exp, arrived, add, sem):
    load_exp = pltpu.make_async_copy(exp_hbm, rows_exp, sem.at[0])
    load_arr = pltpu.make_async_copy(arr_hbm, arrived, sem.at[1])
    load_exp.start()
    load_arr.start()
    bases = []
    for q in range(ZB):
        bases.append(pltpu.make_async_copy(base_hbm.at[q], new.at[pl.ds(q * CX * CY, CX * CY)], sem.at[2 + q]))
        bases[q].start()
    ext_out[...] = ext_in[...]
    new[pl.ds(ROWS, 8), :] = jnp.zeros((8, WIDTH), f32)
    load_exp.wait()
    load_arr.wait()

    def scale(n, _):
        for u in range(UNROLL):
            t = n * UNROLL + u
            add[t] = rows_exp[t] * arrived[t].astype(f32)
        return 0

    lax.fori_loop(0, NDEV // UNROLL, scale, 0)
    for load in bases:
        load.wait()

    def source(t, _):
        tx, ty = t // GY, lax.rem(t, GY)

        def eight(first):
            at = [ids[tx, ty, 0, first + c] for c in range(8)]
            values = [new[pl.ds(n, 1), :] - add[t, pl.ds(first + c, 1), :] for c, n in enumerate(at)]
            for n, value in zip(at, values):
                new[pl.ds(n, 1), :] = value

        eight(0)
        eight(8)

        @pl.when(ids[tx, ty, 0, 16] < ROWS)
        def _():
            eight(16)

            @pl.when(ids[tx, ty, 0, 24] < ROWS)
            def _():
                eight(24)

        return 0

    lax.fori_loop(0, NDEV, source, 0)
    stores = []
    for q in range(ZB):
        rows_of = new.at[pl.ds(q * CX * CY, CX * CY)]
        stores.append(pltpu.make_async_copy(
            rows_of.reshape(CX, CY, WIDTH), out_hbm.at[:, :, pl.ds(q * WIDTH, WIDTH)], sem.at[2 + q]
        ))
        stores[q].start()
    for store in stores:
        store.wait()


def update(ids, ext, rows_exp, base, arrived):
    v = pltpu.VMEM
    return pl.pallas_call(
        update_kernel,
        out_shape=(jax.ShapeDtypeStruct((STARS, BLOCKS), f32), jax.ShapeDtypeStruct((CX, CY, ZB * WIDTH), f32)),
        in_specs=[whole(pltpu.SMEM), whole(v), whole(pltpu.HBM), whole(pltpu.HBM), whole(pltpu.HBM)],
        out_specs=[whole(v), whole(pltpu.HBM)],
        scratch_shapes=[
            v((ROWS + 8, WIDTH), f32), v((NDEV, CAP, WIDTH), f32), v((NDEV, CAP, WIDTH), bf16), v((NDEV, CAP, WIDTH), f32),
            DMA((6,)),
        ],
        name="update",
        compiler_params=pltpu.CompilerParams(vmem_limit_bytes=62 << 20),
    )(ids, ext, rows_exp, base.reshape(ZB, CX * CY, WIDTH), arrived)


def on_device(log_density, weights, observed, inverse_var, star_counts, block_ids):
    ids, inv, pos = bucket(block_ids.T)
    ext, ids, rows_exp, base, arrived = step(
        ids, inv, pos, log_density, weights, star_counts, observed.T, inverse_var.T
    )
    ext, new = update(ids, ext, rows_exp, base, arrived)
    return (new, ext.T)


def solution(mesh):
    placed = (
        P("gx", "gy", None),
        P(("gx", "gy"), None, None, None),
        P(("gx", "gy"), None),
        P(("gx", "gy"), None),
        P(("gx", "gy")),
        P(("gx", "gy"), None),
    )
    return jax.shard_map(
        on_device,
        mesh=mesh,
        in_specs=placed,
        out_specs=(P("gx", "gy", None), P(("gx", "gy"), None)),
        check_vma=False,
    )
```

```python
import jax
import jax.numpy as jnp
from jax import lax
from jax.experimental import pallas as pl
from jax.experimental.pallas import tpu as pltpu
from jax.sharding import PartitionSpec as P

MESH = pl.DeviceIdType.MESH
DMA = pltpu.SemaphoreType.DMA
shift_kappa = 0.5
prior_weight = 0.05
step_rate = 2.0
f32, bf16, i32 = jnp.float32, jnp.bfloat16, jnp.int32

GX, GY = 16, 8
NDEV, CAP, WIDTH = 128, 32, 128
BLOCKS, SLOTS, STARS = 64, 32, 32
REQ = BLOCKS * SLOTS
CX, CY, ZB = 32, 64, 4
ROWS = CX * CY * ZB
LOCAL_BITS = 13
UNROLL = 4
center_weight = shift_kappa + 6.0


def whole(space):
    return pl.BlockSpec(memory_space=space)


def remote(src, dst, send, recv, to):
    return pltpu.make_async_remote_copy(
        src_ref=src, dst_ref=dst, send_sem=send, recv_sem=recv, device_id=to, device_id_type=MESH
    )


def drain(ref, sem):
    pltpu.make_async_copy(ref, ref, sem).wait()


def send_order():
    dist = lambda o: sum(min(v, 4 - v) for v in o[:3])
    rest = [(a, b, c, d) for a in range(4) for b in range(4) for c in range(4) for d in range(2)][1:]
    rest = [rest[j * 37 % len(rest)] for j in range(len(rest))]
    load, order = [0] * 6, []

    def loaded(o):
        now = list(load)
        for axis in range(3):
            now[2 * axis] += o[axis] in (1, 2)
            now[2 * axis + 1] += o[axis] in (3, 2)
        return now

    while rest:
        far = max(map(dist, rest))
        spread = lambda o: (max(loaded(o)) - min(loaded(o)), sum(v * v for v in loaded(o)))
        best = min((o for o in rest if dist(o) == far), key=spread)
        load = loaded(best)
        rest.remove(best)
        order.append(best)
    return [((a * 4 + b) * 4 + c) * 2 + d for a, b, c, d in order] + [0]


def packed_order():
    order = send_order()
    return [sum(order[n + u] * NDEV ** u for u in range(UNROLL)) for n in range(0, NDEV, UNROLL)]


def pick(words, at, first=0):
    if len(words) == 1:
        return jnp.int32(words[0])
    half = len(words) // 2
    return jnp.where(at < first + half, pick(words[:half], at, first), pick(words[half:], at, first + half))


def partners(gx, gy, trip):
    word, found = pick(packed_order(), trip), []
    for u in range(UNROLL):
        o = lax.rem(word // NDEV ** u, NDEV)
        x = lax.rem(gx // 4 + o // 32, 4)
        y = lax.rem(gx + lax.rem(o // 8, 4), 4)
        z = lax.rem(gy // 2 + lax.rem(o // 2, 4), 4)
        found.append((x * 4 + y, z * 2 + lax.rem(gy + o, 2)))
    return found


def bucket(blocks, out_ids, inv_ref, pos_ref, at_ref, bt_ref):
    ids = jnp.concatenate([blocks[k:k + 1, :] for k in range(SLOTS)], axis=1)
    target = ids >> LOCAL_BITS
    within = ids & (ROWS - 1)
    within = (within & (ZB - 1)) * (CX * CY) + (within >> 2)
    order = lax.broadcasted_iota(i32, (1, REQ), 1)
    order = (order & (BLOCKS - 1)) * SLOTS + (order >> 6)
    at_ref[...] = jnp.where(lax.broadcasted_iota(i32, (NDEV, REQ), 0) == target, 1.0, 0.0).astype(bf16)
    step = 256
    before = lax.broadcasted_iota(i32, (step, step), 0) < lax.broadcasted_iota(i32, (step, step), 1)
    before = jnp.where(before, 1.0, 0.0).astype(bf16)
    running = jnp.zeros((NDEV, 1), f32)
    slot = lax.broadcasted_iota(i32, (CAP, step), 0)
    for k in range(REQ // step):
        cut = slice(k * step, (k + 1) * step)
        part = at_ref[:, cut]
        prefix = jnp.dot(part, before, preferred_element_type=f32) + running
        wide = part.astype(f32)
        rank = jnp.clip(jnp.sum(wide * prefix, axis=0, keepdims=True).astype(i32), 0, CAP - 1)
        running = running + jnp.sum(wide, axis=1, keepdims=True)
        hit = slot == rank
        pos_ref[:, cut] = target[:, cut] * CAP + rank
        for n, value in enumerate((within[:, cut] >> 7, within[:, cut] & 127, order[:, cut] >> 7, order[:, cut] & 127, None)):
            value = 1.0 if value is None else value.astype(f32)
            bt_ref[n * CAP:(n + 1) * CAP, cut] = jnp.where(hit, value, 0.0).astype(bf16)
    table = lax.dot_general(at_ref[...], bt_ref[...], (((1,), (1,)), ((), ())), preferred_element_type=f32)
    parts = [table[:, n * CAP:(n + 1) * CAP] for n in range(5)]
    present = parts[4] > 0.5
    row = jnp.where(present, parts[0] * 128.0 + parts[1], float(ROWS)).astype(i32)
    out_ids[...] = jnp.clip(row, 0, ROWS).reshape(GX, GY, 1, CAP)
    source = jnp.where(present, parts[2] * 128.0 + parts[3], float(REQ)).astype(i32)
    inv_ref[...] = jnp.clip(source, 0, REQ)


def shifted_sum(field, x, row):
    lane = lax.broadcasted_iota(i32, (8, WIDTH), 1)
    first, final = lane == 0, lane == WIDTH - 1
    at = lambda q, dx, dr: field[q, x + dx, pl.ds(row + dr, 8), :]
    centers = [at(q, 0, 0) for q in range(ZB)]
    up = [pltpu.roll(c, 1, 1) for c in centers]
    down = [pltpu.roll(c, WIDTH - 1, 1) for c in centers]
    sides = []
    for q in range(ZB):
        below = jnp.where(first, up[q - 1] if q > 0 else 0.0, up[q])
        above = jnp.where(final, down[q + 1] if q < ZB - 1 else 0.0, down[q])
        sides.append((at(q, -1, 0) + at(q, 1, 0)) + (at(q, 0, -1) + at(q, 0, 1)) + (below + above))
    return centers, sides


def step_kernel(blocks, dens_hbm, weights_hbm, counts, observed, inverse_var,
                ext_out, ids_out, exp_hbm, base_hbm, arr_hbm,
                dens, out_ids, mid_ids, in_ids, ids_s, inv_v, inv_s, pos_v, pos_s, at_ref, bt_ref,
                rows_exp, served, ret, rows, w_ref, obs4, inv4, ext4, wgt4, sens, stage, parcel,
                xlo, xhi, ylo, yhi, field, smooth, base,
                entered, s_id, r_id, s_row, r_row, local, s_halo, r_halo):
    gx, gy = lax.axis_index("gx"), lax.axis_index("gy")
    me = gx * GY + gy
    gxm, gxp = lax.rem(gx + GX - 1, GX), lax.rem(gx + 1, GX)
    gym, gyp = lax.rem(gy + GY - 1, GY), lax.rem(gy + 1, GY)
    column = [lax.rem(gx + d, GX) for d in (1, 15, 4, 12, 3, 13, 5, 11, 7, 9, 2, 14, 6, 10, 8)]
    line = [lax.rem(gy + d, GY) for d in (1, 7, 2, 6, 3, 5, 4)]
    greeted = [(t, gy) for t in column] + [(gx, t) for t in line] + [(a, b) for a in (gxm, gxp) for b in (gym, gyp)]
    barrier = pltpu.get_barrier_semaphore()
    for to in greeted:
        pl.semaphore_signal(barrier, inc=1, device_id=to, device_id_type=MESH)

    loads = []
    for q in range(ZB):
        part = dens_hbm.at[:, :, pl.ds(q * WIDTH, WIDTH)]
        loads.append(pltpu.make_async_copy(part, field.at[q, pl.ds(2, CX), pl.ds(8, CY)], local.at[q]))
    w_load = pltpu.make_async_copy(weights_hbm, w_ref, local.at[4])
    for load in loads:
        load.start()
    w_load.start()

    bucket(blocks, out_ids, inv_v, pos_v, at_ref, bt_ref)
    to_smem = [pltpu.make_async_copy(inv_v, inv_s, local.at[5]), pltpu.make_async_copy(pos_v, pos_s, local.at[6])]
    for copy in to_smem:
        copy.start()

    pl.semaphore_wait(barrier, len(greeted))
    for t in line:
        pl.semaphore_signal(entered, inc=1, device_id=(gx, t), device_id_type=MESH)
    own = pltpu.make_async_copy(out_ids.at[gx], mid_ids.at[gx], local.at[7])
    own.start()
    for t in column:
        remote(out_ids.at[t], mid_ids.at[gx], s_id.at[0], r_id.at[0], (t, gy)).start()

    for load in loads:
        load.wait()
    halos = [
        (field.at[:, pl.ds(CX, 2), pl.ds(8, CY)], xlo, (gxp, gy)),
        (field.at[:, pl.ds(2, 2), pl.ds(8, CY)], xhi, (gxm, gy)),
        (field.at[:, pl.ds(2, CX), pl.ds(CY, 8)], ylo.at[:, pl.ds(1, CX)], (gx, gyp)),
        (field.at[:, pl.ds(2, CX), pl.ds(8, 8)], yhi.at[:, pl.ds(1, CX)], (gx, gym)),
        (field.at[:, CX + 1, pl.ds(CY, 8)], ylo.at[:, 0], (gxp, gyp)),
        (field.at[:, 2, pl.ds(CY, 8)], ylo.at[:, CX + 1], (gxm, gyp)),
        (field.at[:, CX + 1, pl.ds(8, 8)], yhi.at[:, 0], (gxp, gym)),
        (field.at[:, 2, pl.ds(8, 8)], yhi.at[:, CX + 1], (gxm, gym)),
    ]
    halos = [remote(src, dst, s_halo.at[n], r_halo.at[n], to) for n, (src, dst, to) in enumerate(halos)]

    def gather_source(x, _):
        for q in range(ZB):
            dens[pl.ds(pl.multiple_of(q * CX * CY + x * CY, CY), CY), :] = field[q, x + 2, pl.ds(8, CY), :]
        return 0

    lax.fori_loop(0, CX, gather_source, 0)
    dens[pl.ds(ROWS, 8), :] = jnp.zeros((8, WIDTH), f32)
    own.wait()
    drain(mid_ids.at[pl.ds(0, GX - 1)], r_id.at[0])
    pl.semaphore_wait(entered, len(line))
    own = pltpu.make_async_copy(mid_ids.at[:, gy], in_ids.at[:, gy], local.at[7])
    own.start()
    for t in line:
        remote(mid_ids.at[:, t], in_ids.at[:, gy], s_id.at[1], r_id.at[1], (gx, t)).start()
    for copy in halos:
        copy.start()

    for ref, four in ((observed, obs4), (inverse_var, inv4)):
        wide = jnp.concatenate([ref[...], ref[...]], axis=1)
        four[...] = jnp.concatenate([wide] * 4, axis=0).T
    sens[pl.ds(REQ, 8), :] = jnp.zeros((8, WIDTH), f32)
    own.wait()
    drain(in_ids.at[:, pl.ds(0, GY - 1)], r_id.at[1])
    ids_copy = pltpu.make_async_copy(in_ids, ids_s, local.at[7])
    ids_copy.start()
    ids_copy.wait()

    def serve(tx, ty, at):
        for c in range(CAP):
            rows_exp[at, c, :] = dens[ids_s[tx, ty, 0, c], :]
        values = jnp.exp(rows_exp[at])
        rows_exp[at] = step_rate * values
        served[at] = values.astype(bf16)

    def send_rows(trip, count):
        for u, (tx, ty) in enumerate(partners(gx, gy, trip)):
            at = tx * GY + ty
            serve(tx, ty, at)
            if u < count:
                remote(served.at[at], ret.at[me], s_row.at[0], r_row.at[0], (tx, ty)).start()
        return 0

    trips = NDEV // UNROLL
    lax.fori_loop(0, trips - 1, lambda trip, _: send_rows(trip, UNROLL), 0)
    send_rows(trips - 1, UNROLL - 1)
    keep = pltpu.make_async_copy(served.at[me], ret.at[me], local.at[0])
    keep.start()
    ids_out[...] = in_ids[...]
    exp_store = pltpu.make_async_copy(rows_exp, exp_hbm, local.at[1])
    exp_store.start()

    for copy in halos:
        copy.wait()
    low_x, high_x, low_y, high_y = gx > 0, gx < GX - 1, gy > 0, gy < GY - 1
    blank = jnp.zeros((8, WIDTH), f32)
    for q in range(ZB):
        for n in range(2):
            field[q, n, pl.ds(8, CY), :] = jnp.where(low_x, xlo[q, n], 0.0)
            field[q, CX + 2 + n, pl.ds(8, CY), :] = jnp.where(high_x, xhi[q, n], 0.0)

        def edge(x, _):
            field[q, x + 1, pl.ds(0, 8), :] = jnp.where(low_y, ylo[q, x], 0.0)
            field[q, x + 1, pl.ds(8 + CY, 8), :] = jnp.where(high_y, yhi[q, x], 0.0)
            return 0

        lax.fori_loop(1, CX + 1, edge, 0)
        for x, inside in ((0, low_x), (CX + 1, high_x)):
            field[q, x + 1, pl.ds(0, 8), :] = jnp.where(low_y & inside, ylo[q, x], 0.0)
            field[q, x + 1, pl.ds(8 + CY, 8), :] = jnp.where(high_y & inside, yhi[q, x], 0.0)
    sub = lax.broadcasted_iota(i32, (8, WIDTH), 0)
    top_keep = (sub > 0) | low_y
    bottom_keep = (sub != 1) | high_y

    def smooth_plane(x, inside=None):
        for n in range(9):
            centers, sides = shifted_sum(field, x + 1, 7 + 8 * n)
            for q in range(ZB):
                value = center_weight * centers[q] - sides[q]
                if n == 0:
                    value = jnp.where(top_keep, value, 0.0)
                if n == 8:
                    value = jnp.where(bottom_keep, value, 0.0)
                if inside is not None:
                    value = jnp.where(inside, value, 0.0)
                smooth[q, x, pl.ds(8 * n, 8), :] = value

    def base_plane(x):
        for n in range(8):
            centers, sides = shifted_sum(smooth, x + 1, 8 * n + 1)
            for q in range(ZB):
                prior = center_weight * centers[q] - sides[q]
                now = field[q, x + 2, pl.ds(8 + 8 * n, 8), :]
                base[q, x, pl.ds(8 * n, 8), :] = now - (step_rate * prior_weight) * prior

    smooth_plane(0, low_x)
    smooth_plane(1)
    smooth_plane(2)
    w_load.wait()
    for copy in to_smem:
        copy.wait()
    keep.wait()
    drain(ret.at[pl.ds(0, NDEV - 1)], r_row.at[0])

    def widen(n, _):
        for u in range(UNROLL):
            rows[pl.ds(pl.multiple_of((n * UNROLL + u) * CAP, CAP), CAP), :] = ret[n * UNROLL + u].astype(f32)
        return 0

    lax.fori_loop(0, NDEV // UNROLL, widen, 0)
    deep = 8 * STARS
    mine = (lax.broadcasted_iota(i32, (8, deep), 1) >> 5) == lax.broadcasted_iota(i32, (8, deep), 0)
    lane = lax.broadcasted_iota(i32, (STARS, WIDTH), 1)
    diagonal = (lane & (STARS - 1)) == lax.broadcasted_iota(i32, (STARS, WIDTH), 0)
    star = lax.broadcasted_iota(i32, (1, WIDTH), 1) & (STARS - 1)

    def extinct(i):
        for u in range(UNROLL):
            b = i * UNROLL + u
            totals = [jnp.zeros((STARS, WIDTH), f32) for _ in range(2)]
            for k in range(SLOTS):
                line_k = rows[pl.ds(pos_s[0, k * BLOCKS + b], 1), :]
                totals[k % 2] = totals[k % 2] + w_ref[b, k].astype(f32) * line_k
            total = jnp.sum(totals[0] + totals[1], axis=1, keepdims=True)
            ext = jnp.sum(jnp.where(diagonal, total, 0.0), axis=0, keepdims=True)
            ext4[pl.ds(b, 1), :] = ext
            residual = inv4[pl.ds(b, 1), :] * (ext - obs4[pl.ds(b, 1), :])
            wgt4[pl.ds(b, 1), :] = jnp.where(star < counts[b], residual, 0.0)

    def sensitive(i):
        for u in range(UNROLL):
            b = i * UNROLL + u
            line_b = wgt4[pl.ds(b, 1), :]
            left = jnp.where(mine, jnp.concatenate([line_b, line_b], axis=1), 0.0).astype(bf16)
            for n in range(SLOTS // 8):
                sens[pl.ds(pl.multiple_of(b * SLOTS + n * 8, 8), 8), :] = jnp.dot(
                    left, w_ref[b, pl.ds(n * 8, 8)].reshape(deep, WIDTH), preferred_element_type=f32
                )

    extinct(0)

    def both(i, _):
        sensitive(i - 1)
        extinct(i)
        return 0

    lax.fori_loop(1, BLOCKS // UNROLL, both, 0)
    sensitive(BLOCKS // UNROLL - 1)

    slot_a, slot_b = lax.broadcasted_iota(i32, (CAP, CAP), 0), lax.broadcasted_iota(i32, (CAP, CAP), 1)
    eye, together = slot_a == slot_b, (slot_a >> 3) == (slot_b >> 3)

    def pack(tx, ty, at):
        for c in range(CAP):
            stage[at, c, :] = sens[inv_s[at, c], :]
        across = jnp.broadcast_to(out_ids[tx, ty].astype(f32), (CAP, CAP))
        down = jnp.sum(jnp.where(eye, across, 0.0), axis=1, keepdims=True)
        same = jnp.where((down == across) & together, 1.0, 0.0).astype(bf16)
        parcel[at] = jnp.dot(same, stage[at].astype(bf16), preferred_element_type=f32).astype(bf16)

    def pack_all(to):
        for tx, ty in to:
            pack(tx, ty, tx * GY + ty)

    def send_back(to):
        for tx, ty in to:
            remote(parcel.at[tx * GY + ty], arr_hbm.at[me], s_row.at[1], r_row.at[1], (tx, ty)).start()

    def give_back(it, _):
        to = partners(gx, gy, it)
        pack_all(to)
        smooth_plane(it + 3, (it < CX - 2) | high_x)
        base_plane(it)
        send_back(to)
        return 0

    lax.fori_loop(0, CX - 1, give_back, 0)
    to = partners(gx, gy, trips - 1)
    pack_all(to)
    send_back(to[:UNROLL - 1])
    base_plane(CX - 1)
    keep = pltpu.make_async_copy(parcel.at[me], arr_hbm.at[me], local.at[0])
    keep.start()
    base_store = pltpu.make_async_copy(base, base_hbm, local.at[2])
    base_store.start()
    ext_out[...] = jnp.concatenate([ext4[...], ext4[...]], axis=0).T[:STARS, :BLOCKS]
    keep.wait()
    exp_store.wait()
    base_store.wait()
    drain(out_ids.at[pl.ds(0, GX - 1)], s_id.at[0])
    drain(mid_ids.at[:, pl.ds(0, GY - 1)], s_id.at[1])
    drain(served.at[pl.ds(0, NDEV - 1)], s_row.at[0])
    drain(parcel.at[pl.ds(0, NDEV - 1)], s_row.at[1])
    drain(arr_hbm.at[pl.ds(0, NDEV - 1)], r_row.at[1])


def step(blocks, dens, weights, counts, observed, inverse_var):
    shape = jax.ShapeDtypeStruct
    v = pltpu.VMEM
    return pl.pallas_call(
        step_kernel,
        out_shape=(
            shape((STARS, BLOCKS), f32),
            shape((GX, GY, 1, CAP), i32),
            shape((NDEV, CAP, WIDTH), f32),
            shape((ZB, CX, CY, WIDTH), f32),
            shape((NDEV, CAP, WIDTH), bf16),
        ),
        in_specs=[
            whole(v), whole(pltpu.HBM), whole(pltpu.HBM), whole(pltpu.SMEM), whole(v), whole(v),
        ],
        out_specs=[whole(v), whole(v), whole(pltpu.HBM), whole(pltpu.HBM), whole(pltpu.HBM)],
        scratch_shapes=[
            v((ROWS + 8, WIDTH), f32),
            v((GX, GY, 1, CAP), i32), v((GX, GY, 1, CAP), i32), v((GX, GY, 1, CAP), i32), pltpu.SMEM((GX, GY, 1, CAP), i32),
            v((NDEV, CAP), i32), pltpu.SMEM((NDEV, CAP), i32), v((1, REQ), i32), pltpu.SMEM((1, REQ), i32),
            v((NDEV, REQ), bf16), v((5 * CAP, REQ), bf16),
            v((NDEV, CAP, WIDTH), f32), v((NDEV, CAP, WIDTH), bf16), v((NDEV, CAP, WIDTH), bf16),
            v((NDEV * CAP, WIDTH), f32), v((BLOCKS, SLOTS, STARS, WIDTH), bf16),
            v((WIDTH, WIDTH), f32), v((WIDTH, WIDTH), f32), v((BLOCKS, WIDTH), f32), v((BLOCKS, WIDTH), f32),
            v((REQ + 8, WIDTH), f32), v((NDEV, CAP, WIDTH), f32), v((NDEV, CAP, WIDTH), bf16),
            v((ZB, 2, CY, WIDTH), f32), v((ZB, 2, CY, WIDTH), f32),
            v((ZB, CX + 2, 8, WIDTH), f32), v((ZB, CX + 2, 8, WIDTH), f32),
            v((ZB, CX + 4, CY + 16, WIDTH), f32), v((ZB, CX + 2, CY + 8, WIDTH), f32), v((ZB, CX, CY, WIDTH), f32),
            pltpu.SemaphoreType.REGULAR, DMA((2,)), DMA((2,)), DMA((2,)), DMA((2,)), DMA((8,)), DMA((8,)), DMA((8,)),
        ],
        name="step",
        compiler_params=pltpu.CompilerParams(collective_id=0, has_side_effects=True, vmem_limit_bytes=60 << 20),
    )(blocks, dens, weights, counts, observed, inverse_var)


def update_kernel(ids, ext_in, exp_hbm, base_hbm, arr_hbm, ext_out, out_hbm, new, rows_exp, arrived, add, sem):
    load_exp = pltpu.make_async_copy(exp_hbm, rows_exp, sem.at[0])
    load_arr = pltpu.make_async_copy(arr_hbm, arrived, sem.at[1])
    load_exp.start()
    load_arr.start()
    bases = []
    for q in range(ZB):
        bases.append(pltpu.make_async_copy(base_hbm.at[q], new.at[pl.ds(q * CX * CY, CX * CY)], sem.at[2 + q]))
        bases[q].start()
    ext_out[...] = ext_in[...]
    new[pl.ds(ROWS, 8), :] = jnp.zeros((8, WIDTH), f32)
    load_exp.wait()
    load_arr.wait()

    def scale(n, _):
        for u in range(UNROLL):
            t = n * UNROLL + u
            add[t] = rows_exp[t] * arrived[t].astype(f32)
        return 0

    lax.fori_loop(0, NDEV // UNROLL, scale, 0)
    for load in bases:
        load.wait()

    def source(t, _):
        tx, ty = t // GY, lax.rem(t, GY)

        def eight(first):
            at = [ids[tx, ty, 0, first + c] for c in range(8)]
            values = [new[pl.ds(n, 1), :] - add[t, pl.ds(first + c, 1), :] for c, n in enumerate(at)]
            for n, value in zip(at, values):
                new[pl.ds(n, 1), :] = value

        eight(0)
        eight(8)

        @pl.when(ids[tx, ty, 0, 16] < ROWS)
        def _():
            eight(16)

            @pl.when(ids[tx, ty, 0, 24] < ROWS)
            def _():
                eight(24)

        return 0

    lax.fori_loop(0, NDEV, source, 0)
    stores = []
    for q in range(ZB):
        rows_of = new.at[pl.ds(q * CX * CY, CX * CY)]
        stores.append(pltpu.make_async_copy(
            rows_of.reshape(CX, CY, WIDTH), out_hbm.at[:, :, pl.ds(q * WIDTH, WIDTH)], sem.at[2 + q]
        ))
        stores[q].start()
    for store in stores:
        store.wait()


def update(ids, ext, rows_exp, base, arrived):
    v = pltpu.VMEM
    return pl.pallas_call(
        update_kernel,
        out_shape=(jax.ShapeDtypeStruct((STARS, BLOCKS), f32), jax.ShapeDtypeStruct((CX, CY, ZB * WIDTH), f32)),
        in_specs=[whole(pltpu.SMEM), whole(v), whole(pltpu.HBM), whole(pltpu.HBM), whole(pltpu.HBM)],
        out_specs=[whole(v), whole(pltpu.HBM)],
        scratch_shapes=[
            v((ROWS + 8, WIDTH), f32), v((NDEV, CAP, WIDTH), f32), v((NDEV, CAP, WIDTH), bf16), v((NDEV, CAP, WIDTH), f32),
            DMA((6,)),
        ],
        name="update",
        compiler_params=pltpu.CompilerParams(vmem_limit_bytes=62 << 20),
    )(ids, ext, rows_exp, base.reshape(ZB, CX * CY, WIDTH), arrived)


def on_device(log_density, weights, observed, inverse_var, star_counts, block_ids):
    ext, ids, rows_exp, base, arrived = step(
        block_ids.T, log_density, weights, star_counts, observed.T, inverse_var.T
    )
    ext, new = update(ids, ext, rows_exp, base, arrived)
    return (new, ext.T)


def solution(mesh):
    placed = (
        P("gx", "gy", None),
        P(("gx", "gy"), None, None, None),
        P(("gx", "gy"), None),
        P(("gx", "gy"), None),
        P(("gx", "gy")),
        P(("gx", "gy"), None),
    )
    return jax.shard_map(
        on_device,
        mesh=mesh,
        in_specs=placed,
        out_specs=(P("gx", "gy", None), P(("gx", "gy"), None)),
        check_vma=False,
    )
```

```python
import jax
import jax.numpy as jnp
from jax import lax
from jax.experimental import pallas as pl
from jax.experimental.pallas import tpu as pltpu
from jax.sharding import PartitionSpec as P

MESH = pl.DeviceIdType.MESH
DMA = pltpu.SemaphoreType.DMA
shift_kappa = 0.5
prior_weight = 0.05
step_rate = 2.0
f32, bf16, i32 = jnp.float32, jnp.bfloat16, jnp.int32

GX, GY = 16, 8
NDEV, CAP, WIDTH = 128, 32, 128
BLOCKS, SLOTS, STARS = 64, 32, 32
REQ = BLOCKS * SLOTS
CX, CY, ZB = 32, 64, 4
ROWS = CX * CY * ZB
LOCAL_BITS = 13
UNROLL = 4
center_weight = shift_kappa + 6.0


def whole(space):
    return pl.BlockSpec(memory_space=space)


def remote(src, dst, send, recv, to):
    return pltpu.make_async_remote_copy(
        src_ref=src, dst_ref=dst, send_sem=send, recv_sem=recv, device_id=to, device_id_type=MESH
    )


def drain(ref, sem):
    pltpu.make_async_copy(ref, ref, sem).wait()


def send_order():
    dist = lambda o: sum(min(v, 4 - v) for v in o[:3])
    rest = [(a, b, c, d) for a in range(4) for b in range(4) for c in range(4) for d in range(2)][1:]
    rest = [rest[j * 37 % len(rest)] for j in range(len(rest))]
    load, order = [0] * 6, []

    def loaded(o):
        now = list(load)
        for axis in range(3):
            now[2 * axis] += o[axis] in (1, 2)
            now[2 * axis + 1] += o[axis] in (3, 2)
        return now

    while rest:
        far = max(map(dist, rest))
        spread = lambda o: (max(loaded(o)) - min(loaded(o)), sum(v * v for v in loaded(o)))
        best = min((o for o in rest if dist(o) == far), key=spread)
        load = loaded(best)
        rest.remove(best)
        order.append(best)
    return [((a * 4 + b) * 4 + c) * 2 + d for a, b, c, d in order] + [0]


def packed_order():
    order = send_order()
    return [sum(order[n + u] * NDEV ** u for u in range(UNROLL)) for n in range(0, NDEV, UNROLL)]


def pick(words, at, first=0):
    if len(words) == 1:
        return jnp.int32(words[0])
    half = len(words) // 2
    return jnp.where(at < first + half, pick(words[:half], at, first), pick(words[half:], at, first + half))


def partners(gx, gy, trip):
    word, found = pick(packed_order(), trip), []
    for u in range(UNROLL):
        o = lax.rem(word // NDEV ** u, NDEV)
        x = lax.rem(gx // 4 + o // 32, 4)
        y = lax.rem(gx + lax.rem(o // 8, 4), 4)
        z = lax.rem(gy // 2 + lax.rem(o // 2, 4), 4)
        found.append((x * 4 + y, z * 2 + lax.rem(gy + o, 2)))
    return found


def bucket(blocks, out_ids, inv_ref, pos_ref, at_ref, bt_ref):
    ids = jnp.concatenate([blocks[k:k + 1, :] for k in range(SLOTS)], axis=1)
    target = ids >> LOCAL_BITS
    within = ids & (ROWS - 1)
    within = (within & (ZB - 1)) * (CX * CY) + (within >> 2)
    order = lax.broadcasted_iota(i32, (1, REQ), 1)
    order = (order & (BLOCKS - 1)) * SLOTS + (order >> 6)
    at_ref[...] = jnp.where(lax.broadcasted_iota(i32, (NDEV, REQ), 0) == target, 1.0, 0.0).astype(bf16)
    step = 256
    before = lax.broadcasted_iota(i32, (step, step), 0) < lax.broadcasted_iota(i32, (step, step), 1)
    before = jnp.where(before, 1.0, 0.0).astype(bf16)
    running = jnp.zeros((NDEV, 1), f32)
    slot = lax.broadcasted_iota(i32, (CAP, step), 0)
    for k in range(REQ // step):
        cut = slice(k * step, (k + 1) * step)
        part = at_ref[:, cut]
        prefix = jnp.dot(part, before, preferred_element_type=f32) + running
        wide = part.astype(f32)
        rank = jnp.clip(jnp.sum(wide * prefix, axis=0, keepdims=True).astype(i32), 0, CAP - 1)
        running = running + jnp.sum(wide, axis=1, keepdims=True)
        hit = slot == rank
        pos_ref[:, cut] = target[:, cut] * CAP + rank
        for n, value in enumerate((within[:, cut] >> 7, within[:, cut] & 127, order[:, cut] >> 7, order[:, cut] & 127, None)):
            value = 1.0 if value is None else value.astype(f32)
            bt_ref[n * CAP:(n + 1) * CAP, cut] = jnp.where(hit, value, 0.0).astype(bf16)
    table = lax.dot_general(at_ref[...], bt_ref[...], (((1,), (1,)), ((), ())), preferred_element_type=f32)
    parts = [table[:, n * CAP:(n + 1) * CAP] for n in range(5)]
    present = parts[4] > 0.5
    row = jnp.where(present, parts[0] * 128.0 + parts[1], float(ROWS)).astype(i32)
    out_ids[...] = jnp.clip(row, 0, ROWS).reshape(GX, GY, 1, CAP)
    source = jnp.where(present, parts[2] * 128.0 + parts[3], float(REQ)).astype(i32)
    inv_ref[...] = jnp.clip(source, 0, REQ)


def shifted_sum(field, x, row):
    lane = lax.broadcasted_iota(i32, (8, WIDTH), 1)
    first, final = lane == 0, lane == WIDTH - 1
    at = lambda q, dx, dr: field[q, x + dx, pl.ds(row + dr, 8), :]
    centers = [at(q, 0, 0) for q in range(ZB)]
    up = [pltpu.roll(c, 1, 1) for c in centers]
    down = [pltpu.roll(c, WIDTH - 1, 1) for c in centers]
    sides = []
    for q in range(ZB):
        below = jnp.where(first, up[q - 1] if q > 0 else 0.0, up[q])
        above = jnp.where(final, down[q + 1] if q < ZB - 1 else 0.0, down[q])
        sides.append((at(q, -1, 0) + at(q, 1, 0)) + (at(q, 0, -1) + at(q, 0, 1)) + (below + above))
    return centers, sides


def step_kernel(blocks, dens_hbm, weights_hbm, counts_hbm, observed_hbm, inverse_hbm,
                ext_hbm, ids_hbm, exp_hbm, base_hbm, arr_hbm,
                counts, observed, inverse_var, ext_t,
                dens, out_ids, mid_ids, in_ids, ids_s, inv_v, inv_s, pos_v, pos_s, at_ref, bt_ref,
                rows_exp, served, ret, rows, w_ref, obs4, inv4, ext4, wgt4, sens, stage, parcel,
                xlo, xhi, ylo, yhi, field, smooth, base,
                entered, s_id, r_id, s_row, r_row, local, s_halo, r_halo):
    gx, gy = lax.axis_index("gx"), lax.axis_index("gy")
    me = gx * GY + gy
    gxm, gxp = lax.rem(gx + GX - 1, GX), lax.rem(gx + 1, GX)
    gym, gyp = lax.rem(gy + GY - 1, GY), lax.rem(gy + 1, GY)
    column = [lax.rem(gx + d, GX) for d in (1, 15, 4, 12, 3, 13, 5, 11, 7, 9, 2, 14, 6, 10, 8)]
    line = [lax.rem(gy + d, GY) for d in (1, 7, 2, 6, 3, 5, 4)]
    greeted = [(t, gy) for t in column] + [(gx, t) for t in line] + [(a, b) for a in (gxm, gxp) for b in (gym, gyp)]
    barrier = pltpu.get_barrier_semaphore()
    for to in greeted:
        pl.semaphore_signal(barrier, inc=1, device_id=to, device_id_type=MESH)

    loads = []
    for q in range(ZB):
        part = dens_hbm.at[:, :, pl.ds(q * WIDTH, WIDTH)]
        loads.append(pltpu.make_async_copy(part, field.at[q, pl.ds(2, CX), pl.ds(8, CY)], local.at[q]))
    w_load = pltpu.make_async_copy(weights_hbm, w_ref, local.at[4])
    for load in loads:
        load.start()
    w_load.start()
    small = [
        pltpu.make_async_copy(src, dst, local.at[8 + n])
        for n, (src, dst) in enumerate(((counts_hbm, counts), (observed_hbm, observed), (inverse_hbm, inverse_var)))
    ]
    for load in small:
        load.start()

    bucket(blocks, out_ids, inv_v, pos_v, at_ref, bt_ref)
    to_smem = [pltpu.make_async_copy(inv_v, inv_s, local.at[5]), pltpu.make_async_copy(pos_v, pos_s, local.at[6])]
    for copy in to_smem:
        copy.start()

    pl.semaphore_wait(barrier, len(greeted))
    for t in line:
        pl.semaphore_signal(entered, inc=1, device_id=(gx, t), device_id_type=MESH)
    own = pltpu.make_async_copy(out_ids.at[gx], mid_ids.at[gx], local.at[7])
    own.start()
    for t in column:
        remote(out_ids.at[t], mid_ids.at[gx], s_id.at[0], r_id.at[0], (t, gy)).start()

    for load in loads:
        load.wait()
    halos = [
        (field.at[:, pl.ds(CX, 2), pl.ds(8, CY)], xlo, (gxp, gy)),
        (field.at[:, pl.ds(2, 2), pl.ds(8, CY)], xhi, (gxm, gy)),
        (field.at[:, pl.ds(2, CX), pl.ds(CY, 8)], ylo.at[:, pl.ds(1, CX)], (gx, gyp)),
        (field.at[:, pl.ds(2, CX), pl.ds(8, 8)], yhi.at[:, pl.ds(1, CX)], (gx, gym)),
        (field.at[:, CX + 1, pl.ds(CY, 8)], ylo.at[:, 0], (gxp, gyp)),
        (field.at[:, 2, pl.ds(CY, 8)], ylo.at[:, CX + 1], (gxm, gyp)),
        (field.at[:, CX + 1, pl.ds(8, 8)], yhi.at[:, 0], (gxp, gym)),
        (field.at[:, 2, pl.ds(8, 8)], yhi.at[:, CX + 1], (gxm, gym)),
    ]
    halos = [remote(src, dst, s_halo.at[n], r_halo.at[n], to) for n, (src, dst, to) in enumerate(halos)]

    def gather_source(x, _):
        for q in range(ZB):
            dens[pl.ds(pl.multiple_of(q * CX * CY + x * CY, CY), CY), :] = field[q, x + 2, pl.ds(8, CY), :]
        return 0

    lax.fori_loop(0, CX, gather_source, 0)
    dens[pl.ds(ROWS, 8), :] = jnp.zeros((8, WIDTH), f32)
    own.wait()
    drain(mid_ids.at[pl.ds(0, GX - 1)], r_id.at[0])
    pl.semaphore_wait(entered, len(line))
    own = pltpu.make_async_copy(mid_ids.at[:, gy], in_ids.at[:, gy], local.at[7])
    own.start()
    for t in line:
        remote(mid_ids.at[:, t], in_ids.at[:, gy], s_id.at[1], r_id.at[1], (gx, t)).start()
    for copy in halos:
        copy.start()

    for load in small:
        load.wait()
    for ref, four in ((observed, obs4), (inverse_var, inv4)):
        wide = jnp.concatenate([ref[...], ref[...]], axis=1)
        four[...] = jnp.concatenate([wide] * 4, axis=0).T
    sens[pl.ds(REQ, 8), :] = jnp.zeros((8, WIDTH), f32)
    own.wait()
    drain(in_ids.at[:, pl.ds(0, GY - 1)], r_id.at[1])
    ids_copy = pltpu.make_async_copy(in_ids, ids_s, local.at[7])
    ids_copy.start()
    ids_store = pltpu.make_async_copy(in_ids, ids_hbm, local.at[11])
    ids_store.start()
    ids_copy.wait()

    def serve(tx, ty, at):
        for c in range(CAP):
            rows_exp[at, c, :] = dens[ids_s[tx, ty, 0, c], :]
        values = jnp.exp(rows_exp[at])
        rows_exp[at] = step_rate * values
        served[at] = values.astype(bf16)

    def send_rows(trip, count):
        for u, (tx, ty) in enumerate(partners(gx, gy, trip)):
            at = tx * GY + ty
            serve(tx, ty, at)
            if u < count:
                remote(served.at[at], ret.at[me], s_row.at[0], r_row.at[0], (tx, ty)).start()
        return 0

    trips = NDEV // UNROLL
    lax.fori_loop(0, trips - 1, lambda trip, _: send_rows(trip, UNROLL), 0)
    send_rows(trips - 1, UNROLL - 1)
    keep = pltpu.make_async_copy(served.at[me], ret.at[me], local.at[0])
    keep.start()
    exp_store = pltpu.make_async_copy(rows_exp, exp_hbm, local.at[1])
    exp_store.start()

    for copy in halos:
        copy.wait()
    low_x, high_x, low_y, high_y = gx > 0, gx < GX - 1, gy > 0, gy < GY - 1
    blank = jnp.zeros((8, WIDTH), f32)
    for q in range(ZB):
        for n in range(2):
            field[q, n, pl.ds(8, CY), :] = jnp.where(low_x, xlo[q, n], 0.0)
            field[q, CX + 2 + n, pl.ds(8, CY), :] = jnp.where(high_x, xhi[q, n], 0.0)

        def edge(x, _):
            field[q, x + 1, pl.ds(0, 8), :] = jnp.where(low_y, ylo[q, x], 0.0)
            field[q, x + 1, pl.ds(8 + CY, 8), :] = jnp.where(high_y, yhi[q, x], 0.0)
            return 0

        lax.fori_loop(1, CX + 1, edge, 0)
        for x, inside in ((0, low_x), (CX + 1, high_x)):
            field[q, x + 1, pl.ds(0, 8), :] = jnp.where(low_y & inside, ylo[q, x], 0.0)
            field[q, x + 1, pl.ds(8 + CY, 8), :] = jnp.where(high_y & inside, yhi[q, x], 0.0)
    sub = lax.broadcasted_iota(i32, (8, WIDTH), 0)
    top_keep = (sub > 0) | low_y
    bottom_keep = (sub != 1) | high_y

    def smooth_plane(x, inside=None):
        for n in range(9):
            centers, sides = shifted_sum(field, x + 1, 7 + 8 * n)
            for q in range(ZB):
                value = center_weight * centers[q] - sides[q]
                if n == 0:
                    value = jnp.where(top_keep, value, 0.0)
                if n == 8:
                    value = jnp.where(bottom_keep, value, 0.0)
                if inside is not None:
                    value = jnp.where(inside, value, 0.0)
                smooth[q, x, pl.ds(8 * n, 8), :] = value

    def base_plane(x):
        for n in range(8):
            centers, sides = shifted_sum(smooth, x + 1, 8 * n + 1)
            for q in range(ZB):
                prior = center_weight * centers[q] - sides[q]
                now = field[q, x + 2, pl.ds(8 + 8 * n, 8), :]
                base[q, x, pl.ds(8 * n, 8), :] = now - (step_rate * prior_weight) * prior

    smooth_plane(0, low_x)

    def smooth_all(x, _):
        smooth_plane(x)
        return 0

    lax.fori_loop(1, CX + 1, smooth_all, 0)
    smooth_plane(CX + 1, high_x)
    w_load.wait()
    for copy in to_smem:
        copy.wait()
    keep.wait()
    drain(ret.at[pl.ds(0, NDEV - 1)], r_row.at[0])

    def widen(n, _):
        for u in range(UNROLL):
            rows[pl.ds(pl.multiple_of((n * UNROLL + u) * CAP, CAP), CAP), :] = ret[n * UNROLL + u].astype(f32)
        return 0

    lax.fori_loop(0, NDEV // UNROLL, widen, 0)
    deep = 8 * STARS
    mine = (lax.broadcasted_iota(i32, (8, deep), 1) >> 5) == lax.broadcasted_iota(i32, (8, deep), 0)
    lane = lax.broadcasted_iota(i32, (STARS, WIDTH), 1)
    diagonal = (lane & (STARS - 1)) == lax.broadcasted_iota(i32, (STARS, WIDTH), 0)
    star = lax.broadcasted_iota(i32, (1, WIDTH), 1) & (STARS - 1)

    def extinct(i):
        for u in range(UNROLL):
            b = i * UNROLL + u
            totals = [jnp.zeros((STARS, WIDTH), f32) for _ in range(2)]
            for k in range(SLOTS):
                line_k = rows[pl.ds(pos_s[0, k * BLOCKS + b], 1), :]
                totals[k % 2] = totals[k % 2] + w_ref[b, k].astype(f32) * line_k
            total = jnp.sum(totals[0] + totals[1], axis=1, keepdims=True)
            ext = jnp.sum(jnp.where(diagonal, total, 0.0), axis=0, keepdims=True)
            ext4[pl.ds(b, 1), :] = ext
            residual = inv4[pl.ds(b, 1), :] * (ext - obs4[pl.ds(b, 1), :])
            wgt4[pl.ds(b, 1), :] = jnp.where(star < counts[b], residual, 0.0)

    def sensitive(i):
        for u in range(UNROLL):
            b = i * UNROLL + u
            line_b = wgt4[pl.ds(b, 1), :]
            left = jnp.where(mine, jnp.concatenate([line_b, line_b], axis=1), 0.0).astype(bf16)
            for n in range(SLOTS // 8):
                sens[pl.ds(pl.multiple_of(b * SLOTS + n * 8, 8), 8), :] = jnp.dot(
                    left, w_ref[b, pl.ds(n * 8, 8)].reshape(deep, WIDTH), preferred_element_type=f32
                )

    extinct(0)

    def both(i, _):
        sensitive(i - 1)
        extinct(i)
        return 0

    lax.fori_loop(1, BLOCKS // UNROLL, both, 0)
    sensitive(BLOCKS // UNROLL - 1)
    ext_t[...] = jnp.concatenate([ext4[...], ext4[...]], axis=0).T[:STARS, :BLOCKS]
    ext_store = pltpu.make_async_copy(ext_t, ext_hbm, local.at[12])
    ext_store.start()

    slot_a, slot_b = lax.broadcasted_iota(i32, (CAP, CAP), 0), lax.broadcasted_iota(i32, (CAP, CAP), 1)
    eye, together = slot_a == slot_b, (slot_a >> 3) == (slot_b >> 3)

    def pack(tx, ty, at):
        for c in range(CAP):
            stage[at, c, :] = sens[inv_s[at, c], :]
        across = jnp.broadcast_to(out_ids[tx, ty].astype(f32), (CAP, CAP))
        down = jnp.sum(jnp.where(eye, across, 0.0), axis=1, keepdims=True)
        same = jnp.where((down == across) & together, 1.0, 0.0).astype(bf16)
        parcel[at] = jnp.dot(same, stage[at].astype(bf16), preferred_element_type=f32).astype(bf16)

    def pack_all(to):
        for tx, ty in to:
            pack(tx, ty, tx * GY + ty)

    def send_back(to):
        for tx, ty in to:
            remote(parcel.at[tx * GY + ty], arr_hbm.at[me], s_row.at[1], r_row.at[1], (tx, ty)).start()

    def give_back(it, _):
        to = partners(gx, gy, it)
        pack_all(to)
        base_plane(it)
        send_back(to)
        return 0

    lax.fori_loop(0, CX - 1, give_back, 0)
    to = partners(gx, gy, trips - 1)
    pack_all(to)
    send_back(to[:UNROLL - 1])
    base_plane(CX - 1)
    keep = pltpu.make_async_copy(parcel.at[me], arr_hbm.at[me], local.at[0])
    keep.start()
    base_store = pltpu.make_async_copy(base, base_hbm, local.at[2])
    base_store.start()
    keep.wait()
    ids_store.wait()
    ext_store.wait()
    exp_store.wait()
    base_store.wait()
    drain(out_ids.at[pl.ds(0, GX - 1)], s_id.at[0])
    drain(mid_ids.at[:, pl.ds(0, GY - 1)], s_id.at[1])
    drain(served.at[pl.ds(0, NDEV - 1)], s_row.at[0])
    drain(parcel.at[pl.ds(0, NDEV - 1)], s_row.at[1])
    drain(arr_hbm.at[pl.ds(0, NDEV - 1)], r_row.at[1])


def step(blocks, dens, weights, counts, observed, inverse_var):
    shape = jax.ShapeDtypeStruct
    v = pltpu.VMEM
    return pl.pallas_call(
        step_kernel,
        out_shape=(
            shape((STARS, BLOCKS), f32),
            shape((GX, GY, 1, CAP), i32),
            shape((NDEV, CAP, WIDTH), f32),
            shape((ZB, CX, CY, WIDTH), f32),
            shape((NDEV, CAP, WIDTH), bf16),
        ),
        in_specs=[
            whole(v), whole(pltpu.HBM), whole(pltpu.HBM), whole(pltpu.HBM), whole(pltpu.HBM), whole(pltpu.HBM),
        ],
        out_specs=[whole(pltpu.HBM)] * 5,
        scratch_shapes=[
            pltpu.SMEM((BLOCKS,), i32), v((STARS, BLOCKS), f32), v((STARS, BLOCKS), f32), v((STARS, BLOCKS), f32),
            v((ROWS + 8, WIDTH), f32),
            v((GX, GY, 1, CAP), i32), v((GX, GY, 1, CAP), i32), v((GX, GY, 1, CAP), i32), pltpu.SMEM((GX, GY, 1, CAP), i32),
            v((NDEV, CAP), i32), pltpu.SMEM((NDEV, CAP), i32), v((1, REQ), i32), pltpu.SMEM((1, REQ), i32),
            v((NDEV, REQ), bf16), v((5 * CAP, REQ), bf16),
            v((NDEV, CAP, WIDTH), f32), v((NDEV, CAP, WIDTH), bf16), v((NDEV, CAP, WIDTH), bf16),
            v((NDEV * CAP, WIDTH), f32), v((BLOCKS, SLOTS, STARS, WIDTH), bf16),
            v((WIDTH, WIDTH), f32), v((WIDTH, WIDTH), f32), v((BLOCKS, WIDTH), f32), v((BLOCKS, WIDTH), f32),
            v((REQ + 8, WIDTH), f32), v((NDEV, CAP, WIDTH), f32), v((NDEV, CAP, WIDTH), bf16),
            v((ZB, 2, CY, WIDTH), f32), v((ZB, 2, CY, WIDTH), f32),
            v((ZB, CX + 2, 8, WIDTH), f32), v((ZB, CX + 2, 8, WIDTH), f32),
            v((ZB, CX + 4, CY + 16, WIDTH), f32), v((ZB, CX + 2, CY + 8, WIDTH), f32), v((ZB, CX, CY, WIDTH), f32),
            pltpu.SemaphoreType.REGULAR, DMA((2,)), DMA((2,)), DMA((2,)), DMA((2,)), DMA((13,)), DMA((8,)), DMA((8,)),
        ],
        name="step",
        compiler_params=pltpu.CompilerParams(collective_id=0, has_side_effects=True, vmem_limit_bytes=60 << 20),
    )(blocks, dens, weights, counts, observed, inverse_var)


def update_kernel(ids_hbm, ext_in, exp_hbm, base_hbm, arr_hbm, ext_out, out_hbm, ids, new, rows_exp, arrived, add, sem):
    load_exp = pltpu.make_async_copy(exp_hbm, rows_exp, sem.at[0])
    load_arr = pltpu.make_async_copy(arr_hbm, arrived, sem.at[1])
    load_exp.start()
    load_arr.start()
    load_ids = pltpu.make_async_copy(ids_hbm, ids, sem.at[6])
    load_ids.start()
    bases = []
    for q in range(ZB):
        bases.append(pltpu.make_async_copy(base_hbm.at[q], new.at[pl.ds(q * CX * CY, CX * CY)], sem.at[2 + q]))
        bases[q].start()
    ext_copy = pltpu.make_async_copy(ext_in, ext_out, sem.at[7])
    ext_copy.start()
    new[pl.ds(ROWS, 8), :] = jnp.zeros((8, WIDTH), f32)
    load_exp.wait()
    load_arr.wait()

    def scale(n, _):
        for u in range(UNROLL):
            t = n * UNROLL + u
            add[t] = rows_exp[t] * arrived[t].astype(f32)
        return 0

    lax.fori_loop(0, NDEV // UNROLL, scale, 0)
    load_ids.wait()
    for load in bases:
        load.wait()

    def source(t, _):
        tx, ty = t // GY, lax.rem(t, GY)

        def eight(first):
            at = [ids[tx, ty, 0, first + c] for c in range(8)]
            values = [new[pl.ds(n, 1), :] - add[t, pl.ds(first + c, 1), :] for c, n in enumerate(at)]
            for n, value in zip(at, values):
                new[pl.ds(n, 1), :] = value

        eight(0)
        eight(8)

        @pl.when(ids[tx, ty, 0, 16] < ROWS)
        def _():
            eight(16)

            @pl.when(ids[tx, ty, 0, 24] < ROWS)
            def _():
                eight(24)

        return 0

    lax.fori_loop(0, NDEV, source, 0)
    stores = []
    for q in range(ZB):
        rows_of = new.at[pl.ds(q * CX * CY, CX * CY)]
        stores.append(pltpu.make_async_copy(
            rows_of.reshape(CX, CY, WIDTH), out_hbm.at[:, :, pl.ds(q * WIDTH, WIDTH)], sem.at[2 + q]
        ))
        stores[q].start()
    ext_copy.wait()
    for store in stores:
        store.wait()


def update(ids, ext, rows_exp, base, arrived):
    v = pltpu.VMEM
    return pl.pallas_call(
        update_kernel,
        out_shape=(jax.ShapeDtypeStruct((STARS, BLOCKS), f32), jax.ShapeDtypeStruct((CX, CY, ZB * WIDTH), f32)),
        in_specs=[whole(pltpu.HBM)] * 5,
        out_specs=[whole(pltpu.HBM)] * 2,
        scratch_shapes=[
            pltpu.SMEM((GX, GY, 1, CAP), i32),
            v((ROWS + 8, WIDTH), f32), v((NDEV, CAP, WIDTH), f32), v((NDEV, CAP, WIDTH), bf16), v((NDEV, CAP, WIDTH), f32),
            DMA((8,)),
        ],
        name="update",
        compiler_params=pltpu.CompilerParams(vmem_limit_bytes=62 << 20),
    )(ids, ext, rows_exp, base.reshape(ZB, CX * CY, WIDTH), arrived)


def on_device(log_density, weights, observed, inverse_var, star_counts, block_ids):
    ext, ids, rows_exp, base, arrived = step(
        block_ids.T, log_density, weights, star_counts, observed.T, inverse_var.T
    )
    ext, new = update(ids, ext, rows_exp, base, arrived)
    return (new, ext.T)


def solution(mesh):
    placed = (
        P("gx", "gy", None),
        P(("gx", "gy"), None, None, None),
        P(("gx", "gy"), None),
        P(("gx", "gy"), None),
        P(("gx", "gy")),
        P(("gx", "gy"), None),
    )
    return jax.shard_map(
        on_device,
        mesh=mesh,
        in_specs=placed,
        out_specs=(P("gx", "gy", None), P(("gx", "gy"), None)),
        check_vma=False,
    )
```

```python
import jax
import jax.numpy as jnp
from jax import lax
from jax.experimental import pallas as pl
from jax.experimental.pallas import tpu as pltpu
from jax.sharding import PartitionSpec as P

MESH = pl.DeviceIdType.MESH
DMA = pltpu.SemaphoreType.DMA
shift_kappa = 0.5
prior_weight = 0.05
step_rate = 2.0
f32, bf16, i32 = jnp.float32, jnp.bfloat16, jnp.int32

GX, GY = 16, 8
NDEV, CAP, WIDTH = 128, 32, 128
BLOCKS, SLOTS, STARS = 64, 32, 32
REQ = BLOCKS * SLOTS
CX, CY, ZB = 32, 64, 4
ROWS = CX * CY * ZB
LOCAL_BITS = 13
UNROLL = 4
center_weight = shift_kappa + 6.0


def whole(space):
    return pl.BlockSpec(memory_space=space)


def remote(src, dst, send, recv, to):
    return pltpu.make_async_remote_copy(
        src_ref=src, dst_ref=dst, send_sem=send, recv_sem=recv, device_id=to, device_id_type=MESH
    )


def drain(ref, sem):
    pltpu.make_async_copy(ref, ref, sem).wait()


def send_order():
    dist = lambda o: sum(min(v, 4 - v) for v in o[:3])
    rest = [(a, b, c, d) for a in range(4) for b in range(4) for c in range(4) for d in range(2)][1:]
    rest = [rest[j * 37 % len(rest)] for j in range(len(rest))]
    load, order = [0] * 6, []

    def loaded(o):
        now = list(load)
        for axis in range(3):
            now[2 * axis] += o[axis] in (1, 2)
            now[2 * axis + 1] += o[axis] in (3, 2)
        return now

    while rest:
        far = max(map(dist, rest))
        spread = lambda o: (max(loaded(o)) - min(loaded(o)), sum(v * v for v in loaded(o)))
        best = min((o for o in rest if dist(o) == far), key=spread)
        load = loaded(best)
        rest.remove(best)
        order.append(best)
    return [((a * 4 + b) * 4 + c) * 2 + d for a, b, c, d in order] + [0]


def packed_order():
    order = send_order()
    return [sum(order[n + u] * NDEV ** u for u in range(UNROLL)) for n in range(0, NDEV, UNROLL)]


def pick(words, at, first=0):
    if len(words) == 1:
        return jnp.int32(words[0])
    half = len(words) // 2
    return jnp.where(at < first + half, pick(words[:half], at, first), pick(words[half:], at, first + half))


def partners(gx, gy, trip):
    word, found = pick(packed_order(), trip), []
    for u in range(UNROLL):
        o = lax.rem(word // NDEV ** u, NDEV)
        x = lax.rem(gx // 4 + o // 32, 4)
        y = lax.rem(gx + lax.rem(o // 8, 4), 4)
        z = lax.rem(gy // 2 + lax.rem(o // 2, 4), 4)
        found.append((x * 4 + y, z * 2 + lax.rem(gy + o, 2)))
    return found


def bucket(blocks, out_ids, inv_ref, pos_ref, at_ref, bt_ref):
    ids = jnp.concatenate([blocks[k:k + 1, :] for k in range(SLOTS)], axis=1)
    target = ids >> LOCAL_BITS
    within = ids & (ROWS - 1)
    within = (within & (ZB - 1)) * (CX * CY) + (within >> 2)
    order = lax.broadcasted_iota(i32, (1, REQ), 1)
    order = (order & (BLOCKS - 1)) * SLOTS + (order >> 6)
    at_ref[...] = jnp.where(lax.broadcasted_iota(i32, (NDEV, REQ), 0) == target, 1.0, 0.0).astype(bf16)
    step = 256
    before = lax.broadcasted_iota(i32, (step, step), 0) < lax.broadcasted_iota(i32, (step, step), 1)
    before = jnp.where(before, 1.0, 0.0).astype(bf16)
    running = jnp.zeros((NDEV, 1), f32)
    slot = lax.broadcasted_iota(i32, (CAP, step), 0)
    for k in range(REQ // step):
        cut = slice(k * step, (k + 1) * step)
        part = at_ref[:, cut]
        prefix = jnp.dot(part, before, preferred_element_type=f32) + running
        wide = part.astype(f32)
        rank = jnp.clip(jnp.sum(wide * prefix, axis=0, keepdims=True).astype(i32), 0, CAP - 1)
        running = running + jnp.sum(wide, axis=1, keepdims=True)
        hit = slot == rank
        pos_ref[:, cut] = target[:, cut] * CAP + rank
        for n, value in enumerate((within[:, cut] >> 7, within[:, cut] & 127, order[:, cut] >> 7, order[:, cut] & 127, None)):
            value = 1.0 if value is None else value.astype(f32)
            bt_ref[n * CAP:(n + 1) * CAP, cut] = jnp.where(hit, value, 0.0).astype(bf16)
    table = lax.dot_general(at_ref[...], bt_ref[...], (((1,), (1,)), ((), ())), preferred_element_type=f32)
    parts = [table[:, n * CAP:(n + 1) * CAP] for n in range(5)]
    present = parts[4] > 0.5
    row = jnp.where(present, parts[0] * 128.0 + parts[1], float(ROWS)).astype(i32)
    out_ids[...] = jnp.clip(row, 0, ROWS).reshape(GX, GY, 1, CAP)
    source = jnp.where(present, parts[2] * 128.0 + parts[3], float(REQ)).astype(i32)
    inv_ref[...] = jnp.clip(source, 0, REQ)


def shifted_sum(field, x, row):
    lane = lax.broadcasted_iota(i32, (8, WIDTH), 1)
    first, final = lane == 0, lane == WIDTH - 1
    at = lambda q, dx, dr: field[q, x + dx, pl.ds(row + dr, 8), :]
    centers = [at(q, 0, 0) for q in range(ZB)]
    up = [pltpu.roll(c, 1, 1) for c in centers]
    down = [pltpu.roll(c, WIDTH - 1, 1) for c in centers]
    sides = []
    for q in range(ZB):
        below = jnp.where(first, up[q - 1] if q > 0 else 0.0, up[q])
        above = jnp.where(final, down[q + 1] if q < ZB - 1 else 0.0, down[q])
        sides.append((at(q, -1, 0) + at(q, 1, 0)) + (at(q, 0, -1) + at(q, 0, 1)) + (below + above))
    return centers, sides


def step_kernel(blocks, dens_hbm, weights_hbm, counts_hbm, observed_hbm, inverse_hbm,
                ext_hbm, ids_hbm, exp_hbm, base_hbm, arr_hbm,
                counts, observed, inverse_var, ext_t,
                dens, out_ids, mid_ids, in_ids, ids_s, inv_v, inv_s, pos_v, pos_s, at_ref, bt_ref,
                rows_exp, served, ret, rows, w_ref, obs4, inv4, ext4, wgt4, sens, stage, parcel,
                xlo, xhi, ylo, yhi, field, smooth, base,
                entered, s_id, r_id, s_row, r_row, local, s_halo, r_halo):
    gx, gy = lax.axis_index("gx"), lax.axis_index("gy")
    me = gx * GY + gy
    gxm, gxp = lax.rem(gx + GX - 1, GX), lax.rem(gx + 1, GX)
    gym, gyp = lax.rem(gy + GY - 1, GY), lax.rem(gy + 1, GY)
    column = [lax.rem(gx + d, GX) for d in (1, 15, 4, 12, 3, 13, 5, 11, 7, 9, 2, 14, 6, 10, 8)]
    line = [lax.rem(gy + d, GY) for d in (1, 7, 2, 6, 3, 5, 4)]
    greeted = [(t, gy) for t in column] + [(gx, t) for t in line] + [(a, b) for a in (gxm, gxp) for b in (gym, gyp)]
    barrier = pltpu.get_barrier_semaphore()
    for to in greeted:
        pl.semaphore_signal(barrier, inc=1, device_id=to, device_id_type=MESH)

    loads = []
    for q in range(ZB):
        part = dens_hbm.at[:, :, pl.ds(q * WIDTH, WIDTH)]
        loads.append(pltpu.make_async_copy(part, field.at[q, pl.ds(2, CX), pl.ds(8, CY)], local.at[q]))
    w_load = pltpu.make_async_copy(weights_hbm, w_ref, local.at[4])
    for load in loads:
        load.start()
    w_load.start()
    small = [
        pltpu.make_async_copy(src, dst, local.at[8 + n])
        for n, (src, dst) in enumerate(((counts_hbm, counts), (observed_hbm, observed), (inverse_hbm, inverse_var)))
    ]
    for load in small:
        load.start()

    bucket(blocks, out_ids, inv_v, pos_v, at_ref, bt_ref)
    to_smem = [pltpu.make_async_copy(inv_v, inv_s, local.at[5]), pltpu.make_async_copy(pos_v, pos_s, local.at[6])]
    for copy in to_smem:
        copy.start()

    pl.semaphore_wait(barrier, len(greeted))
    for t in line:
        pl.semaphore_signal(entered, inc=1, device_id=(gx, t), device_id_type=MESH)
    own = pltpu.make_async_copy(out_ids.at[gx], mid_ids.at[gx], local.at[7])
    own.start()
    for t in column:
        remote(out_ids.at[t], mid_ids.at[gx], s_id.at[0], r_id.at[0], (t, gy)).start()

    for load in loads:
        load.wait()
    halos = [
        (field.at[:, pl.ds(CX, 2), pl.ds(8, CY)], xlo, (gxp, gy)),
        (field.at[:, pl.ds(2, 2), pl.ds(8, CY)], xhi, (gxm, gy)),
        (field.at[:, pl.ds(2, CX), pl.ds(CY + 6, 2)], ylo.at[:, pl.ds(1, CX), pl.ds(6, 2)], (gx, gyp)),
        (field.at[:, pl.ds(2, CX), pl.ds(8, 2)], yhi.at[:, pl.ds(1, CX), pl.ds(0, 2)], (gx, gym)),
        (field.at[:, CX + 1, pl.ds(CY, 8)], ylo.at[:, 0], (gxp, gyp)),
        (field.at[:, 2, pl.ds(CY, 8)], ylo.at[:, CX + 1], (gxm, gyp)),
        (field.at[:, CX + 1, pl.ds(8, 8)], yhi.at[:, 0], (gxp, gym)),
        (field.at[:, 2, pl.ds(8, 8)], yhi.at[:, CX + 1], (gxm, gym)),
    ]
    halos = [remote(src, dst, s_halo.at[n], r_halo.at[n], to) for n, (src, dst, to) in enumerate(halos)]
    for copy in halos:
        copy.start()

    def gather_source(x, _):
        for q in range(ZB):
            dens[pl.ds(pl.multiple_of(q * CX * CY + x * CY, CY), CY), :] = field[q, x + 2, pl.ds(8, CY), :]
        return 0

    lax.fori_loop(0, CX, gather_source, 0)
    dens[pl.ds(ROWS, 8), :] = jnp.zeros((8, WIDTH), f32)
    own.wait()
    drain(mid_ids.at[pl.ds(0, GX - 1)], r_id.at[0])
    pl.semaphore_wait(entered, len(line))
    own = pltpu.make_async_copy(mid_ids.at[:, gy], in_ids.at[:, gy], local.at[7])
    own.start()
    for t in line:
        remote(mid_ids.at[:, t], in_ids.at[:, gy], s_id.at[1], r_id.at[1], (gx, t)).start()

    for load in small:
        load.wait()
    for ref, four in ((observed, obs4), (inverse_var, inv4)):
        wide = jnp.concatenate([ref[...], ref[...]], axis=1)
        four[...] = jnp.concatenate([wide] * 4, axis=0).T
    sens[pl.ds(REQ, 8), :] = jnp.zeros((8, WIDTH), f32)
    own.wait()
    drain(in_ids.at[:, pl.ds(0, GY - 1)], r_id.at[1])
    ids_copy = pltpu.make_async_copy(in_ids, ids_s, local.at[7])
    ids_copy.start()
    ids_store = pltpu.make_async_copy(in_ids, ids_hbm, local.at[11])
    ids_store.start()
    ids_copy.wait()

    def serve(tx, ty, at):
        for c in range(CAP):
            rows_exp[at, c, :] = dens[ids_s[tx, ty, 0, c], :]
        values = jnp.exp(rows_exp[at])
        rows_exp[at] = step_rate * values
        served[at] = values.astype(bf16)

    def send_rows(trip, count):
        for u, (tx, ty) in enumerate(partners(gx, gy, trip)):
            at = tx * GY + ty
            serve(tx, ty, at)
            if u < count:
                remote(served.at[at], ret.at[me], s_row.at[0], r_row.at[0], (tx, ty)).start()
        return 0

    trips = NDEV // UNROLL
    lax.fori_loop(0, trips - 1, lambda trip, _: send_rows(trip, UNROLL), 0)
    send_rows(trips - 1, UNROLL - 1)
    keep = pltpu.make_async_copy(served.at[me], ret.at[me], local.at[0])
    keep.start()
    exp_store = pltpu.make_async_copy(rows_exp, exp_hbm, local.at[1])
    exp_store.start()

    for copy in halos:
        copy.wait()
    low_x, high_x, low_y, high_y = gx > 0, gx < GX - 1, gy > 0, gy < GY - 1
    blank = jnp.zeros((8, WIDTH), f32)
    for q in range(ZB):
        for n in range(2):
            field[q, n, pl.ds(8, CY), :] = jnp.where(low_x, xlo[q, n], 0.0)
            field[q, CX + 2 + n, pl.ds(8, CY), :] = jnp.where(high_x, xhi[q, n], 0.0)

        def edge(x, _):
            field[q, x + 1, pl.ds(0, 8), :] = jnp.where(low_y, ylo[q, x], 0.0)
            field[q, x + 1, pl.ds(8 + CY, 8), :] = jnp.where(high_y, yhi[q, x], 0.0)
            return 0

        lax.fori_loop(1, CX + 1, edge, 0)
        for x, inside in ((0, low_x), (CX + 1, high_x)):
            field[q, x + 1, pl.ds(0, 8), :] = jnp.where(low_y & inside, ylo[q, x], 0.0)
            field[q, x + 1, pl.ds(8 + CY, 8), :] = jnp.where(high_y & inside, yhi[q, x], 0.0)
    sub = lax.broadcasted_iota(i32, (8, WIDTH), 0)
    top_keep = (sub > 0) | low_y
    bottom_keep = (sub != 1) | high_y

    def smooth_plane(x, inside=None):
        for n in range(9):
            centers, sides = shifted_sum(field, x + 1, 7 + 8 * n)
            for q in range(ZB):
                value = center_weight * centers[q] - sides[q]
                if n == 0:
                    value = jnp.where(top_keep, value, 0.0)
                if n == 8:
                    value = jnp.where(bottom_keep, value, 0.0)
                if inside is not None:
                    value = jnp.where(inside, value, 0.0)
                smooth[q, x, pl.ds(8 * n, 8), :] = value

    def base_plane(x):
        for n in range(8):
            centers, sides = shifted_sum(smooth, x + 1, 8 * n + 1)
            for q in range(ZB):
                prior = center_weight * centers[q] - sides[q]
                now = field[q, x + 2, pl.ds(8 + 8 * n, 8), :]
                base[q, x, pl.ds(8 * n, 8), :] = now - (step_rate * prior_weight) * prior

    smooth_plane(0, low_x)

    def smooth_all(x, _):
        smooth_plane(x)
        return 0

    lax.fori_loop(1, CX + 1, smooth_all, 0)
    smooth_plane(CX + 1, high_x)
    w_load.wait()
    for copy in to_smem:
        copy.wait()
    keep.wait()
    drain(ret.at[pl.ds(0, NDEV - 1)], r_row.at[0])

    def widen(n, _):
        for u in range(UNROLL):
            rows[pl.ds(pl.multiple_of((n * UNROLL + u) * CAP, CAP), CAP), :] = ret[n * UNROLL + u].astype(f32)
        return 0

    lax.fori_loop(0, NDEV // UNROLL, widen, 0)
    deep = 8 * STARS
    mine = (lax.broadcasted_iota(i32, (8, deep), 1) >> 5) == lax.broadcasted_iota(i32, (8, deep), 0)
    lane = lax.broadcasted_iota(i32, (STARS, WIDTH), 1)
    diagonal = (lane & (STARS - 1)) == lax.broadcasted_iota(i32, (STARS, WIDTH), 0)
    star = lax.broadcasted_iota(i32, (1, WIDTH), 1) & (STARS - 1)

    def extinct(i):
        for u in range(UNROLL):
            b = i * UNROLL + u
            totals = [jnp.zeros((STARS, WIDTH), f32) for _ in range(2)]
            for k in range(SLOTS):
                line_k = rows[pl.ds(pos_s[0, k * BLOCKS + b], 1), :]
                totals[k % 2] = totals[k % 2] + w_ref[b, k].astype(f32) * line_k
            total = jnp.sum(totals[0] + totals[1], axis=1, keepdims=True)
            ext = jnp.sum(jnp.where(diagonal, total, 0.0), axis=0, keepdims=True)
            ext4[pl.ds(b, 1), :] = ext
            residual = inv4[pl.ds(b, 1), :] * (ext - obs4[pl.ds(b, 1), :])
            wgt4[pl.ds(b, 1), :] = jnp.where(star < counts[b], residual, 0.0)

    def sensitive(i):
        for u in range(UNROLL):
            b = i * UNROLL + u
            line_b = wgt4[pl.ds(b, 1), :]
            left = jnp.where(mine, jnp.concatenate([line_b, line_b], axis=1), 0.0).astype(bf16)
            for n in range(SLOTS // 8):
                sens[pl.ds(pl.multiple_of(b * SLOTS + n * 8, 8), 8), :] = jnp.dot(
                    left, w_ref[b, pl.ds(n * 8, 8)].reshape(deep, WIDTH), preferred_element_type=f32
                )

    extinct(0)

    def both(i, _):
        sensitive(i - 1)
        extinct(i)
        return 0

    lax.fori_loop(1, BLOCKS // UNROLL, both, 0)
    sensitive(BLOCKS // UNROLL - 1)
    ext_t[...] = jnp.concatenate([ext4[...], ext4[...]], axis=0).T[:STARS, :BLOCKS]
    ext_store = pltpu.make_async_copy(ext_t, ext_hbm, local.at[12])
    ext_store.start()

    slot_a, slot_b = lax.broadcasted_iota(i32, (CAP, CAP), 0), lax.broadcasted_iota(i32, (CAP, CAP), 1)
    eye, together = slot_a == slot_b, (slot_a >> 3) == (slot_b >> 3)

    def pack(tx, ty, at):
        for c in range(CAP):
            stage[at, c, :] = sens[inv_s[at, c], :]
        across = jnp.broadcast_to(out_ids[tx, ty].astype(f32), (CAP, CAP))
        down = jnp.sum(jnp.where(eye, across, 0.0), axis=1, keepdims=True)
        same = jnp.where((down == across) & together, 1.0, 0.0).astype(bf16)
        parcel[at] = jnp.dot(same, stage[at].astype(bf16), preferred_element_type=f32).astype(bf16)

    def pack_all(to):
        for tx, ty in to:
            pack(tx, ty, tx * GY + ty)

    def send_back(to):
        for tx, ty in to:
            remote(parcel.at[tx * GY + ty], arr_hbm.at[me], s_row.at[1], r_row.at[1], (tx, ty)).start()

    def give_back(it, _):
        to = partners(gx, gy, it)
        pack_all(to)
        base_plane(it)
        send_back(to)
        return 0

    lax.fori_loop(0, CX - 1, give_back, 0)
    to = partners(gx, gy, trips - 1)
    pack_all(to)
    send_back(to[:UNROLL - 1])
    base_plane(CX - 1)
    keep = pltpu.make_async_copy(parcel.at[me], arr_hbm.at[me], local.at[0])
    keep.start()
    base_store = pltpu.make_async_copy(base, base_hbm, local.at[2])
    base_store.start()
    keep.wait()
    ids_store.wait()
    ext_store.wait()
    exp_store.wait()
    base_store.wait()
    drain(out_ids.at[pl.ds(0, GX - 1)], s_id.at[0])
    drain(mid_ids.at[:, pl.ds(0, GY - 1)], s_id.at[1])
    drain(served.at[pl.ds(0, NDEV - 1)], s_row.at[0])
    drain(parcel.at[pl.ds(0, NDEV - 1)], s_row.at[1])
    drain(arr_hbm.at[pl.ds(0, NDEV - 1)], r_row.at[1])


def step(blocks, dens, weights, counts, observed, inverse_var):
    shape = jax.ShapeDtypeStruct
    v = pltpu.VMEM
    return pl.pallas_call(
        step_kernel,
        out_shape=(
            shape((STARS, BLOCKS), f32),
            shape((GX, GY, 1, CAP), i32),
            shape((NDEV, CAP, WIDTH), f32),
            shape((ZB, CX, CY, WIDTH), f32),
            shape((NDEV, CAP, WIDTH), bf16),
        ),
        in_specs=[
            whole(v), whole(pltpu.HBM), whole(pltpu.HBM), whole(pltpu.HBM), whole(pltpu.HBM), whole(pltpu.HBM),
        ],
        out_specs=[whole(pltpu.HBM)] * 5,
        scratch_shapes=[
            pltpu.SMEM((BLOCKS,), i32), v((STARS, BLOCKS), f32), v((STARS, BLOCKS), f32), v((STARS, BLOCKS), f32),
            v((ROWS + 8, WIDTH), f32),
            v((GX, GY, 1, CAP), i32), v((GX, GY, 1, CAP), i32), v((GX, GY, 1, CAP), i32), pltpu.SMEM((GX, GY, 1, CAP), i32),
            v((NDEV, CAP), i32), pltpu.SMEM((NDEV, CAP), i32), v((1, REQ), i32), pltpu.SMEM((1, REQ), i32),
            v((NDEV, REQ), bf16), v((5 * CAP, REQ), bf16),
            v((NDEV, CAP, WIDTH), f32), v((NDEV, CAP, WIDTH), bf16), v((NDEV, CAP, WIDTH), bf16),
            v((NDEV * CAP, WIDTH), f32), v((BLOCKS, SLOTS, STARS, WIDTH), bf16),
            v((WIDTH, WIDTH), f32), v((WIDTH, WIDTH), f32), v((BLOCKS, WIDTH), f32), v((BLOCKS, WIDTH), f32),
            v((REQ + 8, WIDTH), f32), v((NDEV, CAP, WIDTH), f32), v((NDEV, CAP, WIDTH), bf16),
            v((ZB, 2, CY, WIDTH), f32), v((ZB, 2, CY, WIDTH), f32),
            v((ZB, CX + 2, 8, WIDTH), f32), v((ZB, CX + 2, 8, WIDTH), f32),
            v((ZB, CX + 4, CY + 16, WIDTH), f32), v((ZB, CX + 2, CY + 8, WIDTH), f32), v((ZB, CX, CY, WIDTH), f32),
            pltpu.SemaphoreType.REGULAR, DMA((2,)), DMA((2,)), DMA((2,)), DMA((2,)), DMA((13,)), DMA((8,)), DMA((8,)),
        ],
        name="step",
        compiler_params=pltpu.CompilerParams(collective_id=0, has_side_effects=True, vmem_limit_bytes=60 << 20),
    )(blocks, dens, weights, counts, observed, inverse_var)


def update_kernel(ids_hbm, ext_in, exp_hbm, base_hbm, arr_hbm, ext_out, out_hbm, ids, new, rows_exp, arrived, add, sem):
    load_exp = pltpu.make_async_copy(exp_hbm, rows_exp, sem.at[0])
    load_arr = pltpu.make_async_copy(arr_hbm, arrived, sem.at[1])
    load_exp.start()
    load_arr.start()
    load_ids = pltpu.make_async_copy(ids_hbm, ids, sem.at[6])
    load_ids.start()
    bases = []
    for q in range(ZB):
        bases.append(pltpu.make_async_copy(base_hbm.at[q], new.at[pl.ds(q * CX * CY, CX * CY)], sem.at[2 + q]))
        bases[q].start()
    ext_copy = pltpu.make_async_copy(ext_in, ext_out, sem.at[7])
    ext_copy.start()
    new[pl.ds(ROWS, 8), :] = jnp.zeros((8, WIDTH), f32)
    load_exp.wait()
    load_arr.wait()

    def scale(n, _):
        for u in range(UNROLL):
            t = n * UNROLL + u
            add[t] = rows_exp[t] * arrived[t].astype(f32)
        return 0

    lax.fori_loop(0, NDEV // UNROLL, scale, 0)
    load_ids.wait()
    for load in bases:
        load.wait()

    def source(t, _):
        tx, ty = t // GY, lax.rem(t, GY)

        def eight(first):
            at = [ids[tx, ty, 0, first + c] for c in range(8)]
            values = [new[pl.ds(n, 1), :] - add[t, pl.ds(first + c, 1), :] for c, n in enumerate(at)]
            for n, value in zip(at, values):
                new[pl.ds(n, 1), :] = value

        eight(0)
        eight(8)

        @pl.when(ids[tx, ty, 0, 16] < ROWS)
        def _():
            eight(16)

            @pl.when(ids[tx, ty, 0, 24] < ROWS)
            def _():
                eight(24)

        return 0

    lax.fori_loop(0, NDEV, source, 0, unroll=2)
    stores = []
    for q in range(ZB):
        rows_of = new.at[pl.ds(q * CX * CY, CX * CY)]
        stores.append(pltpu.make_async_copy(
            rows_of.reshape(CX, CY, WIDTH), out_hbm.at[:, :, pl.ds(q * WIDTH, WIDTH)], sem.at[2 + q]
        ))
        stores[q].start()
    ext_copy.wait()
    for store in stores:
        store.wait()


def update(ids, ext, rows_exp, base, arrived):
    v = pltpu.VMEM
    return pl.pallas_call(
        update_kernel,
        out_shape=(jax.ShapeDtypeStruct((STARS, BLOCKS), f32), jax.ShapeDtypeStruct((CX, CY, ZB * WIDTH), f32)),
        in_specs=[whole(pltpu.HBM)] * 5,
        out_specs=[whole(pltpu.HBM)] * 2,
        scratch_shapes=[
            pltpu.SMEM((GX, GY, 1, CAP), i32),
            v((ROWS + 8, WIDTH), f32), v((NDEV, CAP, WIDTH), f32), v((NDEV, CAP, WIDTH), bf16), v((NDEV, CAP, WIDTH), f32),
            DMA((8,)),
        ],
        name="update",
        compiler_params=pltpu.CompilerParams(vmem_limit_bytes=62 << 20),
    )(ids, ext, rows_exp, base.reshape(ZB, CX * CY, WIDTH), arrived)


def on_device(log_density, weights, observed, inverse_var, star_counts, block_ids):
    ext, ids, rows_exp, base, arrived = step(
        block_ids.T, log_density, weights, star_counts, observed.T, inverse_var.T
    )
    ext, new = update(ids, ext, rows_exp, base, arrived)
    return (new, ext.T)


def solution(mesh):
    placed = (
        P("gx", "gy", None),
        P(("gx", "gy"), None, None, None),
        P(("gx", "gy"), None),
        P(("gx", "gy"), None),
        P(("gx", "gy")),
        P(("gx", "gy"), None),
    )
    return jax.shard_map(
        on_device,
        mesh=mesh,
        in_specs=placed,
        out_specs=(P("gx", "gy", None), P(("gx", "gy"), None)),
        check_vma=False,
    )
```

```python
import jax
import jax.numpy as jnp
from jax import lax
from jax.experimental import pallas as pl
from jax.experimental.pallas import tpu as pltpu
from jax.sharding import PartitionSpec as P

MESH = pl.DeviceIdType.MESH
DMA = pltpu.SemaphoreType.DMA
shift_kappa = 0.5
prior_weight = 0.05
step_rate = 2.0
f32, bf16, i32 = jnp.float32, jnp.bfloat16, jnp.int32

GX, GY = 16, 8
NDEV, CAP, WIDTH = 128, 32, 128
BLOCKS, SLOTS, STARS = 64, 32, 32
REQ = BLOCKS * SLOTS
CX, CY, ZB = 32, 64, 4
ROWS = CX * CY * ZB
LOCAL_BITS = 13
UNROLL = 4
STAR_UNROLL = 8
center_weight = shift_kappa + 6.0


def whole(space):
    return pl.BlockSpec(memory_space=space)


def remote(src, dst, send, recv, to):
    return pltpu.make_async_remote_copy(
        src_ref=src, dst_ref=dst, send_sem=send, recv_sem=recv, device_id=to, device_id_type=MESH
    )


def drain(ref, sem):
    pltpu.make_async_copy(ref, ref, sem).wait()


def send_order():
    dist = lambda o: sum(min(v, 4 - v) for v in o[:3])
    rest = [(a, b, c, d) for a in range(4) for b in range(4) for c in range(4) for d in range(2)][1:]
    rest = [rest[j * 37 % len(rest)] for j in range(len(rest))]
    load, order = [0] * 6, []

    def loaded(o):
        now = list(load)
        for axis in range(3):
            now[2 * axis] += o[axis] in (1, 2)
            now[2 * axis + 1] += o[axis] in (3, 2)
        return now

    while rest:
        far = max(map(dist, rest))
        spread = lambda o: (max(loaded(o)) - min(loaded(o)), sum(v * v for v in loaded(o)))
        best = min((o for o in rest if dist(o) == far), key=spread)
        load = loaded(best)
        rest.remove(best)
        order.append(best)
    return [((a * 4 + b) * 4 + c) * 2 + d for a, b, c, d in order] + [0]


def packed_order():
    order = send_order()
    return [sum(order[n + u] * NDEV ** u for u in range(UNROLL)) for n in range(0, NDEV, UNROLL)]


def pick(words, at, first=0):
    if len(words) == 1:
        return jnp.int32(words[0])
    half = len(words) // 2
    return jnp.where(at < first + half, pick(words[:half], at, first), pick(words[half:], at, first + half))


def partners(gx, gy, trip):
    word, found = pick(packed_order(), trip), []
    for u in range(UNROLL):
        o = lax.rem(word // NDEV ** u, NDEV)
        x = lax.rem(gx // 4 + o // 32, 4)
        y = lax.rem(gx + lax.rem(o // 8, 4), 4)
        z = lax.rem(gy // 2 + lax.rem(o // 2, 4), 4)
        found.append((x * 4 + y, z * 2 + lax.rem(gy + o, 2)))
    return found


def bucket(blocks, out_ids, inv_ref, pos_ref, at_ref, bt_ref):
    ids = jnp.concatenate([blocks[k:k + 1, :] for k in range(SLOTS)], axis=1)
    target = ids >> LOCAL_BITS
    within = ids & (ROWS - 1)
    within = (within & (ZB - 1)) * (CX * CY) + (within >> 2)
    order = lax.broadcasted_iota(i32, (1, REQ), 1)
    order = (order & (BLOCKS - 1)) * SLOTS + (order >> 6)
    at_ref[...] = jnp.where(lax.broadcasted_iota(i32, (NDEV, REQ), 0) == target, 1.0, 0.0).astype(bf16)
    step = 256
    before = lax.broadcasted_iota(i32, (step, step), 0) < lax.broadcasted_iota(i32, (step, step), 1)
    before = jnp.where(before, 1.0, 0.0).astype(bf16)
    running = jnp.zeros((NDEV, 1), f32)
    slot = lax.broadcasted_iota(i32, (CAP, step), 0)
    for k in range(REQ // step):
        cut = slice(k * step, (k + 1) * step)
        part = at_ref[:, cut]
        prefix = jnp.dot(part, before, preferred_element_type=f32) + running
        wide = part.astype(f32)
        rank = jnp.clip(jnp.sum(wide * prefix, axis=0, keepdims=True).astype(i32), 0, CAP - 1)
        running = running + jnp.sum(wide, axis=1, keepdims=True)
        hit = slot == rank
        pos_ref[:, cut] = target[:, cut] * CAP + rank
        for n, value in enumerate((within[:, cut] >> 7, within[:, cut] & 127, order[:, cut] >> 7, order[:, cut] & 127, None)):
            value = 1.0 if value is None else value.astype(f32)
            bt_ref[n * CAP:(n + 1) * CAP, cut] = jnp.where(hit, value, 0.0).astype(bf16)
    table = lax.dot_general(at_ref[...], bt_ref[...], (((1,), (1,)), ((), ())), preferred_element_type=f32)
    parts = [table[:, n * CAP:(n + 1) * CAP] for n in range(5)]
    present = parts[4] > 0.5
    row = jnp.where(present, parts[0] * 128.0 + parts[1], float(ROWS)).astype(i32)
    out_ids[...] = jnp.clip(row, 0, ROWS).reshape(GX, GY, 1, CAP)
    source = jnp.where(present, parts[2] * 128.0 + parts[3], float(REQ)).astype(i32)
    inv_ref[...] = jnp.clip(source, 0, REQ)


def shifted_sum(field, x, row):
    lane = lax.broadcasted_iota(i32, (8, WIDTH), 1)
    first, final = lane == 0, lane == WIDTH - 1
    at = lambda q, dx, dr: field[q, x + dx, pl.ds(row + dr, 8), :]
    centers = [at(q, 0, 0) for q in range(ZB)]
    up = [pltpu.roll(c, 1, 1) for c in centers]
    down = [pltpu.roll(c, WIDTH - 1, 1) for c in centers]
    sides = []
    for q in range(ZB):
        below = jnp.where(first, up[q - 1] if q > 0 else 0.0, up[q])
        above = jnp.where(final, down[q + 1] if q < ZB - 1 else 0.0, down[q])
        sides.append((at(q, -1, 0) + at(q, 1, 0)) + (at(q, 0, -1) + at(q, 0, 1)) + (below + above))
    return centers, sides


def step_kernel(blocks, dens_hbm, weights_hbm, counts_hbm, observed_hbm, inverse_hbm,
                ext_hbm, ids_hbm, exp_hbm, base_hbm, arr_hbm,
                counts, observed, inverse_var, ext_t,
                dens, out_ids, mid_ids, in_ids, ids_s, inv_v, inv_s, pos_v, pos_s, at_ref, bt_ref,
                rows_exp, served, ret, rows, w_ref, obs4, inv4, ext4, wgt4, sens, stage, parcel,
                xlo, xhi, ylo, yhi, field, smooth, base,
                entered, s_id, r_id, s_row, r_row, local, s_halo, r_halo):
    gx, gy = lax.axis_index("gx"), lax.axis_index("gy")
    me = gx * GY + gy
    gxm, gxp = lax.rem(gx + GX - 1, GX), lax.rem(gx + 1, GX)
    gym, gyp = lax.rem(gy + GY - 1, GY), lax.rem(gy + 1, GY)
    column = [lax.rem(gx + d, GX) for d in (1, 15, 4, 12, 3, 13, 5, 11, 7, 9, 2, 14, 6, 10, 8)]
    line = [lax.rem(gy + d, GY) for d in (1, 7, 2, 6, 3, 5, 4)]
    greeted = [(t, gy) for t in column] + [(gx, t) for t in line] + [(a, b) for a in (gxm, gxp) for b in (gym, gyp)]
    barrier = pltpu.get_barrier_semaphore()
    for to in greeted:
        pl.semaphore_signal(barrier, inc=1, device_id=to, device_id_type=MESH)

    loads = []
    for q in range(ZB):
        part = dens_hbm.at[:, :, pl.ds(q * WIDTH, WIDTH)]
        loads.append(pltpu.make_async_copy(part, field.at[q, pl.ds(2, CX), pl.ds(8, CY)], local.at[q]))
    w_load = pltpu.make_async_copy(weights_hbm, w_ref, local.at[4])
    for load in loads:
        load.start()
    w_load.start()
    small = [
        pltpu.make_async_copy(src, dst, local.at[8 + n])
        for n, (src, dst) in enumerate(((counts_hbm, counts), (observed_hbm, observed), (inverse_hbm, inverse_var)))
    ]
    for load in small:
        load.start()

    bucket(blocks, out_ids, inv_v, pos_v, at_ref, bt_ref)
    to_smem = [pltpu.make_async_copy(inv_v, inv_s, local.at[5]), pltpu.make_async_copy(pos_v, pos_s, local.at[6])]
    for copy in to_smem:
        copy.start()

    pl.semaphore_wait(barrier, len(greeted))
    for t in line:
        pl.semaphore_signal(entered, inc=1, device_id=(gx, t), device_id_type=MESH)
    own = pltpu.make_async_copy(out_ids.at[gx], mid_ids.at[gx], local.at[7])
    own.start()
    for t in column:
        remote(out_ids.at[t], mid_ids.at[gx], s_id.at[0], r_id.at[0], (t, gy)).start()

    for load in loads:
        load.wait()
    halos = [
        (field.at[:, pl.ds(CX, 2), pl.ds(8, CY)], xlo, (gxp, gy)),
        (field.at[:, pl.ds(2, 2), pl.ds(8, CY)], xhi, (gxm, gy)),
        (field.at[:, pl.ds(2, CX), pl.ds(CY + 6, 2)], ylo.at[:, pl.ds(1, CX), pl.ds(6, 2)], (gx, gyp)),
        (field.at[:, pl.ds(2, CX), pl.ds(8, 2)], yhi.at[:, pl.ds(1, CX), pl.ds(0, 2)], (gx, gym)),
        (field.at[:, CX + 1, pl.ds(CY, 8)], ylo.at[:, 0], (gxp, gyp)),
        (field.at[:, 2, pl.ds(CY, 8)], ylo.at[:, CX + 1], (gxm, gyp)),
        (field.at[:, CX + 1, pl.ds(8, 8)], yhi.at[:, 0], (gxp, gym)),
        (field.at[:, 2, pl.ds(8, 8)], yhi.at[:, CX + 1], (gxm, gym)),
    ]
    halos = [remote(src, dst, s_halo.at[n], r_halo.at[n], to) for n, (src, dst, to) in enumerate(halos)]
    for copy in halos:
        copy.start()

    def gather_source(x, _):
        for q in range(ZB):
            dens[pl.ds(pl.multiple_of(q * CX * CY + x * CY, CY), CY), :] = field[q, x + 2, pl.ds(8, CY), :]
        return 0

    lax.fori_loop(0, CX, gather_source, 0)
    dens[pl.ds(ROWS, 8), :] = jnp.zeros((8, WIDTH), f32)
    own.wait()
    drain(mid_ids.at[pl.ds(0, GX - 1)], r_id.at[0])
    pl.semaphore_wait(entered, len(line))
    own = pltpu.make_async_copy(mid_ids.at[:, gy], in_ids.at[:, gy], local.at[7])
    own.start()
    for t in line:
        remote(mid_ids.at[:, t], in_ids.at[:, gy], s_id.at[1], r_id.at[1], (gx, t)).start()

    for load in small:
        load.wait()
    for ref, four in ((observed, obs4), (inverse_var, inv4)):
        wide = jnp.concatenate([ref[...], ref[...]], axis=1)
        four[...] = jnp.concatenate([wide] * 4, axis=0).T
    sens[pl.ds(REQ, 8), :] = jnp.zeros((8, WIDTH), f32)
    own.wait()
    drain(in_ids.at[:, pl.ds(0, GY - 1)], r_id.at[1])
    ids_copy = pltpu.make_async_copy(in_ids, ids_s, local.at[7])
    ids_copy.start()
    ids_store = pltpu.make_async_copy(in_ids, ids_hbm, local.at[11])
    ids_store.start()
    ids_copy.wait()

    def serve(tx, ty, at):
        for c in range(CAP):
            rows_exp[at, c, :] = dens[ids_s[tx, ty, 0, c], :]
        values = jnp.exp(rows_exp[at])
        rows_exp[at] = step_rate * values
        served[at] = values.astype(bf16)

    def send_rows(trip, count):
        to = partners(gx, gy, trip)
        for tx, ty in to:
            serve(tx, ty, tx * GY + ty)
        for tx, ty in to[:count]:
            remote(served.at[tx * GY + ty], ret.at[me], s_row.at[0], r_row.at[0], (tx, ty)).start()
        return 0

    trips = NDEV // UNROLL
    lax.fori_loop(0, trips - 1, lambda trip, _: send_rows(trip, UNROLL), 0)
    send_rows(trips - 1, UNROLL - 1)
    keep = pltpu.make_async_copy(served.at[me], ret.at[me], local.at[0])
    keep.start()
    exp_store = pltpu.make_async_copy(rows_exp, exp_hbm, local.at[1])
    exp_store.start()

    for copy in halos:
        copy.wait()
    low_x, high_x, low_y, high_y = gx > 0, gx < GX - 1, gy > 0, gy < GY - 1
    blank = jnp.zeros((8, WIDTH), f32)
    for q in range(ZB):
        for n in range(2):
            field[q, n, pl.ds(8, CY), :] = jnp.where(low_x, xlo[q, n], 0.0)
            field[q, CX + 2 + n, pl.ds(8, CY), :] = jnp.where(high_x, xhi[q, n], 0.0)

        def edge(x, _):
            field[q, x + 1, pl.ds(0, 8), :] = jnp.where(low_y, ylo[q, x], 0.0)
            field[q, x + 1, pl.ds(8 + CY, 8), :] = jnp.where(high_y, yhi[q, x], 0.0)
            return 0

        lax.fori_loop(1, CX + 1, edge, 0)
        for x, inside in ((0, low_x), (CX + 1, high_x)):
            field[q, x + 1, pl.ds(0, 8), :] = jnp.where(low_y & inside, ylo[q, x], 0.0)
            field[q, x + 1, pl.ds(8 + CY, 8), :] = jnp.where(high_y & inside, yhi[q, x], 0.0)
    sub = lax.broadcasted_iota(i32, (8, WIDTH), 0)
    top_keep = (sub > 0) | low_y
    bottom_keep = (sub != 1) | high_y

    def smooth_plane(x, inside=None):
        for n in range(9):
            centers, sides = shifted_sum(field, x + 1, 7 + 8 * n)
            for q in range(ZB):
                value = center_weight * centers[q] - sides[q]
                if n == 0:
                    value = jnp.where(top_keep, value, 0.0)
                if n == 8:
                    value = jnp.where(bottom_keep, value, 0.0)
                if inside is not None:
                    value = jnp.where(inside, value, 0.0)
                smooth[q, x, pl.ds(8 * n, 8), :] = value

    def base_plane(x):
        for n in range(8):
            centers, sides = shifted_sum(smooth, x + 1, 8 * n + 1)
            for q in range(ZB):
                prior = center_weight * centers[q] - sides[q]
                now = field[q, x + 2, pl.ds(8 + 8 * n, 8), :]
                base[q, x, pl.ds(8 * n, 8), :] = now - (step_rate * prior_weight) * prior

    smooth_plane(0, low_x)

    def smooth_all(x, _):
        smooth_plane(x)
        return 0

    lax.fori_loop(1, CX + 1, smooth_all, 0)
    smooth_plane(CX + 1, high_x)
    w_load.wait()
    for copy in to_smem:
        copy.wait()
    keep.wait()
    drain(ret.at[pl.ds(0, NDEV - 1)], r_row.at[0])

    def widen(n, _):
        for u in range(UNROLL):
            rows[pl.ds(pl.multiple_of((n * UNROLL + u) * CAP, CAP), CAP), :] = ret[n * UNROLL + u].astype(f32)
        return 0

    lax.fori_loop(0, NDEV // UNROLL, widen, 0)
    deep = 8 * STARS
    mine = (lax.broadcasted_iota(i32, (8, deep), 1) >> 5) == lax.broadcasted_iota(i32, (8, deep), 0)
    lane = lax.broadcasted_iota(i32, (STARS, WIDTH), 1)
    diagonal = (lane & (STARS - 1)) == lax.broadcasted_iota(i32, (STARS, WIDTH), 0)
    star = lax.broadcasted_iota(i32, (1, WIDTH), 1) & (STARS - 1)

    def extinct(i):
        for u in range(STAR_UNROLL):
            b = i * STAR_UNROLL + u
            totals = [jnp.zeros((STARS, WIDTH), f32) for _ in range(2)]
            for k in range(SLOTS):
                line_k = rows[pl.ds(pos_s[0, k * BLOCKS + b], 1), :]
                totals[k % 2] = totals[k % 2] + w_ref[b, k].astype(f32) * line_k
            total = jnp.sum(totals[0] + totals[1], axis=1, keepdims=True)
            ext = jnp.sum(jnp.where(diagonal, total, 0.0), axis=0, keepdims=True)
            ext4[pl.ds(b, 1), :] = ext
            residual = inv4[pl.ds(b, 1), :] * (ext - obs4[pl.ds(b, 1), :])
            wgt4[pl.ds(b, 1), :] = jnp.where(star < counts[b], residual, 0.0)

    def sensitive(i):
        for u in range(STAR_UNROLL):
            b = i * STAR_UNROLL + u
            line_b = wgt4[pl.ds(b, 1), :]
            left = jnp.where(mine, jnp.concatenate([line_b, line_b], axis=1), 0.0).astype(bf16)
            for n in range(SLOTS // 8):
                sens[pl.ds(pl.multiple_of(b * SLOTS + n * 8, 8), 8), :] = jnp.dot(
                    left, w_ref[b, pl.ds(n * 8, 8)].reshape(deep, WIDTH), preferred_element_type=f32
                )

    extinct(0)

    def both(i, _):
        sensitive(i - 1)
        extinct(i)
        return 0

    lax.fori_loop(1, BLOCKS // STAR_UNROLL, both, 0)
    sensitive(BLOCKS // STAR_UNROLL - 1)
    ext_t[...] = jnp.concatenate([ext4[...], ext4[...]], axis=0).T[:STARS, :BLOCKS]
    ext_store = pltpu.make_async_copy(ext_t, ext_hbm, local.at[12])
    ext_store.start()

    slot_a, slot_b = lax.broadcasted_iota(i32, (CAP, CAP), 0), lax.broadcasted_iota(i32, (CAP, CAP), 1)
    eye, together = slot_a == slot_b, (slot_a >> 3) == (slot_b >> 3)

    def pack(tx, ty, at):
        for c in range(CAP):
            stage[at, c, :] = sens[inv_s[at, c], :]
        across = jnp.broadcast_to(out_ids[tx, ty].astype(f32), (CAP, CAP))
        down = jnp.sum(jnp.where(eye, across, 0.0), axis=1, keepdims=True)
        same = jnp.where((down == across) & together, 1.0, 0.0).astype(bf16)
        parcel[at] = jnp.dot(same, stage[at].astype(bf16), preferred_element_type=f32).astype(bf16)

    def pack_all(to):
        for tx, ty in to:
            pack(tx, ty, tx * GY + ty)

    def send_back(to):
        for tx, ty in to:
            remote(parcel.at[tx * GY + ty], arr_hbm.at[me], s_row.at[1], r_row.at[1], (tx, ty)).start()

    def give_back(it, _):
        to = partners(gx, gy, it)
        pack_all(to)
        base_plane(it)
        send_back(to)
        return 0

    lax.fori_loop(0, CX - 1, give_back, 0)
    to = partners(gx, gy, trips - 1)
    pack_all(to)
    send_back(to[:UNROLL - 1])
    base_plane(CX - 1)
    keep = pltpu.make_async_copy(parcel.at[me], arr_hbm.at[me], local.at[0])
    keep.start()
    base_store = pltpu.make_async_copy(base, base_hbm, local.at[2])
    base_store.start()
    keep.wait()
    ids_store.wait()
    ext_store.wait()
    exp_store.wait()
    base_store.wait()
    drain(out_ids.at[pl.ds(0, GX - 1)], s_id.at[0])
    drain(mid_ids.at[:, pl.ds(0, GY - 1)], s_id.at[1])
    drain(served.at[pl.ds(0, NDEV - 1)], s_row.at[0])
    drain(parcel.at[pl.ds(0, NDEV - 1)], s_row.at[1])
    drain(arr_hbm.at[pl.ds(0, NDEV - 1)], r_row.at[1])


def step(blocks, dens, weights, counts, observed, inverse_var):
    shape = jax.ShapeDtypeStruct
    v = pltpu.VMEM
    return pl.pallas_call(
        step_kernel,
        out_shape=(
            shape((STARS, BLOCKS), f32),
            shape((GX, GY, 1, CAP), i32),
            shape((NDEV, CAP, WIDTH), f32),
            shape((ZB, CX, CY, WIDTH), f32),
            shape((NDEV, CAP, WIDTH), bf16),
        ),
        in_specs=[
            whole(v), whole(pltpu.HBM), whole(pltpu.HBM), whole(pltpu.HBM), whole(pltpu.HBM), whole(pltpu.HBM),
        ],
        out_specs=[whole(pltpu.HBM)] * 5,
        scratch_shapes=[
            pltpu.SMEM((BLOCKS,), i32), v((STARS, BLOCKS), f32), v((STARS, BLOCKS), f32), v((STARS, BLOCKS), f32),
            v((ROWS + 8, WIDTH), f32),
            v((GX, GY, 1, CAP), i32), v((GX, GY, 1, CAP), i32), v((GX, GY, 1, CAP), i32), pltpu.SMEM((GX, GY, 1, CAP), i32),
            v((NDEV, CAP), i32), pltpu.SMEM((NDEV, CAP), i32), v((1, REQ), i32), pltpu.SMEM((1, REQ), i32),
            v((NDEV, REQ), bf16), v((5 * CAP, REQ), bf16),
            v((NDEV, CAP, WIDTH), f32), v((NDEV, CAP, WIDTH), bf16), v((NDEV, CAP, WIDTH), bf16),
            v((NDEV * CAP, WIDTH), f32), v((BLOCKS, SLOTS, STARS, WIDTH), bf16),
            v((WIDTH, WIDTH), f32), v((WIDTH, WIDTH), f32), v((BLOCKS, WIDTH), f32), v((BLOCKS, WIDTH), f32),
            v((REQ + 8, WIDTH), f32), v((NDEV, CAP, WIDTH), f32), v((NDEV, CAP, WIDTH), bf16),
            v((ZB, 2, CY, WIDTH), f32), v((ZB, 2, CY, WIDTH), f32),
            v((ZB, CX + 2, 8, WIDTH), f32), v((ZB, CX + 2, 8, WIDTH), f32),
            v((ZB, CX + 4, CY + 16, WIDTH), f32), v((ZB, CX + 2, CY + 8, WIDTH), f32), v((ZB, CX, CY, WIDTH), f32),
            pltpu.SemaphoreType.REGULAR, DMA((2,)), DMA((2,)), DMA((2,)), DMA((2,)), DMA((13,)), DMA((8,)), DMA((8,)),
        ],
        name="step",
        compiler_params=pltpu.CompilerParams(collective_id=0, has_side_effects=True, vmem_limit_bytes=60 << 20),
    )(blocks, dens, weights, counts, observed, inverse_var)


def update_kernel(ids_hbm, ext_in, exp_hbm, base_hbm, arr_hbm, ext_out, out_hbm, ids, new, rows_exp, arrived, add, sem):
    load_exp = pltpu.make_async_copy(exp_hbm, rows_exp, sem.at[0])
    load_arr = pltpu.make_async_copy(arr_hbm, arrived, sem.at[1])
    load_exp.start()
    load_arr.start()
    load_ids = pltpu.make_async_copy(ids_hbm, ids, sem.at[6])
    load_ids.start()
    bases = []
    for q in range(ZB):
        bases.append(pltpu.make_async_copy(base_hbm.at[q], new.at[pl.ds(q * CX * CY, CX * CY)], sem.at[2 + q]))
        bases[q].start()
    ext_copy = pltpu.make_async_copy(ext_in, ext_out, sem.at[7])
    ext_copy.start()
    new[pl.ds(ROWS, 8), :] = jnp.zeros((8, WIDTH), f32)
    load_exp.wait()
    load_arr.wait()

    def scale(n, _):
        for u in range(UNROLL):
            t = n * UNROLL + u
            add[t] = rows_exp[t] * arrived[t].astype(f32)
        return 0

    lax.fori_loop(0, NDEV // UNROLL, scale, 0)
    load_ids.wait()
    for load in bases:
        load.wait()

    def source(t, _):
        tx, ty = t // GY, lax.rem(t, GY)

        def eight(first):
            at = [ids[tx, ty, 0, first + c] for c in range(8)]
            values = [new[pl.ds(n, 1), :] - add[t, pl.ds(first + c, 1), :] for c, n in enumerate(at)]
            for n, value in zip(at, values):
                new[pl.ds(n, 1), :] = value

        eight(0)
        eight(8)

        @pl.when(ids[tx, ty, 0, 16] < ROWS)
        def _():
            eight(16)

            @pl.when(ids[tx, ty, 0, 24] < ROWS)
            def _():
                eight(24)

        return 0

    lax.fori_loop(0, NDEV, source, 0, unroll=2)
    stores = []
    for q in range(ZB):
        rows_of = new.at[pl.ds(q * CX * CY, CX * CY)]
        stores.append(pltpu.make_async_copy(
            rows_of.reshape(CX, CY, WIDTH), out_hbm.at[:, :, pl.ds(q * WIDTH, WIDTH)], sem.at[2 + q]
        ))
        stores[q].start()
    ext_copy.wait()
    for store in stores:
        store.wait()


def update(ids, ext, rows_exp, base, arrived):
    v = pltpu.VMEM
    return pl.pallas_call(
        update_kernel,
        out_shape=(jax.ShapeDtypeStruct((STARS, BLOCKS), f32), jax.ShapeDtypeStruct((CX, CY, ZB * WIDTH), f32)),
        in_specs=[whole(pltpu.HBM)] * 5,
        out_specs=[whole(pltpu.HBM)] * 2,
        scratch_shapes=[
            pltpu.SMEM((GX, GY, 1, CAP), i32),
            v((ROWS + 8, WIDTH), f32), v((NDEV, CAP, WIDTH), f32), v((NDEV, CAP, WIDTH), bf16), v((NDEV, CAP, WIDTH), f32),
            DMA((8,)),
        ],
        name="update",
        compiler_params=pltpu.CompilerParams(vmem_limit_bytes=62 << 20),
    )(ids, ext, rows_exp, base.reshape(ZB, CX * CY, WIDTH), arrived)


def on_device(log_density, weights, observed, inverse_var, star_counts, block_ids):
    ext, ids, rows_exp, base, arrived = step(
        block_ids.T, log_density, weights, star_counts, observed.T, inverse_var.T
    )
    ext, new = update(ids, ext, rows_exp, base, arrived)
    return (new, ext.T)


def solution(mesh):
    placed = (
        P("gx", "gy", None),
        P(("gx", "gy"), None, None, None),
        P(("gx", "gy"), None),
        P(("gx", "gy"), None),
        P(("gx", "gy")),
        P(("gx", "gy"), None),
    )
    return jax.shard_map(
        on_device,
        mesh=mesh,
        in_specs=placed,
        out_specs=(P("gx", "gy", None), P(("gx", "gy"), None)),
        check_vma=False,
    )
```
